32 devices in a mesh: batch: 4 (over y, core), own: 8 (over z, x).
Axes of the slice: x: 2, y: 2, z: 4, core: 2. Of those that a mesh axis runs over, the one named last changes fastest.
Arguments:
- hidden_in: bfloat16 [4, 1024, 2048], P('batch', 'own'), may hold values from -6 to 6
- norm_gain: float32 [2048], replicated, may hold values from 0.5 to 1.5
- input_proj: bfloat16 [3, 2048, 2, 4096], P(None, None, None, 'own'), may hold values from -0.125 to 0.125
- conv_weight: float32 [4, 4096], replicated, may hold values from -3 to 3
- conv_bias: float32 [4096], replicated, may hold values from -0.5 to 0.5
- state_proj: bfloat16 [3, 4096, 160], P(None, 'own'), may hold values from -0.09375 to 0.09375
- step_proj: bfloat16 [3, 128, 4096], P(None, None, 'own'), may hold values from -0.5 to 0.5
- step_bias: float32 [3, 4096], P(None, 'own'), may hold values from -9 to -3
- log_decay: float32 [16, 4096], replicated, may hold values from 0 to 2.8
- skip_gain: float32 [4096], replicated, may hold values from 0.5 to 1.5
- output_proj: bfloat16 [3, 4096, 2048], P(None, 'own'), may hold values from -0.5 to 0.5
- modality: int32 [4, 1024], P('batch'), may hold values from 0 to 2, as said below
- grad_out: bfloat16 [4, 1024, 2048], P('batch', 'own'), may hold values from -6 to 6
Outputs:
- block_out: bfloat16 [4, 1024, 2048], P('batch', 'own')
- grad_hidden: float32 [4, 1024, 2048], P('batch', 'own')
- grad_gain: float32 [2048], replicated
- grad_input_proj: float32 [3, 2048, 2, 4096], P(None, None, None, 'own')
- grad_conv_weight: float32 [4, 4096], replicated
- grad_conv_bias: float32 [4096], replicated
- grad_state_proj: float32 [3, 4096, 160], P(None, 'own')
- grad_step_proj: float32 [3, 128, 4096], P(None, None, 'own')
- grad_step_bias: float32 [3, 4096], P(None, 'own')
- grad_log_decay: float32 [16, 4096], replicated
- grad_skip_gain: float32 [4096], replicated
- grad_output_proj: float32 [3, 4096, 2048], P(None, 'own')
The draws below stay inside these ranges and needn't reach their ends.
Inputs may be any that keep to these rules, and one draw needn't show every extreme that they name: Among the 1 sequence of one batch index (an aligned block of rows), each modality has at most 448 tokens, and one modality has exactly 448.
All inputs are finite; a program needn't handle non-finite values.
Results may differ from the reference program's by a relative error of at most 0.011.
The reference program's roundings to bfloat16 on the way count: a program that leaves them out, or rounds other values in their place, can miss the bound.
Values may be sent and summed in bfloat16 or wider, within the bound.
No kernel may reach another device: no remote copies, remote signals or barrier semaphores. Data moves between devices by JAX's collectives and lax.ppermute only.
A program may use at most 320 MiB of HBM per device.

```python
import jax
import jax.numpy as jnp
from jax import lax

D = 2048
E = 4096
N = 16
K = 4
R = 128
M = 3
SEQ_B = 1
P_SIZE = 160
LEN = 1024
SEQS = 4
CAP = 448


def draw_modality(key, part):
    groups = SEQS // SEQ_B
    group_rows = SEQ_B * LEN
    subkeys = jax.random.split(key, 3)
    heavy = jax.random.randint(subkeys[0], (groups, 1), 0, 3)
    second = jax.random.randint(subkeys[1], (groups, 1), group_rows - 2 * CAP, CAP + 1)
    orders = jax.vmap(lambda subkey: jax.random.permutation(subkey, group_rows))(jax.random.split(subkeys[2], groups))
    labels = jnp.where(orders < CAP, heavy, jnp.where(orders < CAP + second, (heavy + 1) % 3, (heavy + 2) % 3))
    return labels.reshape(SEQS, LEN).astype(jnp.int32)


def levels(own_key, shape, cuts, smallest, top_value):
    factor_of = 1.0
    for dim, blocks in cuts:
        draws = jax.random.uniform(jax.random.fold_in(jax.random.fold_in(own_key, 6), dim), (blocks,), jnp.float32, smallest / len(cuts), top_value / len(cuts))
        factor_of = factor_of * jnp.repeat(jnp.exp(draws), shape[dim] // blocks).reshape((-1,) + (1,) * (len(shape) - 1 - dim))
    return factor_of


def centred(rng, extent, spread, bound, cuts=(), kind=jnp.bfloat16):
    entries = spread * jax.random.normal(rng, extent, jnp.float32)
    if cuts:
        entries = entries * levels(rng, extent, cuts, -0.22, 0.18)
    return jnp.clip(entries, -bound, bound).astype(kind)


def setup_inputs(seed: int = 0) -> dict:
    seeds = jax.random.split(jax.random.key(seed), 14)
    hidden_in = centred(seeds[0], (SEQS, LEN, D), 1.0, 6.0, ((0, 4), (1, 8)))
    norm_gain = jnp.clip(1.0 + 0.1 * jax.random.normal(seeds[1], (D,), jnp.float32), 0.5, 1.5)
    input_proj = centred(seeds[2], (M, D, 2, E), D ** -0.5, 0.125, ((3, 8),))
    conv_weight = centred(seeds[3], (K, E), K ** -0.5, 3.0, (), jnp.float32)
    conv_bias = jnp.clip(jax.random.uniform(seeds[4], (E,), jnp.float32, -0.5, 0.5), -0.5, 0.5)
    state_proj = centred(seeds[5], (M, E, P_SIZE), E ** -0.5, 0.09375, ((1, 8),))
    step_proj = centred(seeds[6], (M, R, E), R ** -0.5, 0.5, ((2, 8),))
    step_bias = jnp.clip(-9.0 + 6.0 * jax.random.uniform(seeds[7], (M, E), jnp.float32) ** levels(seeds[7], (M, E), ((1, 8),), -0.2, 0.2), -9.0, -3.0)
    log_decay = jnp.clip(jax.random.uniform(seeds[8], (N, E), jnp.float32, 0.0, 2.8), 0.0, 2.8)
    skip_gain = jnp.clip(jax.random.uniform(seeds[9], (E,), jnp.float32, 0.5, 1.5), 0.5, 1.5)
    output_proj = centred(seeds[10], (M, E, D), (E // 32) ** -0.5, 0.5, ((1, 8),))
    modality = draw_modality(jax.random.fold_in(seeds[13], 71), 0)
    grad_out = centred(seeds[12], (SEQS, LEN, D), 1.0, 6.0, ((0, 4), (1, 8)))
    return {"hidden_in": hidden_in, "norm_gain": norm_gain, "input_proj": input_proj, "conv_weight": conv_weight, "conv_bias": conv_bias, "state_proj": state_proj, "step_proj": step_proj, "step_bias": step_bias, "log_decay": log_decay, "skip_gain": skip_gain, "output_proj": output_proj, "modality": modality, "grad_out": grad_out}


@jax.custom_vjp
def low(v):
    return lax.optimization_barrier(v.astype(jnp.bfloat16)).astype(jnp.float32)

@jax.custom_vjp
def low_back(v):
    return v

def low_keep(v):
    return (low(v), None)

def low_pass(kept, grad):
    return (grad,)

def back_keep(v):
    return (v, None)

def back_low(kept, grad):
    return (low(grad),)
low.defvjp(low_keep, low_pass)
low_back.defvjp(back_keep, back_low)
epsilon = 1e-05
time_block = 64
highest = lax.Precision.HIGHEST

def select_rows(rows, weights, modal):
    summed = jnp.zeros(rows.shape[:-1] + (weights.shape[2],), jnp.float32)
    for modal_id in range(weights.shape[0]):
        product = jnp.einsum('slf,fg->slg', rows, weights[modal_id], precision=highest)
        summed = jnp.where(modal[..., None] == modal_id, product, summed)
    return summed

def select_vector(table, modal):
    summed = jnp.zeros(modal.shape + (table.shape[1],), jnp.float32)
    for modal_id in range(table.shape[0]):
        summed = jnp.where(modal[..., None] == modal_id, table[modal_id], summed)
    return summed

def run_scan(act_vec, step_vec, b_state, c_state, rates, skip_vec, initial):
    seq_count, length, chans = act_vec.shape
    block_len = min(time_block, length)

    def advance(carried, inputs):
        act_t, step_t, write_t, read_t = inputs
        decays = jnp.exp(step_t[:, None, :] * rates[None])
        carried = decays * carried + (step_t * act_t)[:, None, :] * write_t[:, :, None]
        emitted = lax.optimization_barrier(jnp.sum(carried * read_t[:, :, None], axis=1)) + skip_vec * act_t
        return (carried, emitted)

    def run_block(carried, inputs):
        return lax.scan(advance, carried, inputs)

    def by_time(series):
        return jnp.transpose(series, (1, 0, 2)).reshape(length // block_len, block_len, seq_count, series.shape[2])
    final, emitted = lax.scan(jax.checkpoint(run_block), initial, (by_time(act_vec), by_time(step_vec), by_time(b_state), by_time(c_state)))
    return (jnp.transpose(emitted.reshape(length, seq_count, chans), (1, 0, 2)), final)

def conv_act(source, weight, offset_vec):
    length = source.shape[1]
    padded = jnp.pad(source, ((0, 0), (K - 1, 0), (0, 0)))
    summed = offset_vec + jnp.zeros_like(source)
    for offset in range(K):
        summed = summed + weight[offset] * padded[:, offset:offset + length]
    return jax.nn.silu(summed)

def forward(resid, norm_gain, input_proj, conv_weight, conv_bias, state_proj, step_proj, step_bias, log_decay, skip_gain, output_proj, modal):
    mean_sq = lax.optimization_barrier(jnp.mean(resid * resid, axis=-1, keepdims=True))
    normed = low(resid * lax.rsqrt(mean_sq + epsilon) * norm_gain)
    mixed = low_back(low(select_rows(normed, input_proj.reshape(M, D, 2 * E), modal)))
    conv_in = mixed[..., :E]
    gate_vec = mixed[..., E:]
    act_vec = low(conv_act(conv_in, conv_weight, conv_bias))
    act_scan = low_back(act_vec)
    proj = low_back(select_rows(act_vec, state_proj, modal))
    step_in = low(proj[..., :R])
    b_state = proj[..., R:R + N]
    c_state = proj[..., R + N:]
    step_lin = low_back(select_rows(step_in, step_proj, modal))
    pre_step = step_lin + select_vector(step_bias, modal)
    delta = low_back(low(jax.nn.softplus(pre_step)))
    rates = -jnp.exp(log_decay)
    initial = jnp.zeros((resid.shape[0], N, E), jnp.float32)
    scanned = run_scan(act_scan, delta, b_state, c_state, rates, skip_gain, initial)[0]
    gated = low_back(low(scanned * jax.nn.silu(gate_vec)))
    return resid + select_rows(gated, output_proj, modal)

def reference(hidden_in, norm_gain, input_proj, conv_weight, conv_bias, state_proj, step_proj, step_bias, log_decay, skip_gain, output_proj, modality, grad_out):
    params = (norm_gain, input_proj.astype(jnp.float32), conv_weight, conv_bias, state_proj.astype(jnp.float32), step_proj.astype(jnp.float32), step_bias, log_decay, skip_gain, output_proj.astype(jnp.float32))
    groups = SEQS // SEQ_B
    hidden_groups = hidden_in.reshape(groups, SEQ_B, LEN, D)
    modal_groups = modality.reshape(groups, SEQ_B, LEN)
    cot_groups = grad_out.reshape(groups, SEQ_B, LEN, D)

    def one_group(carried, inputs):
        hidden_group, modal_group, cot_group = inputs

        def forward_group(resid, *weights):
            return forward(resid, *weights, modal_group)
        result, pull = jax.vjp(forward_group, hidden_group.astype(jnp.float32), *params)
        pulled = pull(cot_group.astype(jnp.float32))
        carried = jax.tree.map(jnp.add, carried, tuple(pulled[1:]))
        return (carried, (result.astype(jnp.bfloat16), pulled[0]))
    zeroed = tuple((jnp.zeros_like(param) for param in params))
    totals, outputs = lax.scan(one_group, zeroed, (hidden_groups, modal_groups, cot_groups))
    block_out = outputs[0].reshape(SEQS, LEN, D)
    grad_hidden = outputs[1].reshape(SEQS, LEN, D)
    return (block_out, grad_hidden, totals[0], totals[1], totals[2], totals[3], totals[4], totals[5], totals[6], totals[7], totals[8], totals[9])
```

```python
import functools

import jax
import jax.numpy as jnp
from jax import lax
from jax.experimental import pallas as pl
from jax.experimental.pallas import tpu as pltpu
from jax.sharding import PartitionSpec as P

M = 3
epsilon = 1e-05
LANES = 128
log2e = 1.4426950408889634
bf16 = jnp.bfloat16
f32 = jnp.float32


def contract(a, b, ca, cb):
    return lax.dot_general(a, b, (((ca,), (cb,)), ((), ())), preferred_element_type=f32)


def pick(mod, parts):
    out = parts[-1]
    for m in reversed(range(len(parts) - 1)):
        out = jnp.where(mod == m, parts[m], out)
    return out


def sigmoid(v):
    return 1.0 / (1.0 + jnp.exp(-v))


def fold_rows(vs):
    sub = lax.broadcasted_iota(jnp.int32, vs[0].shape, 0)
    for shift in (1, 2, 4):
        mask = (sub & shift) == 0
        vs = [
            jnp.where(mask, a, b) + pltpu.roll(jnp.where(mask, b, a), shift, 0)
            for a, b in zip(vs[0::2], vs[1::2])
        ]
    return vs[0]


def lane_total(v):
    width = v.shape[1] // LANES
    total = v[:, :LANES]
    for k in range(1, width):
        total = total + v[:, k * LANES : (k + 1) * LANES]
    return jnp.sum(total, axis=1, keepdims=True)


def cost(flops, nbytes):
    return pl.CostEstimate(flops=int(flops), bytes_accessed=int(nbytes), transcendentals=0)


def in_body(x_ref, wc_ref, wg_ref, cw_ref, cb_ref, sp_ref, modc_ref, modr_ref,
            ci_ref, gate_ref, act_ref, proj_ref, pad, *, rows, block):
    tile = pl.program_id(0)
    pad[0:8, :] = jnp.zeros((8, pad.shape[1]), f32)

    def matmul(r, _):
        at = pl.multiple_of(r * block, block)
        x = x_ref[pl.ds(at, block), :]
        mc = modc_ref[pl.ds(at, block), :]
        conv = pick(mc, [contract(x, wc_ref[m], 1, 0) for m in range(M)]).astype(bf16)
        ci_ref[pl.ds(at, block), :] = conv
        pad[pl.ds(at + 8, block), :] = conv.astype(f32)
        gate_ref[pl.ds(at, block), :] = pick(
            mc, [contract(x, wg_ref[m], 1, 0) for m in range(M)]
        ).astype(bf16)
        return 0

    lax.fori_loop(0, rows // block, matmul, 0)
    taps = cw_ref[...]
    base = cb_ref[...]

    def convolve(r, _):
        at = pl.multiple_of(r * LANES, LANES)
        v = pad[pl.ds(at, LANES + 8), :]
        s = base
        for k in range(4):
            s = s + taps[k : k + 1, :] * v[5 + k : 5 + k + LANES, :]
        act = (s * sigmoid(s)).astype(bf16)
        act_ref[pl.ds(at, LANES), :] = act
        part = pick(modr_ref[r], [contract(sp_ref[m], act, 1, 1) for m in range(M)])

        @pl.when(tile == 0)
        def _():
            proj_ref[r] = part

        @pl.when(tile != 0)
        def _():
            proj_ref[r] += part

        return 0

    lax.fori_loop(0, rows // LANES, convolve, 0)


def input_stage(x, w, cw, cb, sp, modc, modr):
    rows, width = x.shape
    chans = cw.shape[1]
    psize = sp.shape[1]
    tc = min(256, chans)
    tiles = chans // tc
    full = lambda shape: pl.BlockSpec(shape, lambda j: (0,) * len(shape))
    col = lambda r: pl.BlockSpec((r, tc), lambda j: (0, j))
    return pl.pallas_call(
        functools.partial(in_body, rows=rows, block=256),
        grid=(tiles,),
        in_specs=[
            full((rows, width)),
            pl.BlockSpec((M, width, tc), lambda j: (0, 0, j)),
            pl.BlockSpec((M, width, tc), lambda j: (0, 0, j + tiles)),
            col(4),
            col(1),
            pl.BlockSpec((M, psize, tc), lambda j: (0, 0, j)),
            full((rows, 1)),
            full(modr.shape),
        ],
        out_specs=[col(rows), col(rows), col(rows), full((rows // LANES, psize, LANES))],
        out_shape=[
            jax.ShapeDtypeStruct((rows, chans), bf16),
            jax.ShapeDtypeStruct((rows, chans), bf16),
            jax.ShapeDtypeStruct((rows, chans), bf16),
            jax.ShapeDtypeStruct((rows // LANES, psize, LANES), f32),
        ],
        scratch_shapes=[pltpu.VMEM((rows + 8, tc), f32)],
        cost_estimate=cost(2 * M * rows * width * 2 * chans, 2 * (rows * width + M * width * 2 * chans)),
        name="input_stage",
    )(x, w, w, cw, cb, sp, modc, modr)


def mm_body(x_ref, w_ref, modc_ref, o_ref, *, rows, block, rhs_dim):
    def step(r, _):
        at = pl.multiple_of(r * block, block)
        x = x_ref[pl.ds(at, block), :]
        mc = modc_ref[pl.ds(at, block), :]
        o_ref[pl.ds(at, block), :] = pick(
            mc, [contract(x, w_ref[m], 1, rhs_dim) for m in range(M)]
        ).astype(o_ref.dtype)
        return 0

    lax.fori_loop(0, rows // block, step, 0)


def select_matmul(x, w, modc, transposed, dtype, name):
    rows, depth = x.shape
    cols = w.shape[1] if transposed else w.shape[2]
    tn = min(256, cols)
    wspec = (
        pl.BlockSpec((M, tn, depth), lambda j: (0, j, 0))
        if transposed
        else pl.BlockSpec((M, depth, tn), lambda j: (0, 0, j))
    )
    return pl.pallas_call(
        functools.partial(mm_body, rows=rows, block=256, rhs_dim=1 if transposed else 0),
        grid=(cols // tn,),
        in_specs=[
            pl.BlockSpec((rows, depth), lambda j: (0, 0)),
            wspec,
            pl.BlockSpec((rows, 1), lambda j: (0, 0)),
        ],
        out_specs=pl.BlockSpec((rows, tn), lambda j: (0, j)),
        out_shape=jax.ShapeDtypeStruct((rows, cols), dtype),
        cost_estimate=cost(2 * M * rows * depth * cols, 2 * (rows * depth + M * depth * cols + rows * cols)),
        name=name,
    )(x, w, modc)


def dgrad_body(gc_ref, gg_ref, wc_ref, modc_ref, o_ref, *, rows, block, chans):
    def step(r, _):
        at = pl.multiple_of(r * block, block)
        gc = gc_ref[pl.ds(at, block), :]
        gg = gg_ref[pl.ds(at, block), :]
        mc = modc_ref[pl.ds(at, block), :]
        o_ref[pl.ds(at, block), :] = pick(
            mc,
            [
                contract(gc, wc_ref[m, :, :chans], 1, 1) + contract(gg, wc_ref[m, :, chans:], 1, 1)
                for m in range(M)
            ],
        ).astype(o_ref.dtype)
        return 0

    lax.fori_loop(0, rows // block, step, 0)


def input_dgrad(gc, gg, w, modc):
    rows, chans = gc.shape
    width = w.shape[1]
    tn = 256
    return pl.pallas_call(
        functools.partial(dgrad_body, rows=rows, block=256, chans=chans),
        grid=(width // tn,),
        in_specs=[
            pl.BlockSpec((rows, chans), lambda j: (0, 0)),
            pl.BlockSpec((rows, chans), lambda j: (0, 0)),
            pl.BlockSpec((M, tn, 2 * chans), lambda j: (0, j, 0)),
            pl.BlockSpec((rows, 1), lambda j: (0, 0)),
        ],
        out_specs=pl.BlockSpec((rows, tn), lambda j: (0, j)),
        out_shape=jax.ShapeDtypeStruct((rows, width), bf16),
        cost_estimate=cost(4 * M * rows * chans * width, 2 * (2 * rows * chans + 2 * M * chans * width + rows * width)),
        name="input_dgrad",
    )(gc, gg, w, modc)


def wgrad_body(pos_ref, xt_ref, g_ref, modl_ref, o_ref):
    g = g_ref[...]
    xt = xt_ref[...]
    for m in range(M):
        o_ref[m] = contract(jnp.where(modl_ref[...] == m, xt, jnp.zeros_like(xt)), g, 1, 0).astype(o_ref.dtype)


def half_wgrad(half, xt, g, modl, dtype, name):
    width, rows = xt.shape
    cols = g.shape[1]
    td = min(256, width // 2)
    steps = width // 2 // td
    return pl.pallas_call(
        wgrad_body,
        grid_spec=pltpu.PrefetchScalarGridSpec(
            num_scalar_prefetch=1,
            grid=(steps,),
            in_specs=[
                pl.BlockSpec((td, rows), lambda i, pos: (i + pos[0] * steps, 0)),
                pl.BlockSpec((rows, cols), lambda i, pos: (0, 0)),
                pl.BlockSpec((1, rows), lambda i, pos: (0, 0)),
            ],
            out_specs=pl.BlockSpec((M, td, cols), lambda i, pos: (0, i, 0)),
        ),
        out_shape=jax.ShapeDtypeStruct((M, width // 2, cols), dtype),
        cost_estimate=cost(M * rows * width * cols, rows * width + 2 * rows * cols + 2 * M * width * cols),
        name=name,
    )(half, xt, g, modl)


def row_of(ref, t):
    return jnp.broadcast_to(ref[pl.ds(t, 1), :], (8, ref.shape[1]))


def scan_fwd_body(pj_ref, act_ref, gate_ref, gg_ref, sp_ref, sb_ref, ld_ref, skip_ref, modc_ref,
                  delta_ref, sig_ref, gated_ref, ggate_ref, prev_ref, gct_ref,
                  state, d_s, u_s, y_s, gs_s, r_s):
    span, chans = act_ref.shape
    rank = sp_ref.shape[1]

    @pl.when(pl.program_id(0) == 0)
    def _():
        state[...] = jnp.zeros_like(state)

    mc = modc_ref[...]
    step_in = pj_ref[0, :rank, :]
    pre = pick(mc, [contract(step_in, sp_ref[m], 0, 0) + sb_ref[m : m + 1, :] for m in range(M)])
    z = jnp.exp(-jnp.abs(pre))
    delta = (jnp.maximum(pre, 0.0) + jnp.log1p(z)).astype(bf16)
    delta_ref[...] = delta
    inv = 1.0 / (1.0 + z)
    sig_ref[...] = jnp.where(pre >= 0, inv, z * inv)
    act = act_ref[...].astype(f32)
    d = delta.astype(f32)
    d_s[...] = d
    u_s[...] = d * act
    gate = gate_ref[...].astype(f32)
    s = sigmoid(gate)
    ggf = gg_ref[...].astype(f32)
    gs_s[...] = ggf * (gate * s)
    r_s[...] = -jnp.exp(ld_ref[...]) * log2e
    b = pj_ref[0, rank : rank + 16, :].astype(f32) + pj_ref[0, rank + 32 : rank + 48, :].astype(f32)
    c = pj_ref[0, rank + 16 : rank + 32, :].astype(f32) + pj_ref[0, rank + 48 : rank + 64, :].astype(f32)
    lane = lax.broadcasted_iota(jnp.int32, (8, LANES), 1)

    def eight(i, carry):
        st0, st1, gc0, gc1 = carry
        back = lax.rem(span - i * 8, span)
        bb = pltpu.roll(b, back, 1)
        cc = pltpu.roll(c, back, 1)
        ys = []
        for j in range(8):
            t = i * 8 + j
            db, ub, gsb = row_of(d_s, t), row_of(u_s, t), row_of(gs_s, t)
            at = pl.multiple_of(t * 16, 16)
            prev_ref[pl.ds(at, 8), :] = st0
            prev_ref[pl.ds(at + 8, 8), :] = st1
            st0 = jnp.exp2(db * r_s[0:8, :]) * st0 + ub * bb[0:8, j : j + 1]
            st1 = jnp.exp2(db * r_s[8:16, :]) * st1 + ub * bb[8:16, j : j + 1]
            ys.append(st0 * cc[0:8, j : j + 1] + st1 * cc[8:16, j : j + 1])
            gc0 = jnp.where(lane == t, lane_total(st0 * gsb), gc0)
            gc1 = jnp.where(lane == t, lane_total(st1 * gsb), gc1)
        y_s[pl.ds(pl.multiple_of(i * 8, 8), 8), :] = fold_rows(ys)
        return st0, st1, gc0, gc1

    none = jnp.zeros((8, LANES), f32)
    st0, st1, gc0, gc1 = lax.fori_loop(0, span // 8, eight, (state[0:8, :], state[8:16, :], none, none))
    state[0:8, :] = st0
    state[8:16, :] = st1
    gct_ref[0, 0:8, :] = gc0
    gct_ref[0, 8:16, :] = gc1
    scanned = y_s[...] + skip_ref[...] * act
    gated_ref[...] = (scanned * (gate * s)).astype(bf16)
    ggate_ref[...] = (ggf * scanned * (s * (1.0 + gate * (1.0 - s)))).astype(bf16)


def scan_forward(pj, act, gate, gg, step_proj, step_bias, log_decay, skip, modc):
    rows, chans = act.shape
    blocks = rows // LANES
    rank = step_proj.shape[1]
    row = pl.BlockSpec((LANES, chans), lambda i: (i, 0))
    full = lambda shape: pl.BlockSpec(shape, lambda i: (0,) * len(shape))
    return pl.pallas_call(
        scan_fwd_body,
        grid=(blocks,),
        in_specs=[
            pl.BlockSpec((1,) + pj.shape[1:], lambda i: (i, 0, 0)),
            row, row, row,
            full((M, rank, chans)),
            full((M, chans)),
            full((16, chans)),
            full((1, chans)),
            pl.BlockSpec((LANES, 1), lambda i: (i, 0)),
        ],
        out_specs=[
            row, row, row, row,
            pl.BlockSpec((LANES * 16, chans), lambda i: (i, 0)),
            pl.BlockSpec((1, 16, LANES), lambda i: (i, 0, 0)),
        ],
        out_shape=[
            jax.ShapeDtypeStruct((rows, chans), bf16),
            jax.ShapeDtypeStruct((rows, chans), f32),
            jax.ShapeDtypeStruct((rows, chans), bf16),
            jax.ShapeDtypeStruct((rows, chans), bf16),
            jax.ShapeDtypeStruct((rows * 16, chans), f32),
            jax.ShapeDtypeStruct((blocks, 16, LANES), f32),
        ],
        scratch_shapes=[pltpu.VMEM((16, chans), f32)] + [pltpu.VMEM((LANES, chans), f32)] * 4 + [pltpu.VMEM((16, chans), f32)],
        cost_estimate=cost(40e9, 64 * rows * chans + 20 * rows * chans),
        name="scan_forward",
    )(pj, act, gate, gg, step_proj, step_bias, log_decay, skip, modc)


def scan_bwd_body(pj_ref, act_ref, gate_ref, gg_ref, delta_ref, sig_ref, prev_ref, gct_ref,
                  sp_ref, ld_ref, skip_ref, modc_ref, modr_ref,
                  gas_ref, gpt_ref, glogd_ref, gskip_ref, gbias_ref, gstep_ref,
                  carry_w, acc, d_s, u_s, gs_s, g_s, h_s, r_s, n_s):
    span, chans = act_ref.shape
    rank = sp_ref.shape[1]
    first = pl.program_id(0) == 0

    @pl.when(first)
    def _():
        carry_w[...] = jnp.zeros_like(carry_w)
        acc[...] = jnp.zeros_like(acc)
        gskip_ref[...] = jnp.zeros_like(gskip_ref)
        gbias_ref[...] = jnp.zeros_like(gbias_ref)
        gstep_ref[...] = jnp.zeros_like(gstep_ref)

    act = act_ref[...].astype(f32)
    d = delta_ref[...].astype(f32)
    gate = gate_ref[...].astype(f32)
    gs = gg_ref[...].astype(f32) * (gate * sigmoid(gate))
    d_s[...] = d
    u_s[...] = d * act
    gs_s[...] = gs
    rates = -jnp.exp(ld_ref[...])
    n_s[...] = rates
    r_s[...] = rates * log2e
    b = pj_ref[0, rank : rank + 16, :].astype(f32) + pj_ref[0, rank + 32 : rank + 48, :].astype(f32)
    c = pj_ref[0, rank + 16 : rank + 32, :].astype(f32) + pj_ref[0, rank + 48 : rank + 64, :].astype(f32)
    lane = lax.broadcasted_iota(jnp.int32, (8, LANES), 1)

    def eight(k, carry):
        w0, w1, gb0, gb1 = carry
        i = span // 8 - 1 - k
        back = lax.rem(span - i * 8, span)
        bb = pltpu.roll(b, back, 1)
        cc = pltpu.roll(c, back, 1)
        gl = [None] * 8
        hl = [None] * 8
        for j in reversed(range(8)):
            t = i * 8 + j
            db, ub, gsb = row_of(d_s, t), row_of(u_s, t), row_of(gs_s, t)
            at = pl.multiple_of(t * 16, 16)
            a0 = gsb * cc[0:8, j : j + 1] + w0
            a1 = gsb * cc[8:16, j : j + 1] + w1
            gl[j] = a0 * bb[0:8, j : j + 1] + a1 * bb[8:16, j : j + 1]
            w0 = jnp.exp2(db * r_s[0:8, :]) * a0
            w1 = jnp.exp2(db * r_s[8:16, :]) * a1
            q0 = w0 * prev_ref[pl.ds(at, 8), :]
            q1 = w1 * prev_ref[pl.ds(at + 8, 8), :]
            hl[j] = q0 * n_s[0:8, :] + q1 * n_s[8:16, :]
            acc[0:8, :] += q0 * db
            acc[8:16, :] += q1 * db
            gb0 = jnp.where(lane == t, lane_total(a0 * ub), gb0)
            gb1 = jnp.where(lane == t, lane_total(a1 * ub), gb1)
        at8 = pl.ds(pl.multiple_of(i * 8, 8), 8)
        g_s[at8, :] = fold_rows(gl)
        h_s[at8, :] = fold_rows(hl)
        return w0, w1, gb0, gb1

    none = jnp.zeros((8, LANES), f32)
    w0, w1, gb0, gb1 = lax.fori_loop(0, span // 8, eight, (carry_w[0:8, :], carry_w[8:16, :], none, none))
    carry_w[0:8, :] = w0
    carry_w[8:16, :] = w1
    g = g_s[...]
    gas_ref[...] = (g * d + skip_ref[...] * gs).astype(bf16)
    gpre = (act * g + h_s[...]).astype(bf16).astype(f32) * sig_ref[...]
    glin = gpre.astype(bf16)
    mc = modc_ref[...]
    mr = modr_ref[0]
    step_in = pj_ref[0, :rank, :]
    sums = []
    for m in range(M):
        sums.append(jnp.sum(jnp.where(mc == m, gpre, 0.0), axis=0, keepdims=True))
        gstep_ref[m] += contract(jnp.where(mr == m, step_in, jnp.zeros_like(step_in)), glin, 1, 0)
    gbias_ref[...] += jnp.concatenate(sums, axis=0)
    gskip_ref[...] += jnp.sum(gs * act, axis=0, keepdims=True)
    gpt_ref[0, :rank, :] = pick(mr, [contract(sp_ref[m], glin, 1, 1) for m in range(M)]).astype(bf16)
    gpt_ref[0, rank : rank + 16, :] = jnp.concatenate([gb0, gb1], axis=0).astype(bf16)
    gpt_ref[0, rank + 16 : rank + 32, :] = gct_ref[0].astype(bf16)
    glogd_ref[...] = acc[...] * n_s[...]


def scan_backward(pj, act, gate, gg, delta, sig, prev, gct, step_proj, log_decay, skip, modc, modr):
    rows, chans = act.shape
    blocks = rows // LANES
    rank = step_proj.shape[1]
    last = blocks - 1
    row = pl.BlockSpec((LANES, chans), lambda i: (last - i, 0))
    full = lambda shape: pl.BlockSpec(shape, lambda i: (0,) * len(shape))
    slab = lambda shape: pl.BlockSpec((1,) + shape, lambda i: (last - i, 0, 0))
    return pl.pallas_call(
        scan_bwd_body,
        grid=(blocks,),
        in_specs=[
            slab(pj.shape[1:]),
            row, row, row, row, row,
            pl.BlockSpec((LANES * 16, chans), lambda i: (last - i, 0)),
            slab((16, LANES)),
            full((M, rank, chans)),
            full((16, chans)),
            full((1, chans)),
            pl.BlockSpec((LANES, 1), lambda i: (last - i, 0)),
            slab((1, LANES)),
        ],
        out_specs=[
            row,
            slab((rank + 32, LANES)),
            full((16, chans)),
            full((1, chans)),
            full((M, chans)),
            full((M, rank, chans)),
        ],
        out_shape=[
            jax.ShapeDtypeStruct((rows, chans), bf16),
            jax.ShapeDtypeStruct((blocks, rank + 32, LANES), bf16),
            jax.ShapeDtypeStruct((16, chans), f32),
            jax.ShapeDtypeStruct((1, chans), f32),
            jax.ShapeDtypeStruct((M, chans), f32),
            jax.ShapeDtypeStruct((M, rank, chans), f32),
        ],
        scratch_shapes=[pltpu.VMEM((16, chans), f32)] * 2 + [pltpu.VMEM((LANES, chans), f32)] * 5 + [pltpu.VMEM((16, chans), f32)] * 2,
        cost_estimate=cost(60e9, 64 * rows * chans + 20 * rows * chans),
        name="scan_backward",
    )(pj, act, gate, gg, delta, sig, prev, gct, step_proj, log_decay, skip, modc, modr)


def conv_bwd_body(gp_ref, sp_ref, gas_ref, ci_ref, act_ref, cw_ref, cb_ref, modc_ref, modr_ref,
                  gci_ref, gstate_ref, gcw_ref, pad, tail, *, rows):
    cols = pad.shape[1]
    pad[0:8, :] = jnp.zeros((8, cols), f32)
    tail[rows : rows + 8, :] = jnp.zeros((8, cols), f32)
    gstate_ref[...] = jnp.zeros_like(gstate_ref)
    taps = cw_ref[...]
    base = cb_ref[...]

    def first(r, sums):
        at = pl.multiple_of(r * LANES, LANES)
        here = pl.ds(at, LANES)
        pad[pl.ds(at + 8, LANES), :] = ci_ref[here, :].astype(f32)
        v = pad[pl.ds(at, LANES + 8), :]
        shifted = [v[5 + k : 5 + k + LANES, :] for k in range(4)]
        s = base
        for k in range(4):
            s = s + taps[k : k + 1, :] * shifted[k]
        sg = sigmoid(s)
        gp = gp_ref[r]
        ga = pick(modc_ref[here, :], [contract(gp, sp_ref[m], 0, 0) for m in range(M)])
        gcp = (ga + gas_ref[here, :].astype(f32)) * (sg * (1.0 + s * (1.0 - sg)))
        tail[here, :] = gcp
        act = act_ref[here, :]
        mr = modr_ref[r]
        for m in range(M):
            gstate_ref[m] += contract(jnp.where(mr == m, gp, jnp.zeros_like(gp)), act, 1, 0)
        terms = [gcp * part for part in shifted] + [gcp]
        return tuple(
            total + jnp.sum(term.reshape(LANES // 8, 8, cols), axis=0) for total, term in zip(sums, terms)
        )

    sums = lax.fori_loop(0, rows // LANES, first, (jnp.zeros((8, cols), f32),) * 5)
    gcw_ref[...] = jnp.concatenate(
        [jnp.sum(total, axis=0, keepdims=True) for total in sums] + [jnp.zeros((3, cols), f32)], axis=0
    )

    def second(r, _):
        at = pl.multiple_of(r * LANES, LANES)
        v = tail[pl.ds(at, LANES + 8), :]
        s = taps[0:1, :] * v[3 : 3 + LANES, :]
        for k in range(1, 4):
            s = s + taps[k : k + 1, :] * v[3 - k : 3 - k + LANES, :]
        gci_ref[pl.ds(at, LANES), :] = s.astype(bf16)
        return 0

    lax.fori_loop(0, rows // LANES, second, 0)


def conv_backward(gp, sp, gas, ci, act, cw, cb, modc, modr):
    rows, chans = ci.shape
    psize = sp.shape[1]
    tc = min(256, chans)
    col = lambda r: pl.BlockSpec((r, tc), lambda j: (0, j))
    full = lambda shape: pl.BlockSpec(shape, lambda j: (0,) * len(shape))
    wide = pl.BlockSpec((M, psize, tc), lambda j: (0, 0, j))
    return pl.pallas_call(
        functools.partial(conv_bwd_body, rows=rows),
        grid=(chans // tc,),
        in_specs=[full(gp.shape), wide, col(rows), col(rows), col(rows), col(4), col(1), full((rows, 1)), full(modr.shape)],
        out_specs=[col(rows), wide, col(8)],
        out_shape=[
            jax.ShapeDtypeStruct((rows, chans), bf16),
            jax.ShapeDtypeStruct((M, psize, chans), f32),
            jax.ShapeDtypeStruct((8, chans), f32),
        ],
        scratch_shapes=[pltpu.VMEM((rows + 8, tc), f32), pltpu.VMEM((rows + 8, tc), f32)],
        cost_estimate=cost(8 * M * rows * psize * chans, 10 * rows * chans),
        name="conv_backward",
    )(gp, sp, gas, ci, act, cw, cb, modc, modr)


def assemble_body(pos_ref, mc_ref, rc_ref, mg_ref, rg_ref, o_ref, *, half_steps):
    mine = pl.program_id(1) // half_steps == pos_ref[0]

    @pl.when(mine)
    def _():
        o_ref[0, :, 0, :] = mc_ref[0].astype(f32)
        o_ref[0, :, 1, :] = mg_ref[0].astype(f32)

    @pl.when(jnp.logical_not(mine))
    def _():
        o_ref[0, :, 0, :] = rc_ref[0].astype(f32)
        o_ref[0, :, 1, :] = rg_ref[0].astype(f32)


def assemble_input_grad(core, mine_conv, recv_conv, mine_gate, recv_gate):
    _, half, chans = mine_conv.shape
    td = 256
    steps = half // td
    own_map = lambda m, i, pos: (m, jnp.where(i // steps == pos[0], lax.rem(i, steps), 0), 0)
    other_map = lambda m, i, pos: (m, jnp.where(i // steps != pos[0], lax.rem(i, steps), 0), 0)
    mine = pl.BlockSpec((1, td, chans), own_map)
    recv = pl.BlockSpec((1, td, chans), other_map)
    return pl.pallas_call(
        functools.partial(assemble_body, half_steps=steps),
        grid_spec=pltpu.PrefetchScalarGridSpec(
            num_scalar_prefetch=1,
            grid=(M, 2 * steps),
            in_specs=[mine, recv, mine, recv],
            out_specs=pl.BlockSpec((1, td, 2, chans), lambda m, i, pos: (m, i, 0, 0)),
        ),
        out_shape=jax.ShapeDtypeStruct((M, 2 * half, 2, chans), f32),
        cost_estimate=cost(0, 24 * M * half * chans),
        name="assemble_input_grad",
    )(core, mine_conv, recv_conv, mine_gate, recv_gate)


def swap_core(value):
    count = lax.axis_size("batch")
    return lax.ppermute(value, "batch", [(i, i ^ 1) for i in range(count)])


def y_sum(value, wide):
    count = lax.axis_size("batch")
    chips = count // 2
    if chips == 2:
        other = lax.ppermute(value, "batch", [(i, i ^ 2) for i in range(count)])
        return value.astype(f32) + other.astype(f32)
    mine = lax.axis_index("batch") // 2
    buffer = jnp.zeros((chips,) + value.shape, value.dtype)
    for shift in range(chips):
        piece = value if shift == 0 else lax.ppermute(
            value, "batch", [(i, (i + 2 * shift) % count) for i in range(count)]
        )
        buffer = lax.dynamic_update_index_in_dim(buffer, piece, (mine + chips - shift) % chips, 0)
    return jnp.sum(buffer.astype(f32), axis=0)


def batch_total(value):
    return y_sum(value + swap_core(value), True)


def to_owners(pieces):
    return lax.all_to_all(pieces, "own", split_axis=0, concat_axis=0, tiled=False)


def to_all(piece):
    return to_owners(jnp.broadcast_to(piece[None], (lax.axis_size("own"),) + piece.shape))


def split_total(mine, send):
    got = swap_core(send)
    half = (mine + got.astype(f32)).astype(bf16)
    total = y_sum(half, False).astype(bf16)
    return total, swap_core(total)


def join_halves(core, mine, recv, axis):
    low = jnp.where(core == 0, mine, recv)
    high = jnp.where(core == 0, recv, mine)
    return jnp.concatenate([low, high], axis=axis)


def per_device(
    hidden_in, norm_gain, input_proj, conv_weight, conv_bias, state_proj, step_proj, step_bias,
    log_decay, skip_gain, output_proj, modality, grad_out,
):
    own_count = lax.axis_size("own")
    own_index = lax.axis_index("own")
    core = lax.axis_index("batch") % 2
    width = hidden_in.shape[2]
    rows = modality.shape[1]
    span = rows // own_count
    chans = input_proj.shape[3]
    rank = step_proj.shape[1]
    states = log_decay.shape[0]
    psize = state_proj.shape[2]
    chan_at = own_index * chans

    core_at = core.astype(jnp.int32).reshape(1)
    other_at = (1 - core).astype(jnp.int32).reshape(1)

    modc = modality.reshape(rows, 1)
    modl = modality.reshape(1, rows)
    modr = modality.reshape(rows // LANES, 1, LANES)
    w_in = input_proj.reshape(M, width, 2 * chans)
    sp_t = jnp.swapaxes(state_proj, 1, 2)
    part = lambda table: lax.dynamic_slice_in_dim(table, chan_at, chans, table.ndim - 1)
    cw = part(conv_weight)
    cb = part(conv_bias).reshape(1, chans)
    decay = part(log_decay)
    skip = part(skip_gain).reshape(1, chans)

    resid = hidden_in[0].astype(f32)
    inverse = lax.rsqrt(jnp.mean(resid * resid, axis=-1, keepdims=True) + epsilon)
    normed = (resid * inverse * norm_gain).astype(bf16)
    x = lax.all_gather(normed, "own", axis=0, tiled=True)
    cot = lax.all_gather(grad_out[0], "own", axis=0, tiled=True)

    conv_in, gate, act, proj_part = input_stage(x, w_in, cw, cb, sp_t, modc, modr)
    blocks = rows // LANES
    per_owner = blocks // own_count
    pieces = proj_part.astype(bf16).reshape(own_count, per_owner * psize, LANES)
    proj = jnp.sum(to_owners(pieces).astype(f32), axis=0).reshape(per_owner, psize, LANES)
    high = proj.astype(bf16)
    low = (proj[:, rank:] - high[:, rank:].astype(f32)).astype(bf16)
    packed = jnp.concatenate([high, low], axis=1)
    pj = to_all(packed).reshape(blocks, psize + 2 * states, LANES)
    gg = select_matmul(cot, output_proj, modc, True, bf16, "gated_grad")
    delta, sig, gated, ggate, prev, gct = scan_forward(
        pj, act, gate, gg, step_proj, step_bias, decay, skip, modc
    )
    branch = select_matmul(gated, output_proj, modc, False, f32, "output_stage")
    branch = lax.psum_scatter(branch, "own", scatter_dimension=0, tiled=True)
    block_out = (resid + branch).astype(bf16)[None]

    xt = jnp.swapaxes(x, 0, 1)
    gated_t = jnp.swapaxes(gated, 0, 1)
    out_send = half_wgrad(other_at, gated_t, cot, modl, bf16, "output_wgrad_send")
    out_mine = half_wgrad(core_at, gated_t, cot, modl, f32, "output_wgrad_keep")
    out_mine, out_recv = split_total(out_mine, out_send)
    grad_output = join_halves(core, out_mine, out_recv, 1).astype(f32)
    gate_send = half_wgrad(other_at, xt, ggate, modl, bf16, "gate_wgrad_send")
    gate_mine = half_wgrad(core_at, xt, ggate, modl, f32, "gate_wgrad_keep")
    gate_mine, gate_recv = split_total(gate_mine, gate_send)

    gas, gpt, glogd, gskip, gbias, gstep = scan_backward(
        pj, act, gate, gg, delta, sig, prev, gct, step_proj, decay, skip, modc, modr
    )
    gp_own = jnp.sum(to_owners(gpt.reshape(own_count, per_owner * psize, LANES)).astype(f32), axis=0).astype(bf16)
    gp = to_all(gp_own).reshape(blocks, psize, LANES)
    gci, gstate, gcw = conv_backward(gp, sp_t, gas, conv_in, act, cw, cb, modc, modr)

    conv_send = half_wgrad(other_at, xt, gci, modl, bf16, "conv_wgrad_send")
    conv_mine = half_wgrad(core_at, xt, gci, modl, f32, "conv_wgrad_keep")
    conv_mine, conv_recv = split_total(conv_mine, conv_send)
    gnormed = input_dgrad(gci, ggate, w_in, modc)
    gnormed = jnp.sum(to_owners(gnormed.reshape(own_count, span, width)).astype(f32), axis=0)

    weighted = norm_gain * gnormed
    coupled = jnp.mean(resid * weighted, axis=-1, keepdims=True)
    grad_hidden = (
        grad_out[0].astype(f32) + inverse * weighted - resid * (inverse * inverse * inverse) * coupled
    )[None]
    gain_part = jnp.sum(gnormed * resid * inverse, axis=0).reshape(width // LANES, LANES)
    grad_gain = batch_total(jnp.sum(to_all(gain_part), axis=0)).reshape(width)

    grad_input = assemble_input_grad(core_at, conv_mine, conv_recv, gate_mine, gate_recv)

    both = jnp.concatenate([gstep, gstate], axis=1)
    half_width = both.shape[1] // 2
    mine = lax.dynamic_slice_in_dim(both, core * half_width, half_width, 1)
    send = lax.dynamic_slice_in_dim(both, (1 - core) * half_width, half_width, 1).astype(bf16)
    mine, recv = split_total(mine, send)
    both = join_halves(core, mine, recv, 1).astype(f32)
    grad_step = both[:, :rank]
    grad_state = jnp.swapaxes(both[:, rank:], 1, 2)

    small = batch_total(jnp.concatenate([glogd, gcw[:5], gskip, gbias], axis=0))
    grad_bias = small[states + 6 :]
    wide = jnp.swapaxes(to_all(small[: states + 6]), 0, 1).reshape(states + 6, own_count * chans)
    return (
        block_out,
        grad_hidden,
        grad_gain,
        grad_input,
        wide[states : states + 4],
        wide[states + 4],
        grad_state,
        grad_step,
        grad_bias,
        wide[:states],
        wide[states + 5],
        grad_output,
    )


def solution(mesh):
    placed = (
        P("batch", "own", None),
        P(),
        P(None, None, None, "own"),
        P(),
        P(),
        P(None, "own", None),
        P(None, None, "own"),
        P(None, "own"),
        P(),
        P(),
        P(None, "own", None),
        P("batch", None),
        P("batch", "own", None),
    )
    return jax.shard_map(
        per_device,
        mesh=mesh,
        in_specs=placed,
        out_specs=(
            P("batch", "own", None),
            P("batch", "own", None),
            P(),
            P(None, None, None, "own"),
            P(),
            P(),
            P(None, "own", None),
            P(None, None, "own"),
            P(None, "own"),
            P(),
            P(),
            P(None, "own", None),
        ),
        check_vma=False,
    )
```

```python
import functools

import jax
import jax.numpy as jnp
from jax import lax
from jax.experimental import pallas as pl
from jax.experimental.pallas import tpu as pltpu
from jax.sharding import PartitionSpec as P

M = 3
epsilon = 1e-05
LANES = 128
log2e = 1.4426950408889634
bf16 = jnp.bfloat16
f32 = jnp.float32


def contract(a, b, ca, cb):
    return lax.dot_general(a, b, (((ca,), (cb,)), ((), ())), preferred_element_type=f32)


def pick(mod, parts):
    out = parts[-1]
    for m in reversed(range(len(parts) - 1)):
        out = jnp.where(mod == m, parts[m], out)
    return out


def sigmoid(v):
    return 1.0 / (1.0 + jnp.exp(-v))


def fold_rows(vs):
    sub = lax.broadcasted_iota(jnp.int32, vs[0].shape, 0)
    for shift in (1, 2, 4):
        mask = (sub & shift) == 0
        vs = [
            jnp.where(mask, a, b) + pltpu.roll(jnp.where(mask, b, a), shift, 0)
            for a, b in zip(vs[0::2], vs[1::2])
        ]
    return vs[0]


def fold_lanes(vs, shifts):
    lane = lax.broadcasted_iota(jnp.int32, vs[0].shape, 1)
    for shift in shifts:
        mask = (lane & shift) == 0
        vs = [
            jnp.where(mask, a, b) + pltpu.roll(jnp.where(mask, b, a), shift, 1)
            for a, b in zip(vs[0::2], vs[1::2])
        ]
    return vs[0]


def cost(flops, nbytes):
    return pl.CostEstimate(flops=int(flops), bytes_accessed=int(nbytes), transcendentals=0)


def in_body(x_ref, wc_ref, wg_ref, cw_ref, cb_ref, sp_ref, modc_ref, modr_ref,
            ci_ref, gate_ref, act_ref, proj_ref, pad, sums, *, rows, block):
    tile = pl.program_id(0)
    pad[0:8, :] = jnp.zeros((8, pad.shape[1]), f32)

    def matmul(r, _):
        at = pl.multiple_of(r * block, block)
        x = x_ref[pl.ds(at, block), :]
        mc = modc_ref[pl.ds(at, block), :]
        conv = pick(mc, [contract(x, wc_ref[m], 1, 0) for m in range(M)]).astype(bf16)
        ci_ref[pl.ds(at, block), :] = conv
        pad[pl.ds(at + 8, block), :] = conv.astype(f32)
        gate_ref[pl.ds(at, block), :] = pick(
            mc, [contract(x, wg_ref[m], 1, 0) for m in range(M)]
        ).astype(bf16)
        return 0

    lax.fori_loop(0, rows // block, matmul, 0)
    taps = cw_ref[...]
    base = cb_ref[...]

    def convolve(r, _):
        at = pl.multiple_of(r * LANES, LANES)
        v = pad[pl.ds(at, LANES + 8), :]
        s = base
        for k in range(4):
            s = s + taps[k : k + 1, :] * v[5 + k : 5 + k + LANES, :]
        act = (s * sigmoid(s)).astype(bf16)
        act_ref[pl.ds(at, LANES), :] = act
        part = pick(modr_ref[r], [contract(sp_ref[m], act, 1, 1) for m in range(M)])

        @pl.when(tile == 0)
        def _():
            sums[r] = part

        @pl.when(tile != 0)
        def _():
            sums[r] += part

        proj_ref[r] = sums[r].astype(bf16)
        return 0

    lax.fori_loop(0, rows // LANES, convolve, 0)


def input_stage(x, w, cw, cb, sp, modc, modr):
    rows, width = x.shape
    chans = cw.shape[1]
    psize = sp.shape[1]
    tc = min(256, chans)
    tiles = chans // tc
    full = lambda shape: pl.BlockSpec(shape, lambda j: (0,) * len(shape))
    col = lambda r: pl.BlockSpec((r, tc), lambda j: (0, j))
    return pl.pallas_call(
        functools.partial(in_body, rows=rows, block=min(256, rows)),
        grid=(tiles,),
        in_specs=[
            full((rows, width)),
            pl.BlockSpec((M, width, tc), lambda j: (0, 0, j)),
            pl.BlockSpec((M, width, tc), lambda j: (0, 0, j + tiles)),
            col(4),
            col(1),
            pl.BlockSpec((M, psize, tc), lambda j: (0, 0, j)),
            full((rows, 1)),
            full(modr.shape),
        ],
        out_specs=[col(rows), col(rows), col(rows), full((rows // LANES, psize, LANES))],
        out_shape=[
            jax.ShapeDtypeStruct((rows, chans), bf16),
            jax.ShapeDtypeStruct((rows, chans), bf16),
            jax.ShapeDtypeStruct((rows, chans), bf16),
            jax.ShapeDtypeStruct((rows // LANES, psize, LANES), bf16),
        ],
        scratch_shapes=[pltpu.VMEM((rows + 8, tc), f32), pltpu.VMEM((rows // LANES, psize, LANES), f32)],
        cost_estimate=cost(2 * M * rows * width * 2 * chans, 2 * (rows * width + M * width * 2 * chans)),
        name="input_stage",
    )(x, w, w, cw, cb, sp, modc, modr)


def mm_body(x_ref, w_ref, modc_ref, o_ref, *, rows, block, rhs_dim):
    def step(r, _):
        at = pl.multiple_of(r * block, block)
        x = x_ref[pl.ds(at, block), :]
        mc = modc_ref[pl.ds(at, block), :]
        o_ref[pl.ds(at, block), :] = pick(
            mc, [contract(x, w_ref[m], 1, rhs_dim) for m in range(M)]
        ).astype(o_ref.dtype)
        return 0

    lax.fori_loop(0, rows // block, step, 0)


def select_matmul(x, w, modc, transposed, dtype, name):
    rows, depth = x.shape
    cols = w.shape[1] if transposed else w.shape[2]
    tn = min(256, cols)
    wspec = (
        pl.BlockSpec((M, tn, depth), lambda j: (0, j, 0))
        if transposed
        else pl.BlockSpec((M, depth, tn), lambda j: (0, 0, j))
    )
    return pl.pallas_call(
        functools.partial(mm_body, rows=rows, block=min(512, rows), rhs_dim=1 if transposed else 0),
        grid=(cols // tn,),
        in_specs=[
            pl.BlockSpec((rows, depth), lambda j: (0, 0)),
            wspec,
            pl.BlockSpec((rows, 1), lambda j: (0, 0)),
        ],
        out_specs=pl.BlockSpec((rows, tn), lambda j: (0, j)),
        out_shape=jax.ShapeDtypeStruct((rows, cols), dtype),
        cost_estimate=cost(2 * M * rows * depth * cols, 2 * (rows * depth + M * depth * cols + rows * cols)),
        name=name,
    )(x, w, modc)


def gated_body(x_ref, w_ref, modc_ref, scanned_ref, gate_ref, gg_ref, ggate_ref):
    block = min(512, x_ref.shape[0])

    def step(r, _):
        here = pl.ds(pl.multiple_of(r * block, block), block)
        x = x_ref[here, :]
        gg = pick(modc_ref[here, :], [contract(x, w_ref[m], 1, 1) for m in range(M)]).astype(bf16)
        gg_ref[here, :] = gg
        gate = gate_ref[here, :].astype(f32)
        s = sigmoid(gate)
        ggate_ref[here, :] = (gg.astype(f32) * scanned_ref[here, :] * (s * (1.0 + gate * (1.0 - s)))).astype(bf16)
        return 0

    lax.fori_loop(0, x_ref.shape[0] // block, step, 0)


def gated_grads(cot, w, modc, scanned, gate):
    rows, depth = cot.shape
    cols = w.shape[1]
    tn = min(256, cols)
    col = pl.BlockSpec((rows, tn), lambda j: (0, j))
    return pl.pallas_call(
        gated_body,
        grid=(cols // tn,),
        in_specs=[
            pl.BlockSpec((rows, depth), lambda j: (0, 0)),
            pl.BlockSpec((M, tn, depth), lambda j: (0, j, 0)),
            pl.BlockSpec((rows, 1), lambda j: (0, 0)),
            col,
            col,
        ],
        out_specs=[col, col],
        out_shape=[jax.ShapeDtypeStruct((rows, cols), bf16)] * 2,
        cost_estimate=cost(2 * M * rows * depth * cols, 2 * (rows * depth + M * depth * cols + 5 * rows * cols)),
        name="gated_grads",
    )(cot, w, modc, scanned, gate)


def dgrad_body(gc_ref, gg_ref, w_ref, modc_ref, x_ref, gain_ref, o_ref, part_ref, *, rows, block, chans):
    sums = jnp.zeros((8, part_ref.shape[1]), f32)
    for r in range(rows // block):
        here = slice(r * block, (r + 1) * block)
        gc = gc_ref[here, :]
        gg = gg_ref[here, :]
        out = pick(
            modc_ref[here, :],
            [contract(gc, w_ref[m, :, :chans], 1, 1) + contract(gg, w_ref[m, :, chans:], 1, 1) for m in range(M)],
        )
        o_ref[here, :] = out.astype(bf16)
        terms = out * x_ref[here, :].astype(f32)
        sums = sums + jnp.sum(terms.reshape(block // 8, 8, terms.shape[1]), axis=0)
    part_ref[...] = jnp.sum(sums, axis=0, keepdims=True) / gain_ref[...]


def input_dgrad(gc, gg, w, modc, x, gain):
    rows, chans = gc.shape
    width = w.shape[1]
    tn = 256
    col = pl.BlockSpec((rows, tn), lambda j: (0, j))
    row = pl.BlockSpec((1, tn), lambda j: (0, j))
    return pl.pallas_call(
        functools.partial(dgrad_body, rows=rows, block=min(1024, rows), chans=chans),
        grid=(width // tn,),
        in_specs=[
            pl.BlockSpec((rows, chans), lambda j: (0, 0)),
            pl.BlockSpec((rows, chans), lambda j: (0, 0)),
            pl.BlockSpec((M, tn, 2 * chans), lambda j: (0, j, 0)),
            pl.BlockSpec((rows, 1), lambda j: (0, 0)),
            col,
            row,
        ],
        out_specs=[col, row],
        out_shape=[jax.ShapeDtypeStruct((rows, width), bf16), jax.ShapeDtypeStruct((1, width), f32)],
        cost_estimate=cost(4 * M * rows * chans * width, 2 * (2 * rows * chans + 2 * M * chans * width + 2 * rows * width)),
        name="input_dgrad",
    )(gc, gg, w, modc, x, gain)


def wgrad_body(*refs, sets, add):
    xs, gs, mods = refs[1 : 1 + sets], refs[1 + sets : 1 + 2 * sets], refs[1 + 2 * sets : 1 + 3 * sets]
    o_ref, masked = refs[-2], refs[-1]

    @pl.when(pl.program_id(0) == 0)
    def _():
        for n in range(sets):
            g = gs[n][...]
            for m in range(M):
                masked[n, m] = jnp.where(mods[n][...] == m, g, jnp.zeros_like(g))

    there = refs[0][0] >= 0

    def each(m, _):
        parts = [jnp.where(there, contract(xs[n][...], masked[n, m], 0, 0), 0.0) for n in range(sets)]
        total = functools.reduce(jnp.add, parts)
        if add:
            total = total + refs[1 + 3 * sets][m].astype(f32)
        o_ref[m] = total.astype(bf16)
        return 0

    lax.fori_loop(0, M, each, 0)


def half_wgrad(half, xs, gs, mods, got, name):
    sets = len(xs)
    rows, width = xs[0].shape
    cols = gs[0].shape[1]
    td = min(512, width // 2)
    steps = width // 2 // td
    full = lambda shape: pl.BlockSpec(shape, lambda i, pos: (0, 0))
    out_spec = pl.BlockSpec((M, td, cols), lambda i, pos: (0, i, 0))
    extra = () if got is None else (got,)
    return pl.pallas_call(
        functools.partial(wgrad_body, sets=sets, add=got is not None),
        grid_spec=pltpu.PrefetchScalarGridSpec(
            num_scalar_prefetch=1,
            grid=(steps,),
            in_specs=[pl.BlockSpec((rows, td), lambda i, pos: (0, i + pos[0] * steps))] * sets
            + [full((rows, cols))] * sets
            + [full((rows, 1))] * sets
            + [out_spec] * len(extra),
            out_specs=out_spec,
            scratch_shapes=[pltpu.VMEM((sets, M, rows, cols), bf16)],
        ),
        out_shape=jax.ShapeDtypeStruct((M, width // 2, cols), bf16),
        cost_estimate=cost(sets * M * rows * width * cols, sets * (rows * width + 2 * rows * cols) + 2 * M * width * cols),
        name=name,
    )(half, *xs, *gs, *mods, *extra)


def rows_wgrad_body(pos_ref, xt_ref, g_ref, modl_ref, *rest, groups):
    outs = rest[len(rest) - len(groups) :]
    xt = xt_ref[...]
    for n, group in enumerate(groups):
        for k, m in enumerate(group):
            total = contract(jnp.where(modl_ref[...] == m, xt, jnp.zeros_like(xt)), g_ref[...], 1, 0)
            if len(rest) > len(groups):
                total = total + rest[n][k].astype(f32)
            outs[n][k] = total.astype(bf16)


def rows_wgrad(half, xt, g, modl, got, groups, name):
    width, rows = xt.shape
    cols = g.shape[1]
    tn = 512
    out_specs = [pl.BlockSpec((len(group), width // 2, tn), lambda i, pos: (0, 0, i)) for group in groups]
    return pl.pallas_call(
        functools.partial(rows_wgrad_body, groups=groups),
        grid_spec=pltpu.PrefetchScalarGridSpec(
            num_scalar_prefetch=1,
            grid=(cols // tn,),
            in_specs=[
                pl.BlockSpec((width // 2, rows), lambda i, pos: (pos[0], 0)),
                pl.BlockSpec((rows, tn), lambda i, pos: (0, i)),
                pl.BlockSpec((1, rows), lambda i, pos: (0, 0)),
            ]
            + (out_specs if got else []),
            out_specs=out_specs,
        ),
        out_shape=[jax.ShapeDtypeStruct((len(group), width // 2, cols), bf16) for group in groups],
        cost_estimate=cost(M * rows * width * cols, rows * width + 2 * rows * cols + 2 * M * width * cols),
        name=name,
    )(half, xt, g, modl, *got)


UNROLL = 4


def spread(value, ref):
    for t in range(LANES):
        ref[t] = jnp.broadcast_to(value[:, t : t + 1], (16, LANES))


def fold_columns(ref):
    halves = []
    for h in range(2):
        groups = [
            fold_lanes([ref[8 * i + j, 8 * h : 8 * h + 8, :] for j in range(8)], (1, 2, 4)) for i in range(16)
        ]
        halves.append(fold_lanes(groups, (8, 16, 32, 64)))
    return jnp.concatenate(halves, axis=0)


def row_of(ref, t):
    wide = jnp.broadcast_to(ref[pl.ds(t, 1), :], (8, ref.shape[1]))
    return [wide[:, k * LANES : (k + 1) * LANES] for k in range(ref.shape[1] // LANES)]


def add_all(parts):
    while len(parts) > 1:
        parts = [functools.reduce(jnp.add, parts[k : k + 2]) for k in range(0, len(parts), 2)]
    return parts[0]


def state_vectors(pj_ref, rank):
    b = pj_ref[0, rank : rank + 16, :].astype(f32) + pj_ref[0, rank + 32 : rank + 48, :].astype(f32)
    c = pj_ref[0, rank + 16 : rank + 32, :].astype(f32) + pj_ref[0, rank + 48 : rank + 64, :].astype(f32)
    return b, c


def by_modality(mod, rows):
    return jnp.concatenate([jnp.where(mod == m, rows, jnp.zeros_like(rows)) for m in range(M)], axis=0)


def fold_all(ref):
    groups = [fold_rows([ref[8 * i + j] for j in range(8)]) for i in range(LANES // 8)]
    return jnp.concatenate(groups, axis=0)


def scan_fwd_body(pj_ref, act_ref, gate_ref, sp_ref, sb_ref, ld_ref, skip_ref, modc_ref, modr_ref,
                  delta_ref, sig_ref, gated_ref, scanned_ref, prev_ref, final_ref,
                  state, pre_s, d_s, u_s, r_s, b_s, c_s, yp_s):
    span, chans = act_ref.shape
    rank = pj_ref.shape[1] - 64
    tiles = chans // LANES

    @pl.when(pl.program_id(0) == 0)
    def _():
        state[...] = jnp.zeros_like(state)

    pre_s[...] = contract(by_modality(modr_ref[0], pj_ref[0, :rank, :]), sp_ref[...], 0, 0)
    r_s[...] = -jnp.exp(ld_ref[...]) * log2e
    b, c = state_vectors(pj_ref, rank)
    spread(b, b_s)
    spread(c, c_s)
    bias = [sb_ref[m : m + 1, :] for m in range(M)]

    pre = pre_s[...] + pick(modc_ref[...], bias)
    z = jnp.exp(-jnp.abs(pre))
    delta = (jnp.maximum(pre, 0.0) + jnp.log1p(z)).astype(bf16)
    delta_ref[...] = delta
    inv = 1.0 / (1.0 + z)
    sig_ref[...] = jnp.where(pre >= 0, inv, z * inv)
    act = act_ref[...].astype(f32)
    d = delta.astype(f32)
    d_s[...] = d
    u_s[...] = d * act

    def positions(i, carry):
        st = list(carry)
        for j in range(UNROLL):
            t = i * UNROLL + j
            at = pl.multiple_of(t * 16, 16)
            d_row, u_row = row_of(d_s, t), row_of(u_s, t)
            for k in range(tiles):
                cols = slice(k * LANES, (k + 1) * LANES)
                out = []
                for h in range(2):
                    n = 2 * k + h
                    rows = slice(8 * h, 8 * h + 8)
                    prev_ref[pl.ds(at + 8 * h, 8), cols] = st[n]
                    st[n] = jnp.exp2(d_row[k] * r_s[rows, cols]) * st[n] + u_row[k] * b_s[t, rows, :]
                    out.append(st[n] * c_s[t, rows, :])
                yp_s[t, :, cols] = out[0] + out[1]
        return tuple(st)

    first = tuple(
        state[8 * h : 8 * h + 8, k * LANES : (k + 1) * LANES] for k in range(tiles) for h in range(2)
    )
    st = lax.fori_loop(0, span // UNROLL, positions, first)
    for k in range(tiles):
        for h in range(2):
            state[8 * h : 8 * h + 8, k * LANES : (k + 1) * LANES] = st[2 * k + h]
    final_ref[...] = state[...]
    scanned = fold_all(yp_s) + skip_ref[...] * act
    scanned_ref[...] = scanned
    gate = gate_ref[...].astype(f32)
    gated_ref[...] = (scanned * (gate * sigmoid(gate))).astype(bf16)


def scan_forward(pj, act, gate, step_proj, step_bias, log_decay, skip, modc, modr):
    rows, chans = act.shape
    blocks = rows // LANES
    row = pl.BlockSpec((LANES, chans), lambda i: (i, 0))
    full = lambda shape: pl.BlockSpec(shape, lambda i: (0,) * len(shape))
    return pl.pallas_call(
        scan_fwd_body,
        grid=(blocks,),
        in_specs=[
            pl.BlockSpec((1,) + pj.shape[1:], lambda i: (i, 0, 0)),
            row, row,
            full(step_proj.shape),
            full((M, chans)),
            full((16, chans)),
            full((1, chans)),
            pl.BlockSpec((LANES, 1), lambda i: (i, 0)),
            pl.BlockSpec((1, 1, LANES), lambda i: (i, 0, 0)),
        ],
        out_specs=[
            row, row, row, row,
            pl.BlockSpec((LANES * 16, chans), lambda i: (i, 0)),
            full((16, chans)),
        ],
        out_shape=[
            jax.ShapeDtypeStruct((rows, chans), bf16),
            jax.ShapeDtypeStruct((rows, chans), f32),
            jax.ShapeDtypeStruct((rows, chans), bf16),
            jax.ShapeDtypeStruct((rows, chans), f32),
            jax.ShapeDtypeStruct((rows * 16, chans), f32),
            jax.ShapeDtypeStruct((16, chans), f32),
        ],
        scratch_shapes=[pltpu.VMEM((16, chans), f32)] + [pltpu.VMEM((LANES, chans), f32)] * 3
        + [pltpu.VMEM((16, chans), f32)]
        + [pltpu.VMEM((LANES, 16, LANES), f32)] * 2
        + [pltpu.VMEM((LANES, 8, chans), f32)],
        cost_estimate=cost(40e9, 64 * rows * chans + 20 * rows * chans),
        name="scan_forward",
    )(pj, act, gate, step_proj, step_bias, log_decay, skip, modc, modr)


def scan_bwd_body(pj_ref, act_ref, gate_ref, gg_ref, delta_ref, sig_ref, prev_ref, final_ref,
                  sp_ref, ld_ref, skip_ref, modc_ref, modr_ref,
                  gas_ref, gpt_ref, glogd_ref, gskip_ref, gbias_ref, gstep_ref,
                  carry_w, acc, later, d_s, u_s, gs_s, r_s, b_s, c_s, gp_s, hp_s, p_s, q_s):
    span, chans = act_ref.shape
    rank = pj_ref.shape[1] - 64
    tiles = chans // LANES

    @pl.when(pl.program_id(0) == 0)
    def _():
        carry_w[...] = jnp.zeros_like(carry_w)
        acc[...] = jnp.zeros_like(acc)
        later[...] = final_ref[...]
        gskip_ref[...] = jnp.zeros_like(gskip_ref)
        gbias_ref[...] = jnp.zeros_like(gbias_ref)
        gstep_ref[...] = jnp.zeros_like(gstep_ref)

    rates = -jnp.exp(ld_ref[...])
    r_s[...] = rates * log2e
    b, c = state_vectors(pj_ref, rank)
    spread(b, b_s)
    spread(c, c_s)

    act = act_ref[...].astype(f32)
    d = delta_ref[...].astype(f32)
    gate = gate_ref[...].astype(f32)
    gs = gg_ref[...].astype(f32) * (gate * sigmoid(gate))
    d_s[...] = d
    u_s[...] = d * act
    gs_s[...] = gs

    def positions(i, carry):
        w, total = list(carry[0]), list(carry[1])
        for j in range(UNROLL):
            t = span - 1 - (i * UNROLL + j)
            at = pl.multiple_of(t * 16, 16)
            grad = []
            d_row, u_row, gs_row = row_of(d_s, t), row_of(u_s, t), row_of(gs_s, t)
            for k in range(tiles):
                cols = slice(k * LANES, (k + 1) * LANES)
                gl, hl = [], []
                for h in range(2):
                    n = 2 * k + h
                    rows = slice(8 * h, 8 * h + 8)
                    rate = r_s[rows, cols]
                    adj = gs_row[k] * c_s[t, rows, :] + w[n]
                    gl.append(adj * b_s[t, rows, :])
                    w[n] = jnp.exp2(d_row[k] * rate) * adj
                    q = w[n] * prev_ref[pl.ds(at + 8 * h, 8), cols]
                    hl.append(q * rate)
                    total[n] = total[n] + q * d_row[k]
                    grad.append(adj * u_row[k])
                gp_s[t, :, cols] = gl[0] + gl[1]
                hp_s[t, :, cols] = hl[0] + hl[1]
            p_s[t, 0:8, :] = add_all(grad[0::2])
            p_s[t, 8:16, :] = add_all(grad[1::2])
        return tuple(w), tuple(total)

    places = [(slice(8 * h, 8 * h + 8), slice(k * LANES, (k + 1) * LANES)) for k in range(tiles) for h in range(2)]
    def read_grad(t, state):
        gs_row = row_of(gs_s, t)
        for h in range(2):
            rows = slice(8 * h, 8 * h + 8)
            q_s[t, rows, :] = add_all(
                [state(h)[:, k * LANES : (k + 1) * LANES] * gs_row[k] for k in range(tiles)]
            )

    def reads(i, _):
        for j in range(UNROLL):
            t = i * UNROLL + j
            at = pl.multiple_of(jnp.minimum(t + 1, span - 1) * 16, 16)
            read_grad(t, lambda h: prev_ref[pl.ds(at + 8 * h, 8), :])
        return 0

    lax.fori_loop(0, span // UNROLL, reads, 0)
    read_grad(span - 1, lambda h: later[8 * h : 8 * h + 8, :])
    later[...] = prev_ref[0:16, :]

    @pl.when(pl.program_id(0) >= 0)
    def _():
        gpt_ref[0, rank + 16 : rank + 32, :] = fold_columns(q_s).astype(bf16)

    held = (carry_w, acc)
    results = lax.fori_loop(
        0, span // UNROLL, positions, tuple(tuple(ref[at] for at in places) for ref in held)
    )
    for ref, values in zip(held, results):
        for n, at in enumerate(places):
            ref[at] = values[n]
    gb = fold_columns(p_s)
    g = fold_all(gp_s)
    gas_ref[...] = (g * d + skip_ref[...] * gs).astype(bf16)
    gpre = (act * g + fold_all(hp_s) * (1.0 / log2e)).astype(bf16).astype(f32) * sig_ref[...]
    glin = gpre.astype(bf16)
    mc = modc_ref[...]
    gbias_ref[...] += jnp.concatenate(
        [jnp.sum(jnp.where(mc == m, gpre, 0.0), axis=0, keepdims=True) for m in range(M)], axis=0
    )
    gskip_ref[...] += jnp.sum(gs * act, axis=0, keepdims=True)
    mr = modr_ref[0]
    gstep_ref[...] += contract(by_modality(mr, pj_ref[0, :rank, :]), glin, 1, 0)
    lin = contract(sp_ref[...], glin, 1, 1)
    gpt_ref[0, :rank, :] = pick(mr, [lin[m * rank : (m + 1) * rank] for m in range(M)]).astype(bf16)
    gpt_ref[0, rank : rank + 16, :] = gb.astype(bf16)
    glogd_ref[...] = acc[...] * rates


def scan_backward(pj, act, gate, gg, delta, sig, prev, final, step_proj, log_decay, skip, modc, modr):
    rows, chans = act.shape
    blocks = rows // LANES
    rank = step_proj.shape[0] // M
    last = blocks - 1
    row = pl.BlockSpec((LANES, chans), lambda i: (last - i, 0))
    full = lambda shape: pl.BlockSpec(shape, lambda i: (0,) * len(shape))
    slab = lambda shape: pl.BlockSpec((1,) + shape, lambda i: (last - i, 0, 0))
    return pl.pallas_call(
        scan_bwd_body,
        grid=(blocks,),
        in_specs=[
            slab(pj.shape[1:]),
            row, row, row, row, row,
            pl.BlockSpec((LANES * 16, chans), lambda i: (last - i, 0)),
            full((16, chans)),
            full(step_proj.shape),
            full((16, chans)),
            full((1, chans)),
            pl.BlockSpec((LANES, 1), lambda i: (last - i, 0)),
            slab((1, LANES)),
        ],
        out_specs=[
            row,
            slab((rank + 32, LANES)),
            full((16, chans)),
            full((1, chans)),
            full((M, chans)),
            full(step_proj.shape),
        ],
        out_shape=[
            jax.ShapeDtypeStruct((rows, chans), bf16),
            jax.ShapeDtypeStruct((blocks, rank + 32, LANES), bf16),
            jax.ShapeDtypeStruct((16, chans), f32),
            jax.ShapeDtypeStruct((1, chans), f32),
            jax.ShapeDtypeStruct((M, chans), f32),
            jax.ShapeDtypeStruct(step_proj.shape, f32),
        ],
        scratch_shapes=[pltpu.VMEM((16, chans), f32)] * 3
        + [pltpu.VMEM((LANES, chans), f32)] * 3
        + [pltpu.VMEM((16, chans), f32)]
        + [pltpu.VMEM((LANES, 16, LANES), f32)] * 2
        + [pltpu.VMEM((LANES, 8, chans), f32)] * 2
        + [pltpu.VMEM((LANES, 16, LANES), f32)] * 2,
        cost_estimate=cost(60e9, 64 * rows * chans + 20 * rows * chans),
        name="scan_backward",
    )(pj, act, gate, gg, delta, sig, prev, final, step_proj, log_decay, skip, modc, modr)


def conv_bwd_body(gp_ref, sp_ref, gas_ref, ci_ref, act_ref, cw_ref, cb_ref, modc_ref, modr_ref,
                  gci_ref, gstate_ref, gcw_ref, pad, tail, *, rows):
    cols = pad.shape[1]
    pad[0:8, :] = jnp.zeros((8, cols), f32)
    tail[rows : rows + 8, :] = jnp.zeros((8, cols), f32)
    gstate_ref[...] = jnp.zeros_like(gstate_ref)
    taps = cw_ref[...]
    base = cb_ref[...]

    def first(r, sums):
        at = pl.multiple_of(r * LANES, LANES)
        here = pl.ds(at, LANES)
        pad[pl.ds(at + 8, LANES), :] = ci_ref[here, :].astype(f32)
        v = pad[pl.ds(at, LANES + 8), :]
        shifted = [v[5 + k : 5 + k + LANES, :] for k in range(4)]
        s = base
        for k in range(4):
            s = s + taps[k : k + 1, :] * shifted[k]
        sg = sigmoid(s)
        gp = gp_ref[r]
        ga = pick(modc_ref[here, :], [contract(gp, sp_ref[m], 0, 0) for m in range(M)])
        gcp = (ga + gas_ref[here, :].astype(f32)) * (sg * (1.0 + s * (1.0 - sg)))
        tail[here, :] = gcp
        act = act_ref[here, :]
        mr = modr_ref[r]
        for m in range(M):
            gstate_ref[m] += contract(jnp.where(mr == m, gp, jnp.zeros_like(gp)), act, 1, 0)
        terms = [gcp * part for part in shifted] + [gcp]
        return tuple(
            total + jnp.sum(term.reshape(LANES // 8, 8, cols), axis=0) for total, term in zip(sums, terms)
        )

    sums = lax.fori_loop(0, rows // LANES, first, (jnp.zeros((8, cols), f32),) * 5)
    gcw_ref[...] = jnp.concatenate(
        [jnp.sum(total, axis=0, keepdims=True) for total in sums] + [jnp.zeros((3, cols), f32)], axis=0
    )

    def second(r, _):
        at = pl.multiple_of(r * LANES, LANES)
        v = tail[pl.ds(at, LANES + 8), :]
        s = taps[0:1, :] * v[3 : 3 + LANES, :]
        for k in range(1, 4):
            s = s + taps[k : k + 1, :] * v[3 - k : 3 - k + LANES, :]
        gci_ref[pl.ds(at, LANES), :] = s.astype(bf16)
        return 0

    lax.fori_loop(0, rows // LANES, second, 0)


def conv_backward(gp, sp, gas, ci, act, cw, cb, modc, modr):
    rows, chans = ci.shape
    psize = sp.shape[1]
    tc = min(256, chans)
    col = lambda r: pl.BlockSpec((r, tc), lambda j: (0, j))
    full = lambda shape: pl.BlockSpec(shape, lambda j: (0,) * len(shape))
    wide = pl.BlockSpec((M, psize, tc), lambda j: (0, 0, j))
    return pl.pallas_call(
        functools.partial(conv_bwd_body, rows=rows),
        grid=(chans // tc,),
        in_specs=[full(gp.shape), wide, col(rows), col(rows), col(rows), col(4), col(1), full((rows, 1)), full(modr.shape)],
        out_specs=[col(rows), wide, col(8)],
        out_shape=[
            jax.ShapeDtypeStruct((rows, chans), bf16),
            jax.ShapeDtypeStruct((M, psize, chans), f32),
            jax.ShapeDtypeStruct((8, chans), f32),
        ],
        scratch_shapes=[pltpu.VMEM((rows + 8, tc), f32), pltpu.VMEM((rows + 8, tc), f32)],
        cost_estimate=cost(8 * M * rows * psize * chans, 10 * rows * chans),
        name="conv_backward",
    )(gp, sp, gas, ci, act, cw, cb, modc, modr)


def interleave_body(pos_ref, conv_ref, gate_ref, *rest, group):
    o_ref = rest[-1]
    sub = lax.broadcasted_iota(jnp.int32, (8, LANES), 0)

    def step(r, _):
        at = pl.multiple_of(r * group, group)
        sources = [ref[0, pl.ds(at, group), :].astype(f32) for ref in (conv_ref, gate_ref)]
        for h in range(group // 8):
            vs = [
                source[8 * h : 8 * h + 8, k * LANES : (k + 1) * LANES] for k in range(4) for source in sources
            ]
            for shift in (1, 2, 4):
                mask = (sub & shift) == 0
                swapped = list(vs)
                for j in range(8):
                    if j & shift == 0:
                        a, b = vs[j], vs[j | shift]
                        swapped[j] = jnp.where(mask, a, pltpu.roll(b, shift, 0))
                        swapped[j | shift] = jnp.where(mask, pltpu.roll(a, 8 - shift, 0), b)
                vs = swapped
            for d in range(8):
                o_ref[0, pl.ds((at + 8 * h + d) * 8, 8), :] = vs[d]
        return 0

    lax.fori_loop(0, conv_ref.shape[1] // group, step, 0)


def split_body(pos_ref, conv_ref, gate_ref, *rest):
    o_ref = rest[-1]
    o_ref[0, :, 0, :] = conv_ref[0].astype(f32)
    o_ref[0, :, 1, :] = gate_ref[0].astype(f32)


def place_input_grad(half, conv, gate, target):
    _, height, chans = conv.shape
    td = min(512, height)
    steps = height // td
    packed = chans == 4 * LANES
    if packed:
        shape, block = (M, 2 * height * 8, LANES), (1, td * 8, LANES)
        where = lambda m, i, pos: (m, i + pos[0] * steps, 0)
        body = functools.partial(interleave_body, group=64)
    else:
        shape, block = (M, 2 * height, 2, chans), (1, td, 2, chans)
        where = lambda m, i, pos: (m, i + pos[0] * steps, 0, 0)
        body = split_body
    source = pl.BlockSpec((1, td, chans), lambda m, i, pos: (m, i, 0))
    extra = () if target is None else (target,)
    return pl.pallas_call(
        body,
        grid_spec=pltpu.PrefetchScalarGridSpec(
            num_scalar_prefetch=1,
            grid=(M, steps),
            in_specs=[source, source] + [pl.BlockSpec(memory_space=pl.ANY)] * len(extra),
            out_specs=pl.BlockSpec(block, where),
        ),
        out_shape=jax.ShapeDtypeStruct(shape, f32),
        input_output_aliases={} if target is None else {3: 0},
        cost_estimate=cost(0, 12 * M * height * chans),
        name="place_input_grad",
    )(half, conv, gate, *extra)


def input_grad_layout(value, width, chans):
    if value.ndim == 4:
        return value
    return value.reshape(M, width, chans // LANES, 2, LANES).transpose(0, 1, 3, 2, 4).reshape(M, width, 2, chans)


def join_body(pos_ref, mine_ref, got_ref, o_ref):
    mine = pl.program_id(1) == pos_ref[0]

    @pl.when(mine)
    def _():
        o_ref[0] = mine_ref[0].astype(f32)

    @pl.when(jnp.logical_not(mine))
    def _():
        o_ref[0] = got_ref[0].astype(f32)


def join_halves(core, mine, got):
    _, height, cols = mine.shape
    part = pl.BlockSpec((1, height, cols), lambda m, i, pos: (m, 0, 0))
    return pl.pallas_call(
        join_body,
        grid_spec=pltpu.PrefetchScalarGridSpec(
            num_scalar_prefetch=1,
            grid=(M, 2),
            in_specs=[part, part],
            out_specs=pl.BlockSpec((1, height, cols), lambda m, i, pos: (m, i, 0)),
        ),
        out_shape=jax.ShapeDtypeStruct((M, 2 * height, cols), f32),
        cost_estimate=cost(0, 12 * M * height * cols),
        name="join_halves",
    )(core, mine, got)


def after(value, *others):
    return lax.optimization_barrier((value,) + others)[0]


def swap_core(value):
    count = lax.axis_size("batch")
    return lax.ppermute(value, "batch", [(i, i ^ 1) for i in range(count)])


def y_others(value):
    count = lax.axis_size("batch")
    return [
        lax.ppermute(value, "batch", [(i, (i + shift) % count) for i in range(count)]) for shift in range(2, count, 2)
    ]


def y_sum(value, *before):
    others = [after(other, *before) for other in y_others(value)]
    if len(others) == 1:
        return value.astype(f32) + others[0].astype(f32)
    chips = len(others) + 1
    mine = lax.axis_index("batch") // 2
    buffer = jnp.zeros((chips,) + value.shape, value.dtype)
    for shift, piece in enumerate([value] + others):
        buffer = lax.dynamic_update_index_in_dim(buffer, piece, (mine + chips - shift) % chips, 0)
    return jnp.sum(buffer.astype(f32), axis=0)


def rounded(value):
    return lax.reduce_precision(value, 8, 7)


def batch_total(value, first, second):
    value = value + after(swap_core(value), first)
    return y_sum(value, second)


def batch_total_rounded(value, first, second):
    value = rounded(value)
    value = rounded(value + after(swap_core(value.astype(bf16)), first).astype(f32))
    total = value
    for other in y_others(value.astype(bf16)):
        total = total + after(other, second).astype(f32)
    return total


def to_owners(pieces):
    return lax.all_to_all(pieces, "own", split_axis=0, concat_axis=0, tiled=False)


def to_all(piece):
    return to_owners(jnp.broadcast_to(piece[None], (lax.axis_size("own"),) + piece.shape))


def gather_small(piece, *before):
    count = lax.axis_size("own")
    mine = lax.axis_index("own")
    held = piece[None]
    bit = 1
    while bit < count:
        got = lax.ppermute(held, "own", [(i, i ^ bit) for i in range(count)])
        got = after(got, before[0])
        before = before[1:] or before
        low = (mine & bit) == 0
        held = jnp.concatenate([jnp.where(low, held, got), jnp.where(low, got, held)], axis=0)
        bit *= 2
    return held


def per_device(
    hidden_in, norm_gain, input_proj, conv_weight, conv_bias, state_proj, step_proj, step_bias,
    log_decay, skip_gain, output_proj, modality, grad_out,
):
    own_count = lax.axis_size("own")
    own_index = lax.axis_index("own")
    core = lax.axis_index("batch") % 2
    width = hidden_in.shape[2]
    rows = modality.shape[1]
    span = rows // own_count
    chans = input_proj.shape[3]
    rank = step_proj.shape[1]
    states = log_decay.shape[0]
    psize = state_proj.shape[2]
    chan_at = own_index * chans

    core_at = core.astype(jnp.int32).reshape(1)
    other_at = (1 - core).astype(jnp.int32).reshape(1)

    modc = modality.reshape(rows, 1)
    modl = modality.reshape(1, rows)
    modr = modality.reshape(rows // LANES, 1, LANES)
    w_in = input_proj.reshape(M, width, 2 * chans)
    sp_t = jnp.swapaxes(state_proj, 1, 2)
    step_rows = step_proj.reshape(M * rank, chans)
    part = lambda table: lax.dynamic_slice_in_dim(table, chan_at, chans, table.ndim - 1)
    cw = part(conv_weight)
    cb = part(conv_bias).reshape(1, chans)
    decay = part(log_decay)
    skip = part(skip_gain).reshape(1, chans)

    resid = hidden_in[0].astype(f32)
    inverse = lax.rsqrt(jnp.mean(resid * resid, axis=-1, keepdims=True) + epsilon)
    normed = (resid * inverse * norm_gain).astype(bf16)
    mod_others, normed_others = y_others(modality), y_others(normed)
    x = lax.all_gather(normed, "own", axis=0, tiled=True)
    cot = lax.all_gather(after(grad_out[0], x, w_in, *mod_others, *normed_others), "own", axis=0, tiled=True)

    conv_in, gate, act, proj_part = input_stage(x, w_in, cw, cb, sp_t, modc, modr)
    modcs = [modc] + [other.reshape(rows, 1) for other in mod_others]
    blocks = rows // LANES
    per_owner = blocks // own_count
    pieces = proj_part.reshape(own_count, per_owner * psize, LANES)
    proj = jnp.sum(to_owners(pieces).astype(f32), axis=0).reshape(per_owner, psize, LANES)
    high = proj.astype(bf16)
    low = (proj[:, rank:] - high[:, rank:].astype(f32)).astype(bf16)
    packed = jnp.concatenate([high, low], axis=1)
    pj = to_all(packed).reshape(blocks, psize + 2 * states, LANES)
    xs = [x] + [lax.all_gather(after(other, pj), "own", axis=0, tiled=True) for other in normed_others]
    delta, sig, gated, scanned, prev, final = scan_forward(
        pj, act, gate, step_rows, step_bias, decay, skip, modc, modr
    )
    gg, ggate = gated_grads(cot, output_proj, modc, scanned, gate)
    ggates = [ggate] + y_others(ggate)
    branch_part = select_matmul(gated, output_proj, modc, False, bf16, "output_stage")
    branch = lax.psum_scatter(branch_part, "own", scatter_dimension=0, tiled=True)
    block_out = (resid + branch.astype(f32)).astype(bf16)[None]

    gated_t = jnp.swapaxes(gated, 0, 1)
    groups = ((0,), (1, 2))
    out_got = [
        swap_core(value) for value in rows_wgrad(other_at, gated_t, cot, modl, [], groups, "output_wgrad_send")
    ]
    out_half = rows_wgrad(core_at, gated_t, cot, modl, out_got, groups, "output_wgrad_keep")
    out_total = [y_sum(out_half[0]).astype(bf16)]

    gas, gpt, glogd, gskip, gbias, gstep = scan_backward(
        after(pj, branch_part, *out_half), act, gate, gg, delta, sig, prev, final, step_rows, decay, skip, modc, modr
    )
    gpt = after(gpt, out_total[0])
    gp_own = jnp.sum(to_owners(gpt.reshape(own_count, per_owner * psize, LANES)).astype(f32), axis=0).astype(bf16)
    gp = to_all(gp_own).reshape(blocks, psize, LANES)

    ggates = [ggate] + [after(other, gp_own) for other in ggates[1:]]
    gate_send = half_wgrad(other_at, xs, ggates, modcs, None, "gate_wgrad_send")
    gate_got = swap_core(gate_send)

    gp = after(gp, gate_send)
    gci, gstate, gcw = conv_backward(gp, sp_t, gas, conv_in, act, cw, cb, modc, modr)
    others = y_others(gci)
    gnormed, gain_part = input_dgrad(gci, ggate, w_in, modc, x, norm_gain.reshape(1, width))

    gcis = [gci] + [after(other, gnormed) for other in others]
    gnormed = to_owners(after(gnormed, *others).reshape(own_count, span, width))
    conv_send = half_wgrad(other_at, xs, gcis, modcs, None, "conv_wgrad_send")
    gate_mine = half_wgrad(core_at, xs, ggates, modcs, after(gate_got, conv_send, branch), "gate_wgrad_keep")
    gate_recv = swap_core(gate_mine)
    gain_rows = width // chans
    small = batch_total(
        jnp.concatenate([glogd, gcw[:5], gskip, gain_part.reshape(gain_rows, chans), gbias], axis=0),
        conv_send, gate_mine,
    )
    conv_got = after(swap_core(conv_send), gate_mine, small)
    conv_mine = half_wgrad(core_at, xs, gcis, modcs, conv_got, "conv_wgrad_keep")
    conv_recv = swap_core(conv_mine)
    half_placed = place_input_grad(core_at, conv_mine, gate_mine, None)
    grad_input = place_input_grad(other_at, conv_recv, gate_recv, half_placed)
    gnormed = after(gnormed, half_placed)
    out_total.append(y_sum(after(out_half[1], small), half_placed).astype(bf16))
    out_total = jnp.concatenate(out_total, axis=0)
    grad_output = join_halves(core_at, after(out_total, gnormed), swap_core(out_total))
    gnormed = jnp.sum(gnormed.astype(f32), axis=0)

    weighted = norm_gain * gnormed
    coupled = jnp.mean(resid * weighted, axis=-1, keepdims=True)
    grad_hidden = (
        grad_out[0].astype(f32) + inverse * weighted - resid * (inverse * inverse * inverse) * coupled
    )[None]

    weights = batch_total_rounded(
        jnp.concatenate([gstep, gstate.reshape(M * psize, chans)], axis=0), conv_send, grad_input
    )
    grad_step = weights[: M * rank].reshape(M, rank, chans)
    grad_state = jnp.swapaxes(weights[M * rank :].reshape(M, psize, chans), 1, 2)
    grad_bias = small[states + 6 + gain_rows :]
    wide = gather_small(small[: states + 6 + gain_rows], conv_mine, half_placed, grad_input)
    grad_gain = jnp.sum(wide[:, states + 6 :], axis=0).reshape(width)
    wide = jnp.swapaxes(wide[:, : states + 6], 0, 1).reshape(states + 6, own_count * chans)
    grad_input = input_grad_layout(grad_input, width, chans)
    return (
        block_out,
        grad_hidden,
        grad_gain,
        grad_input,
        wide[states : states + 4],
        wide[states + 4],
        grad_state,
        grad_step,
        grad_bias,
        wide[:states],
        wide[states + 5],
        grad_output,
    )


def solution(mesh):
    placed = (
        P("batch", "own", None),
        P(),
        P(None, None, None, "own"),
        P(),
        P(),
        P(None, "own", None),
        P(None, None, "own"),
        P(None, "own"),
        P(),
        P(),
        P(None, "own", None),
        P("batch", None),
        P("batch", "own", None),
    )
    return jax.shard_map(
        per_device,
        mesh=mesh,
        in_specs=placed,
        out_specs=(
            P("batch", "own", None),
            P("batch", "own", None),
            P(),
            P(None, None, None, "own"),
            P(),
            P(),
            P(None, "own", None),
            P(None, None, "own"),
            P(None, "own"),
            P(),
            P(),
            P(None, "own", None),
        ),
        check_vma=False,
    )
```

```python
import functools

import jax
import jax.numpy as jnp
from jax import lax
from jax.experimental import pallas as pl
from jax.experimental.pallas import tpu as pltpu
from jax.sharding import PartitionSpec as P

M = 3
epsilon = 1e-05
LANES = 128
log2e = 1.4426950408889634
bf16 = jnp.bfloat16
f32 = jnp.float32


def contract(a, b, ca, cb):
    return lax.dot_general(a, b, (((ca,), (cb,)), ((), ())), preferred_element_type=f32)


def pick(mod, parts):
    out = parts[-1]
    for m in reversed(range(len(parts) - 1)):
        out = jnp.where(mod == m, parts[m], out)
    return out


def sigmoid(v):
    return 1.0 / (1.0 + jnp.exp(-v))


def fold_rows(vs):
    sub = lax.broadcasted_iota(jnp.int32, vs[0].shape, 0)
    for shift in (1, 2, 4):
        mask = (sub & shift) == 0
        vs = [
            jnp.where(mask, a, b) + pltpu.roll(jnp.where(mask, b, a), shift, 0)
            for a, b in zip(vs[0::2], vs[1::2])
        ]
    return vs[0]


def fold_lanes(vs, shifts):
    lane = lax.broadcasted_iota(jnp.int32, vs[0].shape, 1)
    for shift in shifts:
        mask = (lane & shift) == 0
        vs = [
            jnp.where(mask, a, b) + pltpu.roll(jnp.where(mask, b, a), shift, 1)
            for a, b in zip(vs[0::2], vs[1::2])
        ]
    return vs[0]


def cost(flops, nbytes):
    return pl.CostEstimate(flops=int(flops), bytes_accessed=int(nbytes), transcendentals=0)


def in_body(x_ref, wc_ref, wg_ref, cw_ref, cb_ref, sp_ref, modc_ref, modr_ref,
            ci_ref, gate_ref, act_ref, proj_ref, pad, sums, *, rows, block):
    tile = pl.program_id(0)
    pad[0:8, :] = jnp.zeros((8, pad.shape[1]), f32)

    def matmul(r, _):
        at = pl.multiple_of(r * block, block)
        x = x_ref[pl.ds(at, block), :]
        mc = modc_ref[pl.ds(at, block), :]
        conv = pick(mc, [contract(x, wc_ref[m], 1, 0) for m in range(M)]).astype(bf16)
        ci_ref[pl.ds(at, block), :] = conv
        pad[pl.ds(at + 8, block), :] = conv.astype(f32)
        gate_ref[pl.ds(at, block), :] = pick(
            mc, [contract(x, wg_ref[m], 1, 0) for m in range(M)]
        ).astype(bf16)
        return 0

    lax.fori_loop(0, rows // block, matmul, 0)
    taps = cw_ref[...]
    base = cb_ref[...]

    def convolve(r, _):
        at = pl.multiple_of(r * LANES, LANES)
        v = pad[pl.ds(at, LANES + 8), :]
        s = base
        for k in range(4):
            s = s + taps[k : k + 1, :] * v[5 + k : 5 + k + LANES, :]
        act = (s * sigmoid(s)).astype(bf16)
        act_ref[pl.ds(at, LANES), :] = act
        part = pick(modr_ref[r], [contract(sp_ref[m], act, 1, 1) for m in range(M)])

        @pl.when(tile == 0)
        def _():
            sums[r] = part

        @pl.when(tile != 0)
        def _():
            sums[r] += part

        proj_ref[r] = sums[r].astype(bf16)
        return 0

    lax.fori_loop(0, rows // LANES, convolve, 0)


def input_stage(x, w, cw, cb, sp, modc, modr):
    rows, width = x.shape
    chans = cw.shape[1]
    psize = sp.shape[1]
    tc = min(256, chans)
    tiles = chans // tc
    full = lambda shape: pl.BlockSpec(shape, lambda j: (0,) * len(shape))
    col = lambda r: pl.BlockSpec((r, tc), lambda j: (0, j))
    return pl.pallas_call(
        functools.partial(in_body, rows=rows, block=min(256, rows)),
        grid=(tiles,),
        in_specs=[
            full((rows, width)),
            pl.BlockSpec((M, width, tc), lambda j: (0, 0, j)),
            pl.BlockSpec((M, width, tc), lambda j: (0, 0, j + tiles)),
            col(4),
            col(1),
            pl.BlockSpec((M, psize, tc), lambda j: (0, 0, j)),
            full((rows, 1)),
            full(modr.shape),
        ],
        out_specs=[col(rows), col(rows), col(rows), full((rows // LANES, psize, LANES))],
        out_shape=[
            jax.ShapeDtypeStruct((rows, chans), bf16),
            jax.ShapeDtypeStruct((rows, chans), bf16),
            jax.ShapeDtypeStruct((rows, chans), bf16),
            jax.ShapeDtypeStruct((rows // LANES, psize, LANES), bf16),
        ],
        scratch_shapes=[pltpu.VMEM((rows + 8, tc), f32), pltpu.VMEM((rows // LANES, psize, LANES), f32)],
        cost_estimate=cost(2 * M * rows * width * 2 * chans, 2 * (rows * width + M * width * 2 * chans)),
        name="input_stage",
    )(x, w, w, cw, cb, sp, modc, modr)


def mm_body(x_ref, w_ref, modc_ref, o_ref, *, rows, block, rhs_dim):
    def step(r, _):
        at = pl.multiple_of(r * block, block)
        x = x_ref[pl.ds(at, block), :]
        mc = modc_ref[pl.ds(at, block), :]
        o_ref[pl.ds(at, block), :] = pick(
            mc, [contract(x, w_ref[m], 1, rhs_dim) for m in range(M)]
        ).astype(o_ref.dtype)
        return 0

    lax.fori_loop(0, rows // block, step, 0)


def select_matmul(x, w, modc, transposed, dtype, name):
    rows, depth = x.shape
    cols = w.shape[1] if transposed else w.shape[2]
    tn = min(256, cols)
    wspec = (
        pl.BlockSpec((M, tn, depth), lambda j: (0, j, 0))
        if transposed
        else pl.BlockSpec((M, depth, tn), lambda j: (0, 0, j))
    )
    return pl.pallas_call(
        functools.partial(mm_body, rows=rows, block=min(512, rows), rhs_dim=1 if transposed else 0),
        grid=(cols // tn,),
        in_specs=[
            pl.BlockSpec((rows, depth), lambda j: (0, 0)),
            wspec,
            pl.BlockSpec((rows, 1), lambda j: (0, 0)),
        ],
        out_specs=pl.BlockSpec((rows, tn), lambda j: (0, j)),
        out_shape=jax.ShapeDtypeStruct((rows, cols), dtype),
        cost_estimate=cost(2 * M * rows * depth * cols, 2 * (rows * depth + M * depth * cols + rows * cols)),
        name=name,
    )(x, w, modc)


def gated_body(x_ref, w_ref, modc_ref, scanned_ref, gate_ref, gg_ref, ggate_ref):
    block = min(512, x_ref.shape[0])

    def step(r, _):
        here = pl.ds(pl.multiple_of(r * block, block), block)
        x = x_ref[here, :]
        gg = pick(modc_ref[here, :], [contract(x, w_ref[m], 1, 1) for m in range(M)]).astype(bf16)
        gg_ref[here, :] = gg
        gate = gate_ref[here, :].astype(f32)
        s = sigmoid(gate)
        ggate_ref[here, :] = (gg.astype(f32) * scanned_ref[here, :] * (s * (1.0 + gate * (1.0 - s)))).astype(bf16)
        return 0

    lax.fori_loop(0, x_ref.shape[0] // block, step, 0)


def gated_grads(cot, w, modc, scanned, gate):
    rows, depth = cot.shape
    cols = w.shape[1]
    tn = min(256, cols)
    col = pl.BlockSpec((rows, tn), lambda j: (0, j))
    return pl.pallas_call(
        gated_body,
        grid=(cols // tn,),
        in_specs=[
            pl.BlockSpec((rows, depth), lambda j: (0, 0)),
            pl.BlockSpec((M, tn, depth), lambda j: (0, j, 0)),
            pl.BlockSpec((rows, 1), lambda j: (0, 0)),
            col,
            col,
        ],
        out_specs=[col, col],
        out_shape=[jax.ShapeDtypeStruct((rows, cols), bf16)] * 2,
        cost_estimate=cost(2 * M * rows * depth * cols, 2 * (rows * depth + M * depth * cols + 5 * rows * cols)),
        name="gated_grads",
    )(cot, w, modc, scanned, gate)


def dgrad_body(gc_ref, gg_ref, w_ref, modc_ref, x_ref, gain_ref, o_ref, part_ref, *, rows, block, chans):
    sums = jnp.zeros((8, part_ref.shape[1]), f32)
    for r in range(rows // block):
        here = slice(r * block, (r + 1) * block)
        gc = gc_ref[here, :]
        gg = gg_ref[here, :]
        out = pick(
            modc_ref[here, :],
            [contract(gc, w_ref[m, :, :chans], 1, 1) + contract(gg, w_ref[m, :, chans:], 1, 1) for m in range(M)],
        )
        o_ref[here, :] = out.astype(bf16)
        terms = out * x_ref[here, :].astype(f32)
        sums = sums + jnp.sum(terms.reshape(block // 8, 8, terms.shape[1]), axis=0)
    part_ref[...] = jnp.sum(sums, axis=0, keepdims=True) / gain_ref[...]


def input_dgrad(gc, gg, w, modc, x, gain):
    rows, chans = gc.shape
    width = w.shape[1]
    tn = 256
    col = pl.BlockSpec((rows, tn), lambda j: (0, j))
    row = pl.BlockSpec((1, tn), lambda j: (0, j))
    return pl.pallas_call(
        functools.partial(dgrad_body, rows=rows, block=min(1024, rows), chans=chans),
        grid=(width // tn,),
        in_specs=[
            pl.BlockSpec((rows, chans), lambda j: (0, 0)),
            pl.BlockSpec((rows, chans), lambda j: (0, 0)),
            pl.BlockSpec((M, tn, 2 * chans), lambda j: (0, j, 0)),
            pl.BlockSpec((rows, 1), lambda j: (0, 0)),
            col,
            row,
        ],
        out_specs=[col, row],
        out_shape=[jax.ShapeDtypeStruct((rows, width), bf16), jax.ShapeDtypeStruct((1, width), f32)],
        cost_estimate=cost(4 * M * rows * chans * width, 2 * (2 * rows * chans + 2 * M * chans * width + 2 * rows * width)),
        name="input_dgrad",
    )(gc, gg, w, modc, x, gain)


def wgrad_body(*refs, sets, add):
    xs, gs, mods = refs[1 : 1 + sets], refs[1 + sets : 1 + 2 * sets], refs[1 + 2 * sets : 1 + 3 * sets]
    o_ref, masked = refs[-2], refs[-1]

    @pl.when(pl.program_id(0) == 0)
    def _():
        for n in range(sets):
            g = gs[n][...]
            for m in range(M):
                masked[n, m] = jnp.where(mods[n][...] == m, g, jnp.zeros_like(g))

    there = refs[0][0] >= 0

    def each(m, _):
        parts = [jnp.where(there, contract(xs[n][...], masked[n, m], 0, 0), 0.0) for n in range(sets)]
        total = functools.reduce(jnp.add, parts)
        if add:
            total = total + refs[1 + 3 * sets][m].astype(f32)
        o_ref[m] = total.astype(bf16)
        return 0

    lax.fori_loop(0, M, each, 0)


def half_wgrad(half, xs, gs, mods, got, name):
    sets = len(xs)
    rows, width = xs[0].shape
    cols = gs[0].shape[1]
    td = min(512, width // 2)
    steps = width // 2 // td
    full = lambda shape: pl.BlockSpec(shape, lambda i, pos: (0, 0))
    out_spec = pl.BlockSpec((M, td, cols), lambda i, pos: (0, i, 0))
    extra = () if got is None else (got,)
    return pl.pallas_call(
        functools.partial(wgrad_body, sets=sets, add=got is not None),
        grid_spec=pltpu.PrefetchScalarGridSpec(
            num_scalar_prefetch=1,
            grid=(steps,),
            in_specs=[pl.BlockSpec((rows, td), lambda i, pos: (0, i + pos[0] * steps))] * sets
            + [full((rows, cols))] * sets
            + [full((rows, 1))] * sets
            + [out_spec] * len(extra),
            out_specs=out_spec,
            scratch_shapes=[pltpu.VMEM((sets, M, rows, cols), bf16)],
        ),
        out_shape=jax.ShapeDtypeStruct((M, width // 2, cols), bf16),
        cost_estimate=cost(sets * M * rows * width * cols, sets * (rows * width + 2 * rows * cols) + 2 * M * width * cols),
        name=name,
    )(half, *xs, *gs, *mods, *extra)


def rows_wgrad_body(pos_ref, xt_ref, g_ref, modl_ref, *rest, groups):
    outs = rest[len(rest) - len(groups) :]
    xt = xt_ref[...]
    for n, group in enumerate(groups):
        for k, m in enumerate(group):
            total = contract(jnp.where(modl_ref[...] == m, xt, jnp.zeros_like(xt)), g_ref[...], 1, 0)
            if len(rest) > len(groups):
                total = total + rest[n][k].astype(f32)
            outs[n][k] = total.astype(bf16)


def rows_wgrad(half, xt, g, modl, got, groups, name):
    width, rows = xt.shape
    cols = g.shape[1]
    tn = 512
    out_specs = [pl.BlockSpec((len(group), width // 2, tn), lambda i, pos: (0, 0, i)) for group in groups]
    return pl.pallas_call(
        functools.partial(rows_wgrad_body, groups=groups),
        grid_spec=pltpu.PrefetchScalarGridSpec(
            num_scalar_prefetch=1,
            grid=(cols // tn,),
            in_specs=[
                pl.BlockSpec((width // 2, rows), lambda i, pos: (pos[0], 0)),
                pl.BlockSpec((rows, tn), lambda i, pos: (0, i)),
                pl.BlockSpec((1, rows), lambda i, pos: (0, 0)),
            ]
            + (out_specs if got else []),
            out_specs=out_specs,
        ),
        out_shape=[jax.ShapeDtypeStruct((len(group), width // 2, cols), bf16) for group in groups],
        cost_estimate=cost(M * rows * width * cols, rows * width + 2 * rows * cols + 2 * M * width * cols),
        name=name,
    )(half, xt, g, modl, *got)


UNROLL = 4


def spread(value, ref):
    for t in range(LANES):
        ref[t] = jnp.broadcast_to(value[:, t : t + 1], (16, LANES))


def fold_columns(ref):
    halves = []
    for h in range(2):
        groups = [
            fold_lanes([ref[8 * i + j, 8 * h : 8 * h + 8, :] for j in range(8)], (1, 2, 4)) for i in range(16)
        ]
        halves.append(fold_lanes(groups, (8, 16, 32, 64)))
    return jnp.concatenate(halves, axis=0)


def row_of(ref, t):
    wide = jnp.broadcast_to(ref[pl.ds(t, 1), :], (8, ref.shape[1]))
    return [wide[:, k * LANES : (k + 1) * LANES] for k in range(ref.shape[1] // LANES)]


def add_all(parts):
    while len(parts) > 1:
        parts = [functools.reduce(jnp.add, parts[k : k + 2]) for k in range(0, len(parts), 2)]
    return parts[0]


def state_vectors(pj_ref, rank):
    b = pj_ref[0, rank : rank + 16, :].astype(f32) + pj_ref[0, rank + 32 : rank + 48, :].astype(f32)
    c = pj_ref[0, rank + 16 : rank + 32, :].astype(f32) + pj_ref[0, rank + 48 : rank + 64, :].astype(f32)
    return b, c


def by_modality(mod, rows):
    return jnp.concatenate([jnp.where(mod == m, rows, jnp.zeros_like(rows)) for m in range(M)], axis=0)


def fold_all(ref):
    groups = [fold_rows([ref[8 * i + j] for j in range(8)]) for i in range(LANES // 8)]
    return jnp.concatenate(groups, axis=0)


def scan_fwd_body(pj_ref, act_ref, gate_ref, sp_ref, sb_ref, ld_ref, skip_ref, modc_ref, modr_ref,
                  delta_ref, sig_ref, gated_ref, scanned_ref, prev_ref, final_ref, b_s, c_s,
                  state, pre_s, d_s, u_s, r_s, yp_s):
    span, chans = act_ref.shape
    rank = pj_ref.shape[1] - 64
    tiles = chans // LANES

    @pl.when(pl.program_id(0) == 0)
    def _():
        state[...] = jnp.zeros_like(state)

    pre_s[...] = contract(by_modality(modr_ref[0], pj_ref[0, :rank, :]), sp_ref[...], 0, 0)
    r_s[...] = -jnp.exp(ld_ref[...]) * log2e
    b, c = state_vectors(pj_ref, rank)
    spread(b, b_s)
    spread(c, c_s)
    bias = [sb_ref[m : m + 1, :] for m in range(M)]

    pre = pre_s[...] + pick(modc_ref[...], bias)
    z = jnp.exp(-jnp.abs(pre))
    delta = (jnp.maximum(pre, 0.0) + jnp.log1p(z)).astype(bf16)
    delta_ref[...] = delta
    inv = 1.0 / (1.0 + z)
    sig_ref[...] = jnp.where(pre >= 0, inv, z * inv)
    act = act_ref[...].astype(f32)
    d = delta.astype(f32)
    d_s[...] = d
    u_s[...] = d * act

    def positions(i, carry):
        st = list(carry)
        for j in range(UNROLL):
            t = i * UNROLL + j
            at = pl.multiple_of(t * 16, 16)
            d_row, u_row = row_of(d_s, t), row_of(u_s, t)
            for k in range(tiles):
                cols = slice(k * LANES, (k + 1) * LANES)
                out = []
                for h in range(2):
                    n = 2 * k + h
                    rows = slice(8 * h, 8 * h + 8)
                    prev_ref[pl.ds(at + 8 * h, 8), cols] = st[n]
                    st[n] = jnp.exp2(d_row[k] * r_s[rows, cols]) * st[n] + u_row[k] * b_s[t, rows, :]
                    out.append(st[n] * c_s[t, rows, :])
                yp_s[t, :, cols] = out[0] + out[1]
        return tuple(st)

    first = tuple(
        state[8 * h : 8 * h + 8, k * LANES : (k + 1) * LANES] for k in range(tiles) for h in range(2)
    )
    st = lax.fori_loop(0, span // UNROLL, positions, first)
    for k in range(tiles):
        for h in range(2):
            state[8 * h : 8 * h + 8, k * LANES : (k + 1) * LANES] = st[2 * k + h]
    final_ref[...] = state[...]
    scanned = fold_all(yp_s) + skip_ref[...] * act
    scanned_ref[...] = scanned
    gate = gate_ref[...].astype(f32)
    gated_ref[...] = (scanned * (gate * sigmoid(gate))).astype(bf16)


def scan_forward(pj, act, gate, step_proj, step_bias, log_decay, skip, modc, modr):
    rows, chans = act.shape
    blocks = rows // LANES
    row = pl.BlockSpec((LANES, chans), lambda i: (i, 0))
    full = lambda shape: pl.BlockSpec(shape, lambda i: (0,) * len(shape))
    wide = pl.BlockSpec((LANES, 16, LANES), lambda i: (i, 0, 0))
    return pl.pallas_call(
        scan_fwd_body,
        grid=(blocks,),
        in_specs=[
            pl.BlockSpec((1,) + pj.shape[1:], lambda i: (i, 0, 0)),
            row, row,
            full(step_proj.shape),
            full((M, chans)),
            full((16, chans)),
            full((1, chans)),
            pl.BlockSpec((LANES, 1), lambda i: (i, 0)),
            pl.BlockSpec((1, 1, LANES), lambda i: (i, 0, 0)),
        ],
        out_specs=[
            row, row, row, row,
            pl.BlockSpec((LANES * 16, chans), lambda i: (i, 0)),
            full((16, chans)),
            wide,
            wide,
        ],
        out_shape=[
            jax.ShapeDtypeStruct((rows, chans), bf16),
            jax.ShapeDtypeStruct((rows, chans), f32),
            jax.ShapeDtypeStruct((rows, chans), bf16),
            jax.ShapeDtypeStruct((rows, chans), f32),
            jax.ShapeDtypeStruct((rows * 16, chans), f32),
            jax.ShapeDtypeStruct((16, chans), f32),
            jax.ShapeDtypeStruct((rows, 16, LANES), f32),
            jax.ShapeDtypeStruct((rows, 16, LANES), f32),
        ],
        scratch_shapes=[pltpu.VMEM((16, chans), f32)] + [pltpu.VMEM((LANES, chans), f32)] * 3
        + [pltpu.VMEM((16, chans), f32)]
        + [pltpu.VMEM((LANES, 8, chans), f32)],
        cost_estimate=cost(40e9, 64 * rows * chans + 20 * rows * chans),
        name="scan_forward",
    )(pj, act, gate, step_proj, step_bias, log_decay, skip, modc, modr)


def scan_bwd_body(pj_ref, act_ref, gate_ref, gg_ref, delta_ref, sig_ref, prev_ref, final_ref, b_s, c_s,
                  sp_ref, ld_ref, skip_ref, modc_ref, modr_ref,
                  gas_ref, gpt_ref, glogd_ref, gskip_ref, gbias_ref, gstep_ref,
                  carry_w, acc, later, d_s, u_s, gs_s, r_s, gp_s, hp_s, p_s, q_s):
    span, chans = act_ref.shape
    rank = pj_ref.shape[1] - 64
    tiles = chans // LANES

    @pl.when(pl.program_id(0) == 0)
    def _():
        carry_w[...] = jnp.zeros_like(carry_w)
        acc[...] = jnp.zeros_like(acc)
        later[...] = final_ref[...]
        gskip_ref[...] = jnp.zeros_like(gskip_ref)
        gbias_ref[...] = jnp.zeros_like(gbias_ref)
        gstep_ref[...] = jnp.zeros_like(gstep_ref)

    rates = -jnp.exp(ld_ref[...])
    r_s[...] = rates * log2e

    act = act_ref[...].astype(f32)
    d = delta_ref[...].astype(f32)
    gate = gate_ref[...].astype(f32)
    gs = gg_ref[...].astype(f32) * (gate * sigmoid(gate))
    d_s[...] = d
    u_s[...] = d * act
    gs_s[...] = gs

    def positions(i, carry):
        w, total = list(carry[0]), list(carry[1])
        for j in range(UNROLL):
            t = span - 1 - (i * UNROLL + j)
            at = pl.multiple_of(t * 16, 16)
            grad = []
            d_row, u_row, gs_row = row_of(d_s, t), row_of(u_s, t), row_of(gs_s, t)
            for k in range(tiles):
                cols = slice(k * LANES, (k + 1) * LANES)
                gl, hl = [], []
                for h in range(2):
                    n = 2 * k + h
                    rows = slice(8 * h, 8 * h + 8)
                    rate = r_s[rows, cols]
                    adj = gs_row[k] * c_s[t, rows, :] + w[n]
                    gl.append(adj * b_s[t, rows, :])
                    w[n] = jnp.exp2(d_row[k] * rate) * adj
                    q = w[n] * prev_ref[pl.ds(at + 8 * h, 8), cols]
                    hl.append(q * rate)
                    total[n] = total[n] + q * d_row[k]
                    grad.append(adj * u_row[k])
                gp_s[t, :, cols] = gl[0] + gl[1]
                hp_s[t, :, cols] = hl[0] + hl[1]
            p_s[t, 0:8, :] = add_all(grad[0::2])
            p_s[t, 8:16, :] = add_all(grad[1::2])
        return tuple(w), tuple(total)

    places = [(slice(8 * h, 8 * h + 8), slice(k * LANES, (k + 1) * LANES)) for k in range(tiles) for h in range(2)]
    def read_grad(t, state):
        gs_row = row_of(gs_s, t)
        for h in range(2):
            rows = slice(8 * h, 8 * h + 8)
            q_s[t, rows, :] = add_all(
                [state(h)[:, k * LANES : (k + 1) * LANES] * gs_row[k] for k in range(tiles)]
            )

    def reads(i, _):
        for j in range(UNROLL):
            t = i * UNROLL + j
            at = pl.multiple_of(jnp.minimum(t + 1, span - 1) * 16, 16)
            read_grad(t, lambda h: prev_ref[pl.ds(at + 8 * h, 8), :])
        return 0

    lax.fori_loop(0, span // UNROLL, reads, 0)
    read_grad(span - 1, lambda h: later[8 * h : 8 * h + 8, :])
    later[...] = prev_ref[0:16, :]

    @pl.when(pl.program_id(0) >= 0)
    def _():
        gpt_ref[0, rank + 16 : rank + 32, :] = fold_columns(q_s).astype(bf16)

    held = (carry_w, acc)
    results = lax.fori_loop(
        0, span // UNROLL, positions, tuple(tuple(ref[at] for at in places) for ref in held)
    )
    for ref, values in zip(held, results):
        for n, at in enumerate(places):
            ref[at] = values[n]
    gb = fold_columns(p_s)
    g = fold_all(gp_s)
    gas_ref[...] = (g * d + skip_ref[...] * gs).astype(bf16)
    gpre = (act * g + fold_all(hp_s) * (1.0 / log2e)).astype(bf16).astype(f32) * sig_ref[...]
    glin = gpre.astype(bf16)
    mc = modc_ref[...]
    gbias_ref[...] += jnp.concatenate(
        [jnp.sum(jnp.where(mc == m, gpre, 0.0), axis=0, keepdims=True) for m in range(M)], axis=0
    )
    gskip_ref[...] += jnp.sum(gs * act, axis=0, keepdims=True)
    mr = modr_ref[0]
    gstep_ref[...] += contract(by_modality(mr, pj_ref[0, :rank, :]), glin, 1, 0)
    lin = contract(sp_ref[...], glin, 1, 1)
    gpt_ref[0, :rank, :] = pick(mr, [lin[m * rank : (m + 1) * rank] for m in range(M)]).astype(bf16)
    gpt_ref[0, rank : rank + 16, :] = gb.astype(bf16)
    glogd_ref[...] = acc[...] * rates


def scan_backward(pj, act, gate, gg, delta, sig, prev, final, b, c, step_proj, log_decay, skip, modc, modr):
    rows, chans = act.shape
    blocks = rows // LANES
    rank = step_proj.shape[0] // M
    last = blocks - 1
    row = pl.BlockSpec((LANES, chans), lambda i: (last - i, 0))
    full = lambda shape: pl.BlockSpec(shape, lambda i: (0,) * len(shape))
    slab = lambda shape: pl.BlockSpec((1,) + shape, lambda i: (last - i, 0, 0))
    wide = pl.BlockSpec((LANES, 16, LANES), lambda i: (last - i, 0, 0))
    return pl.pallas_call(
        scan_bwd_body,
        grid=(blocks,),
        in_specs=[
            slab(pj.shape[1:]),
            row, row, row, row, row,
            pl.BlockSpec((LANES * 16, chans), lambda i: (last - i, 0)),
            full((16, chans)),
            wide,
            wide,
            full(step_proj.shape),
            full((16, chans)),
            full((1, chans)),
            pl.BlockSpec((LANES, 1), lambda i: (last - i, 0)),
            slab((1, LANES)),
        ],
        out_specs=[
            row,
            slab((rank + 32, LANES)),
            full((16, chans)),
            full((1, chans)),
            full((M, chans)),
            full(step_proj.shape),
        ],
        out_shape=[
            jax.ShapeDtypeStruct((rows, chans), bf16),
            jax.ShapeDtypeStruct((blocks, rank + 32, LANES), bf16),
            jax.ShapeDtypeStruct((16, chans), f32),
            jax.ShapeDtypeStruct((1, chans), f32),
            jax.ShapeDtypeStruct((M, chans), f32),
            jax.ShapeDtypeStruct(step_proj.shape, f32),
        ],
        scratch_shapes=[pltpu.VMEM((16, chans), f32)] * 3
        + [pltpu.VMEM((LANES, chans), f32)] * 3
        + [pltpu.VMEM((16, chans), f32)]
        + [pltpu.VMEM((LANES, 8, chans), f32)] * 2
        + [pltpu.VMEM((LANES, 16, LANES), f32)] * 2,
        cost_estimate=cost(60e9, 64 * rows * chans + 20 * rows * chans),
        name="scan_backward",
    )(pj, act, gate, gg, delta, sig, prev, final, b, c, step_proj, log_decay, skip, modc, modr)


def conv_bwd_body(gp_ref, sp_ref, gas_ref, ci_ref, act_ref, cw_ref, cb_ref, modc_ref, modr_ref,
                  gci_ref, gstate_ref, gcw_ref, pad, tail, *, rows):
    cols = pad.shape[1]
    pad[0:8, :] = jnp.zeros((8, cols), f32)
    tail[rows : rows + 8, :] = jnp.zeros((8, cols), f32)
    gstate_ref[...] = jnp.zeros_like(gstate_ref)
    taps = cw_ref[...]
    base = cb_ref[...]

    def first(r, sums):
        at = pl.multiple_of(r * LANES, LANES)
        here = pl.ds(at, LANES)
        pad[pl.ds(at + 8, LANES), :] = ci_ref[here, :].astype(f32)
        v = pad[pl.ds(at, LANES + 8), :]
        shifted = [v[5 + k : 5 + k + LANES, :] for k in range(4)]
        s = base
        for k in range(4):
            s = s + taps[k : k + 1, :] * shifted[k]
        sg = sigmoid(s)
        gp = gp_ref[r]
        ga = pick(modc_ref[here, :], [contract(gp, sp_ref[m], 0, 0) for m in range(M)])
        gcp = (ga + gas_ref[here, :].astype(f32)) * (sg * (1.0 + s * (1.0 - sg)))
        tail[here, :] = gcp
        act = act_ref[here, :]
        mr = modr_ref[r]
        for m in range(M):
            gstate_ref[m] += contract(jnp.where(mr == m, gp, jnp.zeros_like(gp)), act, 1, 0)
        terms = [gcp * part for part in shifted] + [gcp]
        return tuple(
            total + jnp.sum(term.reshape(LANES // 8, 8, cols), axis=0) for total, term in zip(sums, terms)
        )

    sums = lax.fori_loop(0, rows // LANES, first, (jnp.zeros((8, cols), f32),) * 5)
    gcw_ref[...] = jnp.concatenate(
        [jnp.sum(total, axis=0, keepdims=True) for total in sums] + [jnp.zeros((3, cols), f32)], axis=0
    )

    def second(r, _):
        at = pl.multiple_of(r * LANES, LANES)
        v = tail[pl.ds(at, LANES + 8), :]
        s = taps[0:1, :] * v[3 : 3 + LANES, :]
        for k in range(1, 4):
            s = s + taps[k : k + 1, :] * v[3 - k : 3 - k + LANES, :]
        gci_ref[pl.ds(at, LANES), :] = s.astype(bf16)
        return 0

    lax.fori_loop(0, rows // LANES, second, 0)


def conv_backward(gp, sp, gas, ci, act, cw, cb, modc, modr):
    rows, chans = ci.shape
    psize = sp.shape[1]
    tc = min(256, chans)
    col = lambda r: pl.BlockSpec((r, tc), lambda j: (0, j))
    full = lambda shape: pl.BlockSpec(shape, lambda j: (0,) * len(shape))
    wide = pl.BlockSpec((M, psize, tc), lambda j: (0, 0, j))
    return pl.pallas_call(
        functools.partial(conv_bwd_body, rows=rows),
        grid=(chans // tc,),
        in_specs=[full(gp.shape), wide, col(rows), col(rows), col(rows), col(4), col(1), full((rows, 1)), full(modr.shape)],
        out_specs=[col(rows), wide, col(8)],
        out_shape=[
            jax.ShapeDtypeStruct((rows, chans), bf16),
            jax.ShapeDtypeStruct((M, psize, chans), f32),
            jax.ShapeDtypeStruct((8, chans), f32),
        ],
        scratch_shapes=[pltpu.VMEM((rows + 8, tc), f32), pltpu.VMEM((rows + 8, tc), f32)],
        cost_estimate=cost(8 * M * rows * psize * chans, 10 * rows * chans),
        name="conv_backward",
    )(gp, sp, gas, ci, act, cw, cb, modc, modr)


def interleave_body(pos_ref, conv_ref, gate_ref, *rest, group):
    o_ref = rest[-1]
    sub = lax.broadcasted_iota(jnp.int32, (8, LANES), 0)

    def step(r, _):
        at = pl.multiple_of(r * group, group)
        sources = [ref[0, pl.ds(at, group), :].astype(f32) for ref in (conv_ref, gate_ref)]
        for h in range(group // 8):
            vs = [
                source[8 * h : 8 * h + 8, k * LANES : (k + 1) * LANES] for k in range(4) for source in sources
            ]
            for shift in (1, 2, 4):
                mask = (sub & shift) == 0
                swapped = list(vs)
                for j in range(8):
                    if j & shift == 0:
                        a, b = vs[j], vs[j | shift]
                        swapped[j] = jnp.where(mask, a, pltpu.roll(b, shift, 0))
                        swapped[j | shift] = jnp.where(mask, pltpu.roll(a, 8 - shift, 0), b)
                vs = swapped
            for d in range(8):
                o_ref[0, pl.ds((at + 8 * h + d) * 8, 8), :] = vs[d]
        return 0

    lax.fori_loop(0, conv_ref.shape[1] // group, step, 0)


def split_body(pos_ref, conv_ref, gate_ref, *rest):
    o_ref = rest[-1]
    o_ref[0, :, 0, :] = conv_ref[0].astype(f32)
    o_ref[0, :, 1, :] = gate_ref[0].astype(f32)


def place_input_grad(half, conv, gate, target):
    _, height, chans = conv.shape
    td = min(512, height)
    steps = height // td
    packed = chans == 4 * LANES
    if packed:
        shape, block = (M, 2 * height * 8, LANES), (1, td * 8, LANES)
        where = lambda m, i, pos: (m, i + pos[0] * steps, 0)
        body = functools.partial(interleave_body, group=64)
    else:
        shape, block = (M, 2 * height, 2, chans), (1, td, 2, chans)
        where = lambda m, i, pos: (m, i + pos[0] * steps, 0, 0)
        body = split_body
    source = pl.BlockSpec((1, td, chans), lambda m, i, pos: (m, i, 0))
    extra = () if target is None else (target,)
    return pl.pallas_call(
        body,
        grid_spec=pltpu.PrefetchScalarGridSpec(
            num_scalar_prefetch=1,
            grid=(M, steps),
            in_specs=[source, source] + [pl.BlockSpec(memory_space=pl.ANY)] * len(extra),
            out_specs=pl.BlockSpec(block, where),
        ),
        out_shape=jax.ShapeDtypeStruct(shape, f32),
        input_output_aliases={} if target is None else {3: 0},
        cost_estimate=cost(0, 12 * M * height * chans),
        name="place_input_grad",
    )(half, conv, gate, *extra)


def input_grad_layout(value, width, chans):
    if value.ndim == 4:
        return value
    return value.reshape(M, width, chans // LANES, 2, LANES).transpose(0, 1, 3, 2, 4).reshape(M, width, 2, chans)


def join_body(pos_ref, mine_ref, got_ref, o_ref):
    mine = pl.program_id(1) == pos_ref[0]

    @pl.when(mine)
    def _():
        o_ref[0] = mine_ref[0].astype(f32)

    @pl.when(jnp.logical_not(mine))
    def _():
        o_ref[0] = got_ref[0].astype(f32)


def join_halves(core, mine, got):
    _, height, cols = mine.shape
    part = pl.BlockSpec((1, height, cols), lambda m, i, pos: (m, 0, 0))
    return pl.pallas_call(
        join_body,
        grid_spec=pltpu.PrefetchScalarGridSpec(
            num_scalar_prefetch=1,
            grid=(M, 2),
            in_specs=[part, part],
            out_specs=pl.BlockSpec((1, height, cols), lambda m, i, pos: (m, i, 0)),
        ),
        out_shape=jax.ShapeDtypeStruct((M, 2 * height, cols), f32),
        cost_estimate=cost(0, 12 * M * height * cols),
        name="join_halves",
    )(core, mine, got)


def after(value, *others):
    return lax.optimization_barrier((value,) + others)[0]


def swap_core(value):
    count = lax.axis_size("batch")
    return lax.ppermute(value, "batch", [(i, i ^ 1) for i in range(count)])


def y_others(value):
    count = lax.axis_size("batch")
    return [
        lax.ppermute(value, "batch", [(i, (i + shift) % count) for i in range(count)]) for shift in range(2, count, 2)
    ]


def y_sum(value, *before):
    others = [after(other, *before) for other in y_others(value)]
    if len(others) == 1:
        return value.astype(f32) + others[0].astype(f32)
    chips = len(others) + 1
    mine = lax.axis_index("batch") // 2
    buffer = jnp.zeros((chips,) + value.shape, value.dtype)
    for shift, piece in enumerate([value] + others):
        buffer = lax.dynamic_update_index_in_dim(buffer, piece, (mine + chips - shift) % chips, 0)
    return jnp.sum(buffer.astype(f32), axis=0)


def rounded(value):
    return lax.reduce_precision(value, 8, 7)


def split(value):
    high = rounded(value)
    return jnp.concatenate([high, rounded(value - high)], axis=0).astype(bf16)


def joined(value):
    count = value.shape[0] // 2
    return value[:count].astype(f32) + value[count:].astype(f32)


def small_totals(coarse, fine, first, second):
    rows = coarse.shape[0]
    for step, before in ((lambda value: [swap_core(value)], first), (y_others, second)):
        message = lax.optimization_barrier(jnp.concatenate([rounded(coarse).astype(bf16), split(fine)], axis=0))
        coarse, fine = message[:rows].astype(f32), joined(message[rows:])
        for other in step(message):
            other = after(other, *before)
            coarse, fine = coarse + other[:rows].astype(f32), fine + joined(other[rows:])
    return coarse, fine


def to_owners(pieces):
    return lax.all_to_all(pieces, "own", split_axis=0, concat_axis=0, tiled=False)


def to_all(piece):
    return to_owners(jnp.broadcast_to(piece[None], (lax.axis_size("own"),) + piece.shape))


def gather_small(piece, *before):
    count = lax.axis_size("own")
    mine = lax.axis_index("own")
    held = piece[None]
    bit = 1
    while bit < count:
        got = lax.ppermute(held, "own", [(i, i ^ bit) for i in range(count)])
        got = after(got, before[0])
        before = before[1:] or before
        low = (mine & bit) == 0
        held = jnp.concatenate([jnp.where(low, held, got), jnp.where(low, got, held)], axis=0)
        bit *= 2
    return held


def per_device(
    hidden_in, norm_gain, input_proj, conv_weight, conv_bias, state_proj, step_proj, step_bias,
    log_decay, skip_gain, output_proj, modality, grad_out,
):
    own_count = lax.axis_size("own")
    own_index = lax.axis_index("own")
    core = lax.axis_index("batch") % 2
    width = hidden_in.shape[2]
    rows = modality.shape[1]
    span = rows // own_count
    chans = input_proj.shape[3]
    rank = step_proj.shape[1]
    states = log_decay.shape[0]
    psize = state_proj.shape[2]
    chan_at = own_index * chans

    core_at = core.astype(jnp.int32).reshape(1)
    other_at = (1 - core).astype(jnp.int32).reshape(1)

    modc = modality.reshape(rows, 1)
    modl = modality.reshape(1, rows)
    modr = modality.reshape(rows // LANES, 1, LANES)
    w_in = input_proj.reshape(M, width, 2 * chans)
    sp_t = jnp.swapaxes(state_proj, 1, 2)
    step_rows = step_proj.reshape(M * rank, chans)
    part = lambda table: lax.dynamic_slice_in_dim(table, chan_at, chans, table.ndim - 1)
    cw = part(conv_weight)
    cb = part(conv_bias).reshape(1, chans)
    decay = part(log_decay)
    skip = part(skip_gain).reshape(1, chans)

    resid = hidden_in[0].astype(f32)
    inverse = lax.rsqrt(jnp.mean(resid * resid, axis=-1, keepdims=True) + epsilon)
    normed = (resid * inverse * norm_gain).astype(bf16)
    mod_others, normed_others = y_others(modality), y_others(normed)
    x = lax.all_gather(normed, "own", axis=0, tiled=True)
    cot = lax.all_gather(after(grad_out[0], x, w_in, *mod_others, *normed_others), "own", axis=0, tiled=True)

    conv_in, gate, act, proj_part = input_stage(x, w_in, cw, cb, sp_t, modc, modr)
    modcs = [modc] + [other.reshape(rows, 1) for other in mod_others]
    blocks = rows // LANES
    per_owner = blocks // own_count
    pieces = proj_part.reshape(own_count, per_owner * psize, LANES)
    proj = jnp.sum(to_owners(pieces).astype(f32), axis=0).reshape(per_owner, psize, LANES)
    high = proj.astype(bf16)
    low = (proj[:, rank:] - high[:, rank:].astype(f32)).astype(bf16)
    packed = jnp.concatenate([high, low], axis=1)
    pj = to_all(packed).reshape(blocks, psize + 2 * states, LANES)
    xs = [x] + [lax.all_gather(after(other, pj), "own", axis=0, tiled=True) for other in normed_others]
    delta, sig, gated, scanned, prev, final, b_wide, c_wide = scan_forward(
        pj, act, gate, step_rows, step_bias, decay, skip, modc, modr
    )
    branch_part = select_matmul(gated, output_proj, modc, False, bf16, "output_stage")
    branch = lax.psum_scatter(branch_part, "own", scatter_dimension=0, tiled=True)
    block_out = (resid + branch.astype(f32)).astype(bf16)[None]

    gated_t = jnp.swapaxes(gated, 0, 1)
    groups = ((0, 1, 2),)
    out_got = [
        swap_core(value) for value in rows_wgrad(other_at, gated_t, cot, modl, [], groups, "output_wgrad_send")
    ]
    out_half = rows_wgrad(core_at, gated_t, cot, modl, [after(value, branch_part) for value in out_got], groups, "output_wgrad_keep")
    out_total = y_sum(out_half[0]).astype(bf16)

    gg, ggate = gated_grads(after(cot, *out_half), output_proj, modc, scanned, gate)
    ggates = [ggate] + y_others(ggate)
    gas, gpt, glogd, gskip, gbias, gstep = scan_backward(
        after(pj, branch_part, *out_half), act, gate, gg, delta, sig, prev, final, b_wide, c_wide, step_rows, decay, skip, modc, modr
    )
    gp_own = jnp.sum(to_owners(gpt.reshape(own_count, per_owner * psize, LANES)).astype(f32), axis=0).astype(bf16)
    gp_own = after(gp_own, out_total)
    gp = to_all(gp_own).reshape(blocks, psize, LANES)

    ggates = [ggate] + [after(other, gp_own) for other in ggates[1:]]
    gate_send = half_wgrad(other_at, xs, ggates, modcs, None, "gate_wgrad_send")
    gate_got = swap_core(gate_send)

    gp = after(gp, gate_send)
    gci, gstate, gcw = conv_backward(gp, sp_t, gas, conv_in, act, cw, cb, modc, modr)
    others = y_others(gci)
    gnormed, gain_part = input_dgrad(gci, ggate, w_in, modc, x, norm_gain.reshape(1, width))

    gcis = [gci] + [after(other, gnormed) for other in others]
    gnormed = lax.psum_scatter(gnormed, "own", scatter_dimension=0, tiled=True)
    conv_send = half_wgrad(other_at, xs, gcis, modcs, None, "conv_wgrad_send")
    gate_mine = half_wgrad(core_at, xs, ggates, modcs, after(gate_got, conv_send, branch), "gate_wgrad_keep")
    gate_recv = swap_core(gate_mine)
    conv_got = after(swap_core(conv_send), gate_mine)
    conv_mine = half_wgrad(core_at, xs, gcis, modcs, conv_got, "conv_wgrad_keep")
    conv_recv = swap_core(conv_mine)
    grad_output = join_halves(core_at, out_total, swap_core(out_total))
    half_placed = place_input_grad(core_at, after(conv_mine, grad_output), gate_mine, None)
    grad_input = place_input_grad(other_at, after(conv_recv, gnormed), gate_recv, half_placed)
    gnormed = gnormed.astype(f32)

    weighted = norm_gain * gnormed
    coupled = jnp.mean(resid * weighted, axis=-1, keepdims=True)
    grad_hidden = (
        grad_out[0].astype(f32) + inverse * weighted - resid * (inverse * inverse * inverse) * coupled
    )[None]

    gain_rows = width // chans
    weights, small = small_totals(
        jnp.concatenate([gstep, gstate.reshape(M * psize, chans)], axis=0),
        jnp.concatenate([glogd, gcw[:5], gskip, gain_part.reshape(gain_rows, chans), gbias], axis=0),
        (conv_send,), (half_placed,),
    )
    grad_step = weights[: M * rank].reshape(M, rank, chans)
    grad_state = jnp.swapaxes(weights[M * rank :].reshape(M, psize, chans), 1, 2)
    grad_bias = small[states + 6 + gain_rows :]
    wide = gather_small(small[: states + 6 + gain_rows], half_placed, half_placed, grad_input)
    grad_gain = jnp.sum(wide[:, states + 6 :], axis=0).reshape(width)
    wide = jnp.swapaxes(wide[:, : states + 6], 0, 1).reshape(states + 6, own_count * chans)
    grad_input = input_grad_layout(grad_input, width, chans)
    return (
        block_out,
        grad_hidden,
        grad_gain,
        grad_input,
        wide[states : states + 4],
        wide[states + 4],
        grad_state,
        grad_step,
        grad_bias,
        wide[:states],
        wide[states + 5],
        grad_output,
    )


def solution(mesh):
    placed = (
        P("batch", "own", None),
        P(),
        P(None, None, None, "own"),
        P(),
        P(),
        P(None, "own", None),
        P(None, None, "own"),
        P(None, "own"),
        P(),
        P(),
        P(None, "own", None),
        P("batch", None),
        P("batch", "own", None),
    )
    return jax.shard_map(
        per_device,
        mesh=mesh,
        in_specs=placed,
        out_specs=(
            P("batch", "own", None),
            P("batch", "own", None),
            P(),
            P(None, None, None, "own"),
            P(),
            P(),
            P(None, "own", None),
            P(None, None, "own"),
            P(None, "own"),
            P(),
            P(),
            P(None, "own", None),
        ),
        check_vma=False,
    )
```

```python
import functools

import jax
import jax.numpy as jnp
from jax import lax
from jax.experimental import pallas as pl
from jax.experimental.pallas import tpu as pltpu
from jax.sharding import PartitionSpec as P

M = 3
epsilon = 1e-05
LANES = 128
log2e = 1.4426950408889634
bf16 = jnp.bfloat16
f32 = jnp.float32


def contract(a, b, ca, cb):
    return lax.dot_general(a, b, (((ca,), (cb,)), ((), ())), preferred_element_type=f32)


def pick(mod, parts):
    out = parts[-1]
    for m in reversed(range(len(parts) - 1)):
        out = jnp.where(mod == m, parts[m], out)
    return out


def sigmoid(v):
    return 1.0 / (1.0 + jnp.exp(-v))


def fold_rows(vs):
    sub = lax.broadcasted_iota(jnp.int32, vs[0].shape, 0)
    for shift in (1, 2, 4):
        mask = (sub & shift) == 0
        vs = [
            jnp.where(mask, a, b) + pltpu.roll(jnp.where(mask, b, a), shift, 0)
            for a, b in zip(vs[0::2], vs[1::2])
        ]
    return vs[0]


def fold_lanes(vs, shifts):
    lane = lax.broadcasted_iota(jnp.int32, vs[0].shape, 1)
    for shift in shifts:
        mask = (lane & shift) == 0
        vs = [
            jnp.where(mask, a, b) + pltpu.roll(jnp.where(mask, b, a), shift, 1)
            for a, b in zip(vs[0::2], vs[1::2])
        ]
    return vs[0]


def cost(flops, nbytes):
    return pl.CostEstimate(flops=int(flops), bytes_accessed=int(nbytes), transcendentals=0)


def in_body(x_ref, wc_ref, wg_ref, cw_ref, cb_ref, sp_ref, modc_ref, modr_ref,
            ci_ref, gate_ref, act_ref, proj_ref, pad, sums, *, rows, block):
    tile = pl.program_id(0)
    pad[0:8, :] = jnp.zeros((8, pad.shape[1]), f32)

    def matmul(r, _):
        at = pl.multiple_of(r * block, block)
        x = x_ref[pl.ds(at, block), :]
        mc = modc_ref[pl.ds(at, block), :]
        conv = pick(mc, [contract(x, wc_ref[m], 1, 0) for m in range(M)]).astype(bf16)
        ci_ref[pl.ds(at, block), :] = conv
        pad[pl.ds(at + 8, block), :] = conv.astype(f32)
        gate_ref[pl.ds(at, block), :] = pick(
            mc, [contract(x, wg_ref[m], 1, 0) for m in range(M)]
        ).astype(bf16)
        return 0

    lax.fori_loop(0, rows // block, matmul, 0)
    taps = cw_ref[...]
    base = cb_ref[...]

    def convolve(r, _):
        at = pl.multiple_of(r * LANES, LANES)
        v = pad[pl.ds(at, LANES + 8), :]
        s = base
        for k in range(4):
            s = s + taps[k : k + 1, :] * v[5 + k : 5 + k + LANES, :]
        act = (s * sigmoid(s)).astype(bf16)
        act_ref[pl.ds(at, LANES), :] = act
        part = pick(modr_ref[r], [contract(sp_ref[m], act, 1, 1) for m in range(M)])

        @pl.when(tile == 0)
        def _():
            sums[r] = part

        @pl.when(tile != 0)
        def _():
            sums[r] += part

        proj_ref[r] = sums[r].astype(bf16)
        return 0

    lax.fori_loop(0, rows // LANES, convolve, 0)


def input_stage(x, w, cw, cb, sp, modc, modr):
    rows, width = x.shape
    chans = cw.shape[1]
    psize = sp.shape[1]
    tc = min(256, chans)
    tiles = chans // tc
    full = lambda shape: pl.BlockSpec(shape, lambda j: (0,) * len(shape))
    col = lambda r: pl.BlockSpec((r, tc), lambda j: (0, j))
    return pl.pallas_call(
        functools.partial(in_body, rows=rows, block=min(512, rows)),
        grid=(tiles,),
        in_specs=[
            full((rows, width)),
            pl.BlockSpec((M, width, tc), lambda j: (0, 0, j)),
            pl.BlockSpec((M, width, tc), lambda j: (0, 0, j + tiles)),
            col(4),
            col(1),
            pl.BlockSpec((M, psize, tc), lambda j: (0, 0, j)),
            full((rows, 1)),
            full(modr.shape),
        ],
        out_specs=[col(rows), col(rows), col(rows), full((rows // LANES, psize, LANES))],
        out_shape=[
            jax.ShapeDtypeStruct((rows, chans), bf16),
            jax.ShapeDtypeStruct((rows, chans), bf16),
            jax.ShapeDtypeStruct((rows, chans), bf16),
            jax.ShapeDtypeStruct((rows // LANES, psize, LANES), bf16),
        ],
        scratch_shapes=[pltpu.VMEM((rows + 8, tc), f32), pltpu.VMEM((rows // LANES, psize, LANES), f32)],
        cost_estimate=cost(2 * M * rows * width * 2 * chans, 2 * (rows * width + M * width * 2 * chans)),
        name="input_stage",
    )(x, w, w, cw, cb, sp, modc, modr)


def mm_body(x_ref, w_ref, modc_ref, o_ref, *, rows, block, rhs_dim):
    def step(r, _):
        at = pl.multiple_of(r * block, block)
        x = x_ref[pl.ds(at, block), :]
        mc = modc_ref[pl.ds(at, block), :]
        o_ref[pl.ds(at, block), :] = pick(
            mc, [contract(x, w_ref[m], 1, rhs_dim) for m in range(M)]
        ).astype(o_ref.dtype)
        return 0

    lax.fori_loop(0, rows // block, step, 0)


def select_matmul(x, w, modc, transposed, dtype, name):
    rows, depth = x.shape
    cols = w.shape[1] if transposed else w.shape[2]
    tn = min(256, cols)
    wspec = (
        pl.BlockSpec((M, tn, depth), lambda j: (0, j, 0))
        if transposed
        else pl.BlockSpec((M, depth, tn), lambda j: (0, 0, j))
    )
    return pl.pallas_call(
        functools.partial(mm_body, rows=rows, block=min(1024, rows), rhs_dim=1 if transposed else 0),
        grid=(cols // tn,),
        in_specs=[
            pl.BlockSpec((rows, depth), lambda j: (0, 0)),
            wspec,
            pl.BlockSpec((rows, 1), lambda j: (0, 0)),
        ],
        out_specs=pl.BlockSpec((rows, tn), lambda j: (0, j)),
        out_shape=jax.ShapeDtypeStruct((rows, cols), dtype),
        cost_estimate=cost(2 * M * rows * depth * cols, 2 * (rows * depth + M * depth * cols + rows * cols)),
        name=name,
    )(x, w, modc)


def gated_body(x_ref, w_ref, modc_ref, scanned_ref, gate_ref, gg_ref, ggate_ref):
    block = min(512, x_ref.shape[0])

    def step(r, _):
        here = pl.ds(pl.multiple_of(r * block, block), block)
        x = x_ref[here, :]
        gg = pick(modc_ref[here, :], [contract(x, w_ref[m], 1, 1) for m in range(M)]).astype(bf16)
        gg_ref[here, :] = gg
        gate = gate_ref[here, :].astype(f32)
        s = sigmoid(gate)
        ggate_ref[here, :] = (gg.astype(f32) * scanned_ref[here, :] * (s * (1.0 + gate * (1.0 - s)))).astype(bf16)
        return 0

    lax.fori_loop(0, x_ref.shape[0] // block, step, 0)


def gated_grads(cot, w, modc, scanned, gate):
    rows, depth = cot.shape
    cols = w.shape[1]
    tn = min(256, cols)
    col = pl.BlockSpec((rows, tn), lambda j: (0, j))
    return pl.pallas_call(
        gated_body,
        grid=(cols // tn,),
        in_specs=[
            pl.BlockSpec((rows, depth), lambda j: (0, 0)),
            pl.BlockSpec((M, tn, depth), lambda j: (0, j, 0)),
            pl.BlockSpec((rows, 1), lambda j: (0, 0)),
            col,
            col,
        ],
        out_specs=[col, col],
        out_shape=[jax.ShapeDtypeStruct((rows, cols), bf16)] * 2,
        cost_estimate=cost(2 * M * rows * depth * cols, 2 * (rows * depth + M * depth * cols + 5 * rows * cols)),
        name="gated_grads",
    )(cot, w, modc, scanned, gate)


def dgrad_body(gc_ref, gg_ref, w_ref, modc_ref, x_ref, gain_ref, o_ref, part_ref, *, rows, block, chans):
    sums = jnp.zeros((8, part_ref.shape[1]), f32)
    for r in range(rows // block):
        here = slice(r * block, (r + 1) * block)
        gc = gc_ref[here, :]
        gg = gg_ref[here, :]
        out = pick(
            modc_ref[here, :],
            [contract(gc, w_ref[m, :, :chans], 1, 1) + contract(gg, w_ref[m, :, chans:], 1, 1) for m in range(M)],
        )
        o_ref[here, :] = out.astype(bf16)
        terms = out * x_ref[here, :].astype(f32)
        sums = sums + jnp.sum(terms.reshape(block // 8, 8, terms.shape[1]), axis=0)
    part_ref[...] = jnp.sum(sums, axis=0, keepdims=True) / gain_ref[...]


def input_dgrad(gc, gg, w, modc, x, gain):
    rows, chans = gc.shape
    width = w.shape[1]
    tn = 256
    col = pl.BlockSpec((rows, tn), lambda j: (0, j))
    row = pl.BlockSpec((1, tn), lambda j: (0, j))
    return pl.pallas_call(
        functools.partial(dgrad_body, rows=rows, block=min(1024, rows), chans=chans),
        grid=(width // tn,),
        in_specs=[
            pl.BlockSpec((rows, chans), lambda j: (0, 0)),
            pl.BlockSpec((rows, chans), lambda j: (0, 0)),
            pl.BlockSpec((M, tn, 2 * chans), lambda j: (0, j, 0)),
            pl.BlockSpec((rows, 1), lambda j: (0, 0)),
            col,
            row,
        ],
        out_specs=[col, row],
        out_shape=[jax.ShapeDtypeStruct((rows, width), bf16), jax.ShapeDtypeStruct((1, width), f32)],
        cost_estimate=cost(4 * M * rows * chans * width, 2 * (2 * rows * chans + 2 * M * chans * width + 2 * rows * width)),
        name="input_dgrad",
    )(gc, gg, w, modc, x, gain)


def wgrad_body(*refs, sets, add):
    xs, gs, mods = refs[1 : 1 + sets], refs[1 + sets : 1 + 2 * sets], refs[1 + 2 * sets : 1 + 3 * sets]
    o_ref, masked = refs[-2], refs[-1]

    @pl.when(pl.program_id(0) == 0)
    def _():
        for n in range(sets):
            g = gs[n][...]
            for m in range(M):
                masked[n, m] = jnp.where(mods[n][...] == m, g, jnp.zeros_like(g))

    there = refs[0][0] >= 0

    def each(m, _):
        parts = [jnp.where(there, contract(xs[n][...], masked[n, m], 0, 0), 0.0) for n in range(sets)]
        total = functools.reduce(jnp.add, parts)
        if add:
            total = total + refs[1 + 3 * sets][m].astype(f32)
        o_ref[m] = total.astype(bf16)
        return 0

    lax.fori_loop(0, M, each, 0)


def half_wgrad(half, xs, gs, mods, got, name):
    sets = len(xs)
    rows, width = xs[0].shape
    cols = gs[0].shape[1]
    td = min(512, width // 2)
    steps = width // 2 // td
    full = lambda shape: pl.BlockSpec(shape, lambda i, pos: (0, 0))
    out_spec = pl.BlockSpec((M, td, cols), lambda i, pos: (0, i, 0))
    extra = () if got is None else (got,)
    return pl.pallas_call(
        functools.partial(wgrad_body, sets=sets, add=got is not None),
        grid_spec=pltpu.PrefetchScalarGridSpec(
            num_scalar_prefetch=1,
            grid=(steps,),
            in_specs=[pl.BlockSpec((rows, td), lambda i, pos: (0, i + pos[0] * steps))] * sets
            + [full((rows, cols))] * sets
            + [full((rows, 1))] * sets
            + [out_spec] * len(extra),
            out_specs=out_spec,
            scratch_shapes=[pltpu.VMEM((sets, M, rows, cols), bf16)],
        ),
        out_shape=jax.ShapeDtypeStruct((M, width // 2, cols), bf16),
        cost_estimate=cost(sets * M * rows * width * cols, sets * (rows * width + 2 * rows * cols) + 2 * M * width * cols),
        name=name,
    )(half, *xs, *gs, *mods, *extra)


def rows_wgrad_body(pos_ref, xt_ref, g_ref, modl_ref, *rest, groups):
    outs = rest[len(rest) - len(groups) :]
    xt = xt_ref[...]
    for n, group in enumerate(groups):
        for k, m in enumerate(group):
            total = contract(jnp.where(modl_ref[...] == m, xt, jnp.zeros_like(xt)), g_ref[...], 1, 0)
            if len(rest) > len(groups):
                total = total + rest[n][k].astype(f32)
            outs[n][k] = total.astype(bf16)


def rows_wgrad(half, xt, g, modl, got, groups, name):
    width, rows = xt.shape
    cols = g.shape[1]
    tn = 512
    out_specs = [pl.BlockSpec((len(group), width // 2, tn), lambda i, pos: (0, 0, i)) for group in groups]
    return pl.pallas_call(
        functools.partial(rows_wgrad_body, groups=groups),
        grid_spec=pltpu.PrefetchScalarGridSpec(
            num_scalar_prefetch=1,
            grid=(cols // tn,),
            in_specs=[
                pl.BlockSpec((width // 2, rows), lambda i, pos: (pos[0], 0)),
                pl.BlockSpec((rows, tn), lambda i, pos: (0, i)),
                pl.BlockSpec((1, rows), lambda i, pos: (0, 0)),
            ]
            + (out_specs if got else []),
            out_specs=out_specs,
        ),
        out_shape=[jax.ShapeDtypeStruct((len(group), width // 2, cols), bf16) for group in groups],
        cost_estimate=cost(M * rows * width * cols, rows * width + 2 * rows * cols + 2 * M * width * cols),
        name=name,
    )(half, xt, g, modl, *got)


UNROLL = 4


def spread(value, ref):
    for t in range(LANES):
        ref[t] = jnp.broadcast_to(value[:, t : t + 1], (16, LANES))


def fold_columns(ref):
    halves = []
    for h in range(2):
        groups = [
            fold_lanes([ref[8 * i + j, 8 * h : 8 * h + 8, :] for j in range(8)], (1, 2, 4)) for i in range(16)
        ]
        halves.append(fold_lanes(groups, (8, 16, 32, 64)))
    return jnp.concatenate(halves, axis=0)


def row_of(ref, t):
    wide = jnp.broadcast_to(ref[pl.ds(t, 1), :], (8, ref.shape[1]))
    return [wide[:, k * LANES : (k + 1) * LANES] for k in range(ref.shape[1] // LANES)]


def add_all(parts):
    while len(parts) > 1:
        parts = [functools.reduce(jnp.add, parts[k : k + 2]) for k in range(0, len(parts), 2)]
    return parts[0]


def state_vectors(pj_ref, rank):
    b = pj_ref[0, rank : rank + 16, :].astype(f32) + pj_ref[0, rank + 32 : rank + 48, :].astype(f32)
    c = pj_ref[0, rank + 16 : rank + 32, :].astype(f32) + pj_ref[0, rank + 48 : rank + 64, :].astype(f32)
    return b, c


def by_modality(mod, rows):
    return jnp.concatenate([jnp.where(mod == m, rows, jnp.zeros_like(rows)) for m in range(M)], axis=0)


def fold_all(ref):
    groups = [fold_rows([ref[8 * i + j] for j in range(8)]) for i in range(LANES // 8)]
    return jnp.concatenate(groups, axis=0)


def scan_fwd_body(pj_ref, act_ref, gate_ref, sp_ref, sb_ref, ld_ref, skip_ref, modc_ref, modr_ref,
                  delta_ref, sig_ref, gated_ref, scanned_ref, prev_ref, final_ref, b_s, c_s,
                  state, pre_s, d_s, u_s, r_s, yp_s):
    span, chans = act_ref.shape
    rank = pj_ref.shape[1] - 64
    tiles = chans // LANES

    @pl.when(pl.program_id(0) == 0)
    def _():
        state[...] = jnp.zeros_like(state)

    pre_s[...] = contract(by_modality(modr_ref[0], pj_ref[0, :rank, :]), sp_ref[...], 0, 0)
    r_s[...] = -jnp.exp(ld_ref[...]) * log2e
    b, c = state_vectors(pj_ref, rank)
    spread(b, b_s)
    spread(c, c_s)
    bias = [sb_ref[m : m + 1, :] for m in range(M)]

    pre = pre_s[...] + pick(modc_ref[...], bias)
    z = jnp.exp(-jnp.abs(pre))
    delta = (jnp.maximum(pre, 0.0) + jnp.log1p(z)).astype(bf16)
    delta_ref[...] = delta
    inv = 1.0 / (1.0 + z)
    sig_ref[...] = jnp.where(pre >= 0, inv, z * inv)
    act = act_ref[...].astype(f32)
    d = delta.astype(f32)
    d_s[...] = d
    u_s[...] = d * act

    def positions(i, carry):
        st = list(carry)
        for j in range(UNROLL):
            t = i * UNROLL + j
            at = pl.multiple_of(t * 16, 16)
            d_row, u_row = row_of(d_s, t), row_of(u_s, t)
            for k in range(tiles):
                cols = slice(k * LANES, (k + 1) * LANES)
                out = []
                for h in range(2):
                    n = 2 * k + h
                    rows = slice(8 * h, 8 * h + 8)
                    prev_ref[pl.ds(at + 8 * h, 8), cols] = st[n]
                    st[n] = jnp.exp2(d_row[k] * r_s[rows, cols]) * st[n] + u_row[k] * b_s[t, rows, :]
                    out.append(st[n] * c_s[t, rows, :])
                yp_s[t, :, cols] = out[0] + out[1]
        return tuple(st)

    first = tuple(
        state[8 * h : 8 * h + 8, k * LANES : (k + 1) * LANES] for k in range(tiles) for h in range(2)
    )
    st = lax.fori_loop(0, span // UNROLL, positions, first)
    for k in range(tiles):
        for h in range(2):
            state[8 * h : 8 * h + 8, k * LANES : (k + 1) * LANES] = st[2 * k + h]
    final_ref[...] = state[...]
    scanned = fold_all(yp_s) + skip_ref[...] * act
    scanned_ref[...] = scanned
    gate = gate_ref[...].astype(f32)
    gated_ref[...] = (scanned * (gate * sigmoid(gate))).astype(bf16)


def scan_forward(pj, act, gate, step_proj, step_bias, log_decay, skip, modc, modr):
    rows, chans = act.shape
    blocks = rows // LANES
    row = pl.BlockSpec((LANES, chans), lambda i: (i, 0))
    full = lambda shape: pl.BlockSpec(shape, lambda i: (0,) * len(shape))
    wide = pl.BlockSpec((LANES, 16, LANES), lambda i: (i, 0, 0))
    return pl.pallas_call(
        scan_fwd_body,
        grid=(blocks,),
        in_specs=[
            pl.BlockSpec((1,) + pj.shape[1:], lambda i: (i, 0, 0)),
            row, row,
            full(step_proj.shape),
            full((M, chans)),
            full((16, chans)),
            full((1, chans)),
            pl.BlockSpec((LANES, 1), lambda i: (i, 0)),
            pl.BlockSpec((1, 1, LANES), lambda i: (i, 0, 0)),
        ],
        out_specs=[
            row, row, row, row,
            pl.BlockSpec((LANES * 16, chans), lambda i: (i, 0)),
            full((16, chans)),
            wide,
            wide,
        ],
        out_shape=[
            jax.ShapeDtypeStruct((rows, chans), bf16),
            jax.ShapeDtypeStruct((rows, chans), f32),
            jax.ShapeDtypeStruct((rows, chans), bf16),
            jax.ShapeDtypeStruct((rows, chans), f32),
            jax.ShapeDtypeStruct((rows * 16, chans), f32),
            jax.ShapeDtypeStruct((16, chans), f32),
            jax.ShapeDtypeStruct((rows, 16, LANES), f32),
            jax.ShapeDtypeStruct((rows, 16, LANES), f32),
        ],
        scratch_shapes=[pltpu.VMEM((16, chans), f32)] + [pltpu.VMEM((LANES, chans), f32)] * 3
        + [pltpu.VMEM((16, chans), f32)]
        + [pltpu.VMEM((LANES, 8, chans), f32)],
        cost_estimate=cost(40e9, 64 * rows * chans + 20 * rows * chans),
        name="scan_forward",
    )(pj, act, gate, step_proj, step_bias, log_decay, skip, modc, modr)


def scan_bwd_body(pj_ref, act_ref, gate_ref, gg_ref, delta_ref, sig_ref, prev_ref, final_ref, b_s, c_s,
                  sp_ref, ld_ref, skip_ref, modc_ref, modr_ref,
                  gas_ref, gpt_ref, glogd_ref, gskip_ref, gbias_ref, gstep_ref,
                  carry_w, acc, later, d_s, u_s, gs_s, r_s, gp_s, hp_s, p_s, q_s):
    span, chans = act_ref.shape
    rank = pj_ref.shape[1] - 64
    tiles = chans // LANES

    @pl.when(pl.program_id(0) == 0)
    def _():
        carry_w[...] = jnp.zeros_like(carry_w)
        acc[...] = jnp.zeros_like(acc)
        later[...] = final_ref[...]
        gskip_ref[...] = jnp.zeros_like(gskip_ref)
        gbias_ref[...] = jnp.zeros_like(gbias_ref)
        gstep_ref[...] = jnp.zeros_like(gstep_ref)

    rates = -jnp.exp(ld_ref[...])
    r_s[...] = rates * log2e

    act = act_ref[...].astype(f32)
    d = delta_ref[...].astype(f32)
    gate = gate_ref[...].astype(f32)
    gs = gg_ref[...].astype(f32) * (gate * sigmoid(gate))
    d_s[...] = d
    u_s[...] = d * act
    gs_s[...] = gs

    def positions(i, carry):
        w, total = list(carry[0]), list(carry[1])
        for j in range(UNROLL):
            t = span - 1 - (i * UNROLL + j)
            at = pl.multiple_of(t * 16, 16)
            grad = []
            d_row, u_row, gs_row = row_of(d_s, t), row_of(u_s, t), row_of(gs_s, t)
            for k in range(tiles):
                cols = slice(k * LANES, (k + 1) * LANES)
                gl, hl = [], []
                for h in range(2):
                    n = 2 * k + h
                    rows = slice(8 * h, 8 * h + 8)
                    rate = r_s[rows, cols]
                    adj = gs_row[k] * c_s[t, rows, :] + w[n]
                    gl.append(adj * b_s[t, rows, :])
                    w[n] = jnp.exp2(d_row[k] * rate) * adj
                    q = w[n] * prev_ref[pl.ds(at + 8 * h, 8), cols]
                    hl.append(q * rate)
                    total[n] = total[n] + q * d_row[k]
                    grad.append(adj * u_row[k])
                gp_s[t, :, cols] = gl[0] + gl[1]
                hp_s[t, :, cols] = hl[0] + hl[1]
            p_s[t, 0:8, :] = add_all(grad[0::2])
            p_s[t, 8:16, :] = add_all(grad[1::2])
        return tuple(w), tuple(total)

    places = [(slice(8 * h, 8 * h + 8), slice(k * LANES, (k + 1) * LANES)) for k in range(tiles) for h in range(2)]
    def read_grad(t, state):
        gs_row = row_of(gs_s, t)
        for h in range(2):
            rows = slice(8 * h, 8 * h + 8)
            q_s[t, rows, :] = add_all(
                [state(h)[:, k * LANES : (k + 1) * LANES] * gs_row[k] for k in range(tiles)]
            )

    def reads(i, _):
        for j in range(UNROLL):
            t = i * UNROLL + j
            at = pl.multiple_of(jnp.minimum(t + 1, span - 1) * 16, 16)
            read_grad(t, lambda h: prev_ref[pl.ds(at + 8 * h, 8), :])
        return 0

    lax.fori_loop(0, span // UNROLL, reads, 0)
    read_grad(span - 1, lambda h: later[8 * h : 8 * h + 8, :])
    later[...] = prev_ref[0:16, :]

    @pl.when(pl.program_id(0) >= 0)
    def _():
        gpt_ref[0, rank + 16 : rank + 32, :] = fold_columns(q_s).astype(bf16)

    held = (carry_w, acc)
    results = lax.fori_loop(
        0, span // UNROLL, positions, tuple(tuple(ref[at] for at in places) for ref in held)
    )
    for ref, values in zip(held, results):
        for n, at in enumerate(places):
            ref[at] = values[n]
    gb = fold_columns(p_s)
    g = fold_all(gp_s)
    gas_ref[...] = (g * d + skip_ref[...] * gs).astype(bf16)
    gpre = (act * g + fold_all(hp_s) * (1.0 / log2e)).astype(bf16).astype(f32) * sig_ref[...]
    glin = gpre.astype(bf16)
    mc = modc_ref[...]
    gbias_ref[...] += jnp.concatenate(
        [jnp.sum(jnp.where(mc == m, gpre, 0.0), axis=0, keepdims=True) for m in range(M)], axis=0
    )
    gskip_ref[...] += jnp.sum(gs * act, axis=0, keepdims=True)
    mr = modr_ref[0]
    gstep_ref[...] += contract(by_modality(mr, pj_ref[0, :rank, :]), glin, 1, 0)
    lin = contract(sp_ref[...], glin, 1, 1)
    gpt_ref[0, :rank, :] = pick(mr, [lin[m * rank : (m + 1) * rank] for m in range(M)]).astype(bf16)
    gpt_ref[0, rank : rank + 16, :] = gb.astype(bf16)
    glogd_ref[...] = acc[...] * rates


def scan_backward(pj, act, gate, gg, delta, sig, prev, final, b, c, step_proj, log_decay, skip, modc, modr):
    rows, chans = act.shape
    blocks = rows // LANES
    rank = step_proj.shape[0] // M
    last = blocks - 1
    row = pl.BlockSpec((LANES, chans), lambda i: (last - i, 0))
    full = lambda shape: pl.BlockSpec(shape, lambda i: (0,) * len(shape))
    slab = lambda shape: pl.BlockSpec((1,) + shape, lambda i: (last - i, 0, 0))
    wide = pl.BlockSpec((LANES, 16, LANES), lambda i: (last - i, 0, 0))
    return pl.pallas_call(
        scan_bwd_body,
        grid=(blocks,),
        in_specs=[
            slab(pj.shape[1:]),
            row, row, row, row, row,
            pl.BlockSpec((LANES * 16, chans), lambda i: (last - i, 0)),
            full((16, chans)),
            wide,
            wide,
            full(step_proj.shape),
            full((16, chans)),
            full((1, chans)),
            pl.BlockSpec((LANES, 1), lambda i: (last - i, 0)),
            slab((1, LANES)),
        ],
        out_specs=[
            row,
            slab((rank + 32, LANES)),
            full((16, chans)),
            full((1, chans)),
            full((M, chans)),
            full(step_proj.shape),
        ],
        out_shape=[
            jax.ShapeDtypeStruct((rows, chans), bf16),
            jax.ShapeDtypeStruct((blocks, rank + 32, LANES), bf16),
            jax.ShapeDtypeStruct((16, chans), f32),
            jax.ShapeDtypeStruct((1, chans), f32),
            jax.ShapeDtypeStruct((M, chans), f32),
            jax.ShapeDtypeStruct(step_proj.shape, f32),
        ],
        scratch_shapes=[pltpu.VMEM((16, chans), f32)] * 3
        + [pltpu.VMEM((LANES, chans), f32)] * 3
        + [pltpu.VMEM((16, chans), f32)]
        + [pltpu.VMEM((LANES, 8, chans), f32)] * 2
        + [pltpu.VMEM((LANES, 16, LANES), f32)] * 2,
        cost_estimate=cost(60e9, 64 * rows * chans + 20 * rows * chans),
        name="scan_backward",
    )(pj, act, gate, gg, delta, sig, prev, final, b, c, step_proj, log_decay, skip, modc, modr)


def conv_bwd_body(gp_ref, sp_ref, gas_ref, ci_ref, act_ref, cw_ref, cb_ref, modc_ref, modr_ref,
                  gci_ref, gstate_ref, gcw_ref, pad, tail, *, rows):
    cols = pad.shape[1]
    pad[0:8, :] = jnp.zeros((8, cols), f32)
    tail[rows : rows + 8, :] = jnp.zeros((8, cols), f32)
    gstate_ref[...] = jnp.zeros_like(gstate_ref)
    taps = cw_ref[...]
    base = cb_ref[...]

    def first(r, sums):
        at = pl.multiple_of(r * LANES, LANES)
        here = pl.ds(at, LANES)
        pad[pl.ds(at + 8, LANES), :] = ci_ref[here, :].astype(f32)
        v = pad[pl.ds(at, LANES + 8), :]
        shifted = [v[5 + k : 5 + k + LANES, :] for k in range(4)]
        s = base
        for k in range(4):
            s = s + taps[k : k + 1, :] * shifted[k]
        sg = sigmoid(s)
        gp = gp_ref[r]
        ga = pick(modc_ref[here, :], [contract(gp, sp_ref[m], 0, 0) for m in range(M)])
        gcp = (ga + gas_ref[here, :].astype(f32)) * (sg * (1.0 + s * (1.0 - sg)))
        tail[here, :] = gcp
        act = act_ref[here, :]
        mr = modr_ref[r]
        for m in range(M):
            gstate_ref[m] += contract(jnp.where(mr == m, gp, jnp.zeros_like(gp)), act, 1, 0)
        terms = [gcp * part for part in shifted] + [gcp]
        return tuple(
            total + jnp.sum(term.reshape(LANES // 8, 8, cols), axis=0) for total, term in zip(sums, terms)
        )

    sums = lax.fori_loop(0, rows // LANES, first, (jnp.zeros((8, cols), f32),) * 5)
    gcw_ref[...] = jnp.concatenate(
        [jnp.sum(total, axis=0, keepdims=True) for total in sums] + [jnp.zeros((3, cols), f32)], axis=0
    )

    def second(r, _):
        at = pl.multiple_of(r * LANES, LANES)
        v = tail[pl.ds(at, LANES + 8), :]
        s = taps[0:1, :] * v[3 : 3 + LANES, :]
        for k in range(1, 4):
            s = s + taps[k : k + 1, :] * v[3 - k : 3 - k + LANES, :]
        gci_ref[pl.ds(at, LANES), :] = s.astype(bf16)
        return 0

    lax.fori_loop(0, rows // LANES, second, 0)


def conv_backward(gp, sp, gas, ci, act, cw, cb, modc, modr):
    rows, chans = ci.shape
    psize = sp.shape[1]
    tc = min(256, chans)
    col = lambda r: pl.BlockSpec((r, tc), lambda j: (0, j))
    full = lambda shape: pl.BlockSpec(shape, lambda j: (0,) * len(shape))
    wide = pl.BlockSpec((M, psize, tc), lambda j: (0, 0, j))
    return pl.pallas_call(
        functools.partial(conv_bwd_body, rows=rows),
        grid=(chans // tc,),
        in_specs=[full(gp.shape), wide, col(rows), col(rows), col(rows), col(4), col(1), full((rows, 1)), full(modr.shape)],
        out_specs=[col(rows), wide, col(8)],
        out_shape=[
            jax.ShapeDtypeStruct((rows, chans), bf16),
            jax.ShapeDtypeStruct((M, psize, chans), f32),
            jax.ShapeDtypeStruct((8, chans), f32),
        ],
        scratch_shapes=[pltpu.VMEM((rows + 8, tc), f32), pltpu.VMEM((rows + 8, tc), f32)],
        cost_estimate=cost(8 * M * rows * psize * chans, 10 * rows * chans),
        name="conv_backward",
    )(gp, sp, gas, ci, act, cw, cb, modc, modr)


def interleave_body(pos_ref, conv_ref, gate_ref, *rest, group):
    o_ref = rest[-1]
    sub = lax.broadcasted_iota(jnp.int32, (8, LANES), 0)

    def step(r, _):
        at = pl.multiple_of(r * group, group)
        sources = [ref[0, pl.ds(at, group), :].astype(f32) for ref in (conv_ref, gate_ref)]
        for h in range(group // 8):
            vs = [
                source[8 * h : 8 * h + 8, k * LANES : (k + 1) * LANES] for k in range(4) for source in sources
            ]
            for shift in (1, 2, 4):
                mask = (sub & shift) == 0
                swapped = list(vs)
                for j in range(8):
                    if j & shift == 0:
                        a, b = vs[j], vs[j | shift]
                        swapped[j] = jnp.where(mask, a, pltpu.roll(b, shift, 0))
                        swapped[j | shift] = jnp.where(mask, pltpu.roll(a, 8 - shift, 0), b)
                vs = swapped
            for d in range(8):
                o_ref[0, pl.ds((at + 8 * h + d) * 8, 8), :] = vs[d]
        return 0

    lax.fori_loop(0, conv_ref.shape[1] // group, step, 0)


def split_body(pos_ref, conv_ref, gate_ref, *rest):
    o_ref = rest[-1]
    o_ref[0, :, 0, :] = conv_ref[0].astype(f32)
    o_ref[0, :, 1, :] = gate_ref[0].astype(f32)


def place_input_grad(half, conv, gate, target):
    _, height, chans = conv.shape
    td = min(512, height)
    steps = height // td
    packed = chans == 4 * LANES
    if packed:
        shape, block = (M, 2 * height * 8, LANES), (1, td * 8, LANES)
        where = lambda m, i, pos: (m, i + pos[0] * steps, 0)
        body = functools.partial(interleave_body, group=64)
    else:
        shape, block = (M, 2 * height, 2, chans), (1, td, 2, chans)
        where = lambda m, i, pos: (m, i + pos[0] * steps, 0, 0)
        body = split_body
    source = pl.BlockSpec((1, td, chans), lambda m, i, pos: (m, i, 0))
    extra = () if target is None else (target,)
    return pl.pallas_call(
        body,
        grid_spec=pltpu.PrefetchScalarGridSpec(
            num_scalar_prefetch=1,
            grid=(M, steps),
            in_specs=[source, source] + [pl.BlockSpec(memory_space=pl.ANY)] * len(extra),
            out_specs=pl.BlockSpec(block, where),
        ),
        out_shape=jax.ShapeDtypeStruct(shape, f32),
        input_output_aliases={} if target is None else {3: 0},
        cost_estimate=cost(0, 12 * M * height * chans),
        name="place_input_grad",
    )(half, conv, gate, *extra)


def input_grad_layout(value, width, chans):
    if value.ndim == 4:
        return value
    return value.reshape(M, width, chans // LANES, 2, LANES).transpose(0, 1, 3, 2, 4).reshape(M, width, 2, chans)


def join_body(pos_ref, mine_ref, got_ref, o_ref):
    mine = pl.program_id(1) == pos_ref[0]

    @pl.when(mine)
    def _():
        o_ref[0] = mine_ref[0].astype(f32)

    @pl.when(jnp.logical_not(mine))
    def _():
        o_ref[0] = got_ref[0].astype(f32)


def join_halves(core, mine, got):
    _, height, cols = mine.shape
    part = pl.BlockSpec((1, height, cols), lambda m, i, pos: (m, 0, 0))
    return pl.pallas_call(
        join_body,
        grid_spec=pltpu.PrefetchScalarGridSpec(
            num_scalar_prefetch=1,
            grid=(M, 2),
            in_specs=[part, part],
            out_specs=pl.BlockSpec((1, height, cols), lambda m, i, pos: (m, i, 0)),
        ),
        out_shape=jax.ShapeDtypeStruct((M, 2 * height, cols), f32),
        cost_estimate=cost(0, 12 * M * height * cols),
        name="join_halves",
    )(core, mine, got)


def after(value, *others):
    return lax.optimization_barrier((value,) + others)[0]


def swap_core(value):
    count = lax.axis_size("batch")
    return lax.ppermute(value, "batch", [(i, i ^ 1) for i in range(count)])


def y_others(value):
    count = lax.axis_size("batch")
    return [
        lax.ppermute(value, "batch", [(i, (i + shift) % count) for i in range(count)]) for shift in range(2, count, 2)
    ]


def y_sum(value, *before):
    others = [after(other, *before) for other in y_others(value)]
    if len(others) == 1:
        return value.astype(f32) + others[0].astype(f32)
    chips = len(others) + 1
    mine = lax.axis_index("batch") // 2
    buffer = jnp.zeros((chips,) + value.shape, value.dtype)
    for shift, piece in enumerate([value] + others):
        buffer = lax.dynamic_update_index_in_dim(buffer, piece, (mine + chips - shift) % chips, 0)
    return jnp.sum(buffer.astype(f32), axis=0)


def rounded(value):
    return lax.reduce_precision(value, 8, 7)


def split(value):
    high = rounded(value)
    return jnp.concatenate([high, rounded(value - high)], axis=0).astype(bf16)


def joined(value):
    count = value.shape[0] // 2
    return value[:count].astype(f32) + value[count:].astype(f32)


def small_totals(coarse, fine, first, second):
    rows = coarse.shape[0]
    for step, before in ((lambda value: [swap_core(value)], first), (y_others, second)):
        message = lax.optimization_barrier(jnp.concatenate([rounded(coarse).astype(bf16), split(fine)], axis=0))
        coarse, fine = message[:rows].astype(f32), joined(message[rows:])
        for other in step(message):
            other = after(other, *before)
            coarse, fine = coarse + other[:rows].astype(f32), fine + joined(other[rows:])
    return coarse, fine


def to_owners(pieces):
    return lax.all_to_all(pieces, "own", split_axis=0, concat_axis=0, tiled=False)


def to_all(piece):
    return to_owners(jnp.broadcast_to(piece[None], (lax.axis_size("own"),) + piece.shape))


def gather_small(piece, *before):
    count = lax.axis_size("own")
    mine = lax.axis_index("own")
    held = piece[None]
    bit = 1
    while bit < count:
        got = lax.ppermute(held, "own", [(i, i ^ bit) for i in range(count)])
        got = after(got, before[0])
        before = before[1:] or before
        low = (mine & bit) == 0
        held = jnp.concatenate([jnp.where(low, held, got), jnp.where(low, got, held)], axis=0)
        bit *= 2
    return held


def per_device(
    hidden_in, norm_gain, input_proj, conv_weight, conv_bias, state_proj, step_proj, step_bias,
    log_decay, skip_gain, output_proj, modality, grad_out,
):
    own_count = lax.axis_size("own")
    own_index = lax.axis_index("own")
    core = lax.axis_index("batch") % 2
    width = hidden_in.shape[2]
    rows = modality.shape[1]
    span = rows // own_count
    chans = input_proj.shape[3]
    rank = step_proj.shape[1]
    states = log_decay.shape[0]
    psize = state_proj.shape[2]
    chan_at = own_index * chans

    core_at = core.astype(jnp.int32).reshape(1)
    other_at = (1 - core).astype(jnp.int32).reshape(1)

    modc = modality.reshape(rows, 1)
    modl = modality.reshape(1, rows)
    modr = modality.reshape(rows // LANES, 1, LANES)
    w_in = input_proj.reshape(M, width, 2 * chans)
    sp_t = jnp.swapaxes(state_proj, 1, 2)
    step_rows = step_proj.reshape(M * rank, chans)
    part = lambda table: lax.dynamic_slice_in_dim(table, chan_at, chans, table.ndim - 1)
    cw = part(conv_weight)
    cb = part(conv_bias).reshape(1, chans)
    decay = part(log_decay)
    skip = part(skip_gain).reshape(1, chans)

    resid = hidden_in[0].astype(f32)
    inverse = lax.rsqrt(jnp.mean(resid * resid, axis=-1, keepdims=True) + epsilon)
    normed = (resid * inverse * norm_gain).astype(bf16)
    mod_others, normed_others = y_others(modality), y_others(normed)
    x = lax.all_gather(normed, "own", axis=0, tiled=True)
    cot = lax.all_gather(after(grad_out[0], x, w_in, *mod_others, *normed_others), "own", axis=0, tiled=True)

    conv_in, gate, act, proj_part = input_stage(x, w_in, cw, cb, sp_t, modc, modr)
    modcs = [modc] + [other.reshape(rows, 1) for other in mod_others]
    blocks = rows // LANES
    per_owner = blocks // own_count
    pieces = proj_part.reshape(own_count, per_owner * psize, LANES)
    proj = jnp.sum(to_owners(pieces).astype(f32), axis=0).reshape(per_owner, psize, LANES)
    high = proj.astype(bf16)
    low = (proj[:, rank:] - high[:, rank:].astype(f32)).astype(bf16)
    packed = jnp.concatenate([high, low], axis=1)
    pj = to_all(packed).reshape(blocks, psize + 2 * states, LANES)
    xs = [x] + [lax.all_gather(after(other, pj), "own", axis=0, tiled=True) for other in normed_others]
    delta, sig, gated, scanned, prev, final, b_wide, c_wide = scan_forward(
        pj, act, gate, step_rows, step_bias, decay, skip, modc, modr
    )
    branch_part = select_matmul(gated, output_proj, modc, False, bf16, "output_stage")
    branch = lax.psum_scatter(branch_part, "own", scatter_dimension=0, tiled=True)
    block_out = (resid + branch.astype(f32)).astype(bf16)[None]

    gg, ggate = gated_grads(cot, output_proj, modc, scanned, gate)
    ggates = [ggate] + y_others(ggate)
    gated_t = jnp.swapaxes(gated, 0, 1)
    groups = ((0, 1, 2),)
    out_got = [
        swap_core(value) for value in rows_wgrad(other_at, gated_t, cot, modl, [], groups, "output_wgrad_send")
    ]
    out_half = rows_wgrad(core_at, gated_t, cot, modl, [after(value, branch_part, ggate) for value in out_got], groups, "output_wgrad_keep")
    out_total = y_sum(out_half[0]).astype(bf16)

    gas, gpt, glogd, gskip, gbias, gstep = scan_backward(
        after(pj, branch_part, *out_half), act, gate, gg, delta, sig, prev, final, b_wide, c_wide, step_rows, decay, skip, modc, modr
    )
    gp_own = jnp.sum(to_owners(gpt.reshape(own_count, per_owner * psize, LANES)).astype(f32), axis=0).astype(bf16)
    gp = to_all(gp_own).reshape(blocks, psize, LANES)

    ggates = [ggate] + [after(other, gp_own) for other in ggates[1:]]
    gate_send = half_wgrad(other_at, xs, ggates, modcs, None, "gate_wgrad_send")
    gate_got = swap_core(gate_send)

    gp = after(gp, gate_send, out_total)
    gci, gstate, gcw = conv_backward(gp, sp_t, gas, conv_in, act, cw, cb, modc, modr)
    others = y_others(gci)
    gnormed, gain_part = input_dgrad(gci, ggate, w_in, modc, x, norm_gain.reshape(1, width))

    gcis = [gci] + [after(other, gnormed) for other in others]
    gnormed = lax.psum_scatter(gnormed, "own", scatter_dimension=0, tiled=True)
    conv_send = half_wgrad(other_at, xs, gcis, modcs, None, "conv_wgrad_send")
    gate_mine = half_wgrad(core_at, xs, ggates, modcs, after(gate_got, conv_send, branch), "gate_wgrad_keep")
    gate_recv = swap_core(gate_mine)
    conv_got = after(swap_core(conv_send), gate_mine)
    conv_mine = half_wgrad(core_at, xs, gcis, modcs, conv_got, "conv_wgrad_keep")
    conv_recv = swap_core(conv_mine)
    grad_output = join_halves(core_at, out_total, swap_core(out_total))
    half_placed = place_input_grad(core_at, after(conv_mine, grad_output), gate_mine, None)
    grad_input = place_input_grad(other_at, after(conv_recv, gnormed), gate_recv, half_placed)
    gnormed = gnormed.astype(f32)

    weighted = norm_gain * gnormed
    coupled = jnp.mean(resid * weighted, axis=-1, keepdims=True)
    grad_hidden = (
        grad_out[0].astype(f32) + inverse * weighted - resid * (inverse * inverse * inverse) * coupled
    )[None]

    gain_rows = width // chans
    weights, small = small_totals(
        jnp.concatenate([gstep, gstate.reshape(M * psize, chans)], axis=0),
        jnp.concatenate([glogd, gcw[:5], gskip, gain_part.reshape(gain_rows, chans), gbias], axis=0),
        (conv_send,), (half_placed,),
    )
    grad_step = weights[: M * rank].reshape(M, rank, chans)
    grad_state = jnp.swapaxes(weights[M * rank :].reshape(M, psize, chans), 1, 2)
    grad_bias = small[states + 6 + gain_rows :]
    wide = gather_small(small[: states + 6 + gain_rows], half_placed, half_placed, grad_input)
    grad_gain = jnp.sum(wide[:, states + 6 :], axis=0).reshape(width)
    wide = jnp.swapaxes(wide[:, : states + 6], 0, 1).reshape(states + 6, own_count * chans)
    grad_input = input_grad_layout(grad_input, width, chans)
    return (
        block_out,
        grad_hidden,
        grad_gain,
        grad_input,
        wide[states : states + 4],
        wide[states + 4],
        grad_state,
        grad_step,
        grad_bias,
        wide[:states],
        wide[states + 5],
        grad_output,
    )


def solution(mesh):
    placed = (
        P("batch", "own", None),
        P(),
        P(None, None, None, "own"),
        P(),
        P(),
        P(None, "own", None),
        P(None, None, "own"),
        P(None, "own"),
        P(),
        P(),
        P(None, "own", None),
        P("batch", None),
        P("batch", "own", None),
    )
    return jax.shard_map(
        per_device,
        mesh=mesh,
        in_specs=placed,
        out_specs=(
            P("batch", "own", None),
            P("batch", "own", None),
            P(),
            P(None, None, None, "own"),
            P(),
            P(),
            P(None, "own", None),
            P(None, None, "own"),
            P(None, "own"),
            P(),
            P(),
            P(None, "own", None),
        ),
        check_vma=False,
    )
```

```python
import functools

import jax
import jax.numpy as jnp
from jax import lax
from jax.experimental import pallas as pl
from jax.experimental.pallas import tpu as pltpu
from jax.sharding import PartitionSpec as P

M = 3
epsilon = 1e-05
LANES = 128
log2e = 1.4426950408889634
bf16 = jnp.bfloat16
f32 = jnp.float32


def contract(a, b, ca, cb):
    return lax.dot_general(a, b, (((ca,), (cb,)), ((), ())), preferred_element_type=f32)


def pick(mod, parts):
    out = parts[-1]
    for m in reversed(range(len(parts) - 1)):
        out = jnp.where(mod == m, parts[m], out)
    return out


def sigmoid(v):
    return 1.0 / (1.0 + jnp.exp(-v))


def fold_rows(vs):
    sub = lax.broadcasted_iota(jnp.int32, vs[0].shape, 0)
    for shift in (1, 2, 4):
        mask = (sub & shift) == 0
        vs = [
            jnp.where(mask, a, b) + pltpu.roll(jnp.where(mask, b, a), shift, 0)
            for a, b in zip(vs[0::2], vs[1::2])
        ]
    return vs[0]


def fold_lanes(vs, shifts):
    lane = lax.broadcasted_iota(jnp.int32, vs[0].shape, 1)
    for shift in shifts:
        mask = (lane & shift) == 0
        vs = [
            jnp.where(mask, a, b) + pltpu.roll(jnp.where(mask, b, a), shift, 1)
            for a, b in zip(vs[0::2], vs[1::2])
        ]
    return vs[0]


def cost(flops, nbytes):
    return pl.CostEstimate(flops=int(flops), bytes_accessed=int(nbytes), transcendentals=0)


def in_body(x_ref, wc_ref, wg_ref, cw_ref, cb_ref, sp_ref, modc_ref, modr_ref,
            ci_ref, gate_ref, act_ref, proj_ref, pad, sums, *, rows, block):
    tile = pl.program_id(0)
    pad[0:8, :] = jnp.zeros((8, pad.shape[1]), f32)

    def matmul(r, _):
        at = pl.multiple_of(r * block, block)
        x = x_ref[pl.ds(at, block), :]
        mc = modc_ref[pl.ds(at, block), :]
        conv = pick(mc, [contract(x, wc_ref[m], 1, 0) for m in range(M)]).astype(bf16)
        ci_ref[pl.ds(at, block), :] = conv
        pad[pl.ds(at + 8, block), :] = conv.astype(f32)
        gate_ref[pl.ds(at, block), :] = pick(
            mc, [contract(x, wg_ref[m], 1, 0) for m in range(M)]
        ).astype(bf16)
        return 0

    lax.fori_loop(0, rows // block, matmul, 0)
    taps = cw_ref[...]
    base = cb_ref[...]

    def convolve(r, _):
        at = pl.multiple_of(r * LANES, LANES)
        v = pad[pl.ds(at, LANES + 8), :]
        s = base
        for k in range(4):
            s = s + taps[k : k + 1, :] * v[5 + k : 5 + k + LANES, :]
        act = (s * sigmoid(s)).astype(bf16)
        act_ref[pl.ds(at, LANES), :] = act
        part = pick(modr_ref[r], [contract(sp_ref[m], act, 1, 1) for m in range(M)])

        @pl.when(tile == 0)
        def _():
            sums[r] = part

        @pl.when(tile != 0)
        def _():
            sums[r] += part

        proj_ref[r] = sums[r].astype(bf16)
        return 0

    lax.fori_loop(0, rows // LANES, convolve, 0)


def input_stage(x, w, cw, cb, sp, modc, modr):
    rows, width = x.shape
    chans = cw.shape[1]
    psize = sp.shape[1]
    tc = min(256, chans)
    tiles = chans // tc
    full = lambda shape: pl.BlockSpec(shape, lambda j: (0,) * len(shape))
    col = lambda r: pl.BlockSpec((r, tc), lambda j: (0, j))
    return pl.pallas_call(
        functools.partial(in_body, rows=rows, block=min(512, rows)),
        grid=(tiles,),
        in_specs=[
            full((rows, width)),
            pl.BlockSpec((M, width, tc), lambda j: (0, 0, j)),
            pl.BlockSpec((M, width, tc), lambda j: (0, 0, j + tiles)),
            col(4),
            col(1),
            pl.BlockSpec((M, psize, tc), lambda j: (0, 0, j)),
            full((rows, 1)),
            full(modr.shape),
        ],
        out_specs=[col(rows), col(rows), col(rows), full((rows // LANES, psize, LANES))],
        out_shape=[
            jax.ShapeDtypeStruct((rows, chans), bf16),
            jax.ShapeDtypeStruct((rows, chans), bf16),
            jax.ShapeDtypeStruct((rows, chans), bf16),
            jax.ShapeDtypeStruct((rows // LANES, psize, LANES), bf16),
        ],
        scratch_shapes=[pltpu.VMEM((rows + 8, tc), f32), pltpu.VMEM((rows // LANES, psize, LANES), f32)],
        cost_estimate=cost(2 * M * rows * width * 2 * chans, 2 * (rows * width + M * width * 2 * chans)),
        name="input_stage",
    )(x, w, w, cw, cb, sp, modc, modr)


def mm_body(x_ref, w_ref, modc_ref, o_ref, *, rows, block, rhs_dim):
    def step(r, _):
        at = pl.multiple_of(r * block, block)
        x = x_ref[pl.ds(at, block), :]
        mc = modc_ref[pl.ds(at, block), :]
        o_ref[pl.ds(at, block), :] = pick(
            mc, [contract(x, w_ref[m], 1, rhs_dim) for m in range(M)]
        ).astype(o_ref.dtype)
        return 0

    lax.fori_loop(0, rows // block, step, 0)


def select_matmul(x, w, modc, transposed, dtype, name):
    rows, depth = x.shape
    cols = w.shape[1] if transposed else w.shape[2]
    tn = min(256, cols)
    wspec = (
        pl.BlockSpec((M, tn, depth), lambda j: (0, j, 0))
        if transposed
        else pl.BlockSpec((M, depth, tn), lambda j: (0, 0, j))
    )
    return pl.pallas_call(
        functools.partial(mm_body, rows=rows, block=min(1024, rows), rhs_dim=1 if transposed else 0),
        grid=(cols // tn,),
        in_specs=[
            pl.BlockSpec((rows, depth), lambda j: (0, 0)),
            wspec,
            pl.BlockSpec((rows, 1), lambda j: (0, 0)),
        ],
        out_specs=pl.BlockSpec((rows, tn), lambda j: (0, j)),
        out_shape=jax.ShapeDtypeStruct((rows, cols), dtype),
        cost_estimate=cost(2 * M * rows * depth * cols, 2 * (rows * depth + M * depth * cols + rows * cols)),
        name=name,
    )(x, w, modc)


def gated_body(x_ref, w_ref, modc_ref, scanned_ref, gate_ref, gg_ref, ggate_ref):
    block = min(512, x_ref.shape[0])

    def step(r, _):
        here = pl.ds(pl.multiple_of(r * block, block), block)
        x = x_ref[here, :]
        gg = pick(modc_ref[here, :], [contract(x, w_ref[m], 1, 1) for m in range(M)]).astype(bf16)
        gg_ref[here, :] = gg
        gate = gate_ref[here, :].astype(f32)
        s = sigmoid(gate)
        ggate_ref[here, :] = (gg.astype(f32) * scanned_ref[here, :] * (s * (1.0 + gate * (1.0 - s)))).astype(bf16)
        return 0

    lax.fori_loop(0, x_ref.shape[0] // block, step, 0)


def gated_grads(cot, w, modc, scanned, gate):
    rows, depth = cot.shape
    cols = w.shape[1]
    tn = min(256, cols)
    col = pl.BlockSpec((rows, tn), lambda j: (0, j))
    return pl.pallas_call(
        gated_body,
        grid=(cols // tn,),
        in_specs=[
            pl.BlockSpec((rows, depth), lambda j: (0, 0)),
            pl.BlockSpec((M, tn, depth), lambda j: (0, j, 0)),
            pl.BlockSpec((rows, 1), lambda j: (0, 0)),
            col,
            col,
        ],
        out_specs=[col, col],
        out_shape=[jax.ShapeDtypeStruct((rows, cols), bf16)] * 2,
        cost_estimate=cost(2 * M * rows * depth * cols, 2 * (rows * depth + M * depth * cols + 5 * rows * cols)),
        name="gated_grads",
    )(cot, w, modc, scanned, gate)


def dgrad_body(gc_ref, gg_ref, w_ref, modc_ref, x_ref, gain_ref, o_ref, part_ref, *, rows, block, chans):
    sums = jnp.zeros((8, part_ref.shape[1]), f32)
    for r in range(rows // block):
        here = slice(r * block, (r + 1) * block)
        gc = gc_ref[here, :]
        gg = gg_ref[here, :]
        out = pick(
            modc_ref[here, :],
            [contract(gc, w_ref[m, :, :chans], 1, 1) + contract(gg, w_ref[m, :, chans:], 1, 1) for m in range(M)],
        )
        o_ref[here, :] = out.astype(bf16)
        terms = out * x_ref[here, :].astype(f32)
        sums = sums + jnp.sum(terms.reshape(block // 8, 8, terms.shape[1]), axis=0)
    part_ref[...] = jnp.sum(sums, axis=0, keepdims=True) / gain_ref[...]


def input_dgrad(gc, gg, w, modc, x, gain):
    rows, chans = gc.shape
    width = w.shape[1]
    tn = 256
    col = pl.BlockSpec((rows, tn), lambda j: (0, j))
    row = pl.BlockSpec((1, tn), lambda j: (0, j))
    return pl.pallas_call(
        functools.partial(dgrad_body, rows=rows, block=min(1024, rows), chans=chans),
        grid=(width // tn,),
        in_specs=[
            pl.BlockSpec((rows, chans), lambda j: (0, 0)),
            pl.BlockSpec((rows, chans), lambda j: (0, 0)),
            pl.BlockSpec((M, tn, 2 * chans), lambda j: (0, j, 0)),
            pl.BlockSpec((rows, 1), lambda j: (0, 0)),
            col,
            row,
        ],
        out_specs=[col, row],
        out_shape=[jax.ShapeDtypeStruct((rows, width), bf16), jax.ShapeDtypeStruct((1, width), f32)],
        cost_estimate=cost(4 * M * rows * chans * width, 2 * (2 * rows * chans + 2 * M * chans * width + 2 * rows * width)),
        name="input_dgrad",
    )(gc, gg, w, modc, x, gain)


def wgrad_body(*refs, sets, add):
    xs, gs, mods = refs[1 : 1 + sets], refs[1 + sets : 1 + 2 * sets], refs[1 + 2 * sets : 1 + 3 * sets]
    o_ref, masked = refs[-2], refs[-1]

    @pl.when(pl.program_id(0) == 0)
    def _():
        for n in range(sets):
            g = gs[n][...]
            for m in range(M):
                masked[n, m] = jnp.where(mods[n][...] == m, g, jnp.zeros_like(g))

    there = refs[0][0] >= 0

    def each(m, _):
        parts = [jnp.where(there, contract(xs[n][...], masked[n, m], 0, 0), 0.0) for n in range(sets)]
        total = functools.reduce(jnp.add, parts)
        if add:
            total = total + refs[1 + 3 * sets][m].astype(f32)
        o_ref[m] = total.astype(bf16)
        return 0

    lax.fori_loop(0, M, each, 0)


def half_wgrad(half, xs, gs, mods, got, name):
    sets = len(xs)
    rows, width = xs[0].shape
    cols = gs[0].shape[1]
    td = min(512, width // 2)
    steps = width // 2 // td
    full = lambda shape: pl.BlockSpec(shape, lambda i, pos: (0, 0))
    out_spec = pl.BlockSpec((M, td, cols), lambda i, pos: (0, i, 0))
    extra = () if got is None else (got,)
    return pl.pallas_call(
        functools.partial(wgrad_body, sets=sets, add=got is not None),
        grid_spec=pltpu.PrefetchScalarGridSpec(
            num_scalar_prefetch=1,
            grid=(steps,),
            in_specs=[pl.BlockSpec((rows, td), lambda i, pos: (0, i + pos[0] * steps))] * sets
            + [full((rows, cols))] * sets
            + [full((rows, 1))] * sets
            + [out_spec] * len(extra),
            out_specs=out_spec,
            scratch_shapes=[pltpu.VMEM((sets, M, rows, cols), bf16)],
        ),
        out_shape=jax.ShapeDtypeStruct((M, width // 2, cols), bf16),
        cost_estimate=cost(sets * M * rows * width * cols, sets * (rows * width + 2 * rows * cols) + 2 * M * width * cols),
        name=name,
    )(half, *xs, *gs, *mods, *extra)


def rows_wgrad_body(pos_ref, xt_ref, g_ref, modl_ref, *rest, groups):
    outs = rest[len(rest) - len(groups) :]
    xt = xt_ref[...]
    for n, group in enumerate(groups):
        for k, m in enumerate(group):
            total = contract(jnp.where(modl_ref[...] == m, xt, jnp.zeros_like(xt)), g_ref[...], 1, 0)
            if len(rest) > len(groups):
                total = total + rest[n][k].astype(f32)
            outs[n][k] = total.astype(bf16)


def rows_wgrad(half, xt, g, modl, got, groups, name):
    width, rows = xt.shape
    cols = g.shape[1]
    tn = 512
    out_specs = [pl.BlockSpec((len(group), width // 2, tn), lambda i, pos: (0, 0, i)) for group in groups]
    return pl.pallas_call(
        functools.partial(rows_wgrad_body, groups=groups),
        grid_spec=pltpu.PrefetchScalarGridSpec(
            num_scalar_prefetch=1,
            grid=(cols // tn,),
            in_specs=[
                pl.BlockSpec((width // 2, rows), lambda i, pos: (pos[0], 0)),
                pl.BlockSpec((rows, tn), lambda i, pos: (0, i)),
                pl.BlockSpec((1, rows), lambda i, pos: (0, 0)),
            ]
            + (out_specs if got else []),
            out_specs=out_specs,
        ),
        out_shape=[jax.ShapeDtypeStruct((len(group), width // 2, cols), bf16) for group in groups],
        cost_estimate=cost(M * rows * width * cols, rows * width + 2 * rows * cols + 2 * M * width * cols),
        name=name,
    )(half, xt, g, modl, *got)


UNROLL = 4


def spread(value, ref):
    for t in range(LANES):
        ref[t] = jnp.broadcast_to(value[:, t : t + 1], (16, LANES))


def fold_columns(ref):
    halves = []
    for h in range(2):
        groups = [
            fold_lanes([ref[8 * i + j, 8 * h : 8 * h + 8, :] for j in range(8)], (1, 2, 4)) for i in range(16)
        ]
        halves.append(fold_lanes(groups, (8, 16, 32, 64)))
    return jnp.concatenate(halves, axis=0)


def row_of(ref, t):
    wide = jnp.broadcast_to(ref[pl.ds(t, 1), :], (8, ref.shape[1]))
    return [wide[:, k * LANES : (k + 1) * LANES] for k in range(ref.shape[1] // LANES)]


def add_all(parts):
    while len(parts) > 1:
        parts = [functools.reduce(jnp.add, parts[k : k + 2]) for k in range(0, len(parts), 2)]
    return parts[0]


def state_vectors(pj_ref, rank):
    b = pj_ref[0, rank : rank + 16, :].astype(f32) + pj_ref[0, rank + 32 : rank + 48, :].astype(f32)
    c = pj_ref[0, rank + 16 : rank + 32, :].astype(f32) + pj_ref[0, rank + 48 : rank + 64, :].astype(f32)
    return b, c


def by_modality(mod, rows):
    return jnp.concatenate([jnp.where(mod == m, rows, jnp.zeros_like(rows)) for m in range(M)], axis=0)


def fold_all(ref):
    groups = [fold_rows([ref[8 * i + j] for j in range(8)]) for i in range(LANES // 8)]
    return jnp.concatenate(groups, axis=0)


def scan_fwd_body(pj_ref, act_ref, gate_ref, sp_ref, sb_ref, ld_ref, skip_ref, modc_ref, modr_ref,
                  delta_ref, sig_ref, gated_ref, scanned_ref, prev_ref, final_ref, b_s, c_s,
                  state, pre_s, d_s, u_s, r_s, yp_s):
    span, chans = act_ref.shape
    rank = pj_ref.shape[1] - 64
    tiles = chans // LANES

    @pl.when(pl.program_id(0) == 0)
    def _():
        state[...] = jnp.zeros_like(state)

    pre_s[...] = contract(by_modality(modr_ref[0], pj_ref[0, :rank, :]), sp_ref[...], 0, 0)
    r_s[...] = -jnp.exp(ld_ref[...]) * log2e
    b, c = state_vectors(pj_ref, rank)
    spread(b, b_s)
    spread(c, c_s)
    bias = [sb_ref[m : m + 1, :] for m in range(M)]

    pre = pre_s[...] + pick(modc_ref[...], bias)
    z = jnp.exp(-jnp.abs(pre))
    delta = (jnp.maximum(pre, 0.0) + jnp.log1p(z)).astype(bf16)
    delta_ref[...] = delta
    inv = 1.0 / (1.0 + z)
    sig_ref[...] = jnp.where(pre >= 0, inv, z * inv)
    act = act_ref[...].astype(f32)
    d = delta.astype(f32)
    d_s[...] = d
    u_s[...] = d * act

    def positions(i, carry):
        st = list(carry)
        for j in range(UNROLL):
            t = i * UNROLL + j
            at = pl.multiple_of(t * 16, 16)
            d_row, u_row = row_of(d_s, t), row_of(u_s, t)
            for k in range(tiles):
                cols = slice(k * LANES, (k + 1) * LANES)
                out = []
                for h in range(2):
                    n = 2 * k + h
                    rows = slice(8 * h, 8 * h + 8)
                    prev_ref[pl.ds(at + 8 * h, 8), cols] = st[n]
                    st[n] = jnp.exp2(d_row[k] * r_s[rows, cols]) * st[n] + u_row[k] * b_s[t, rows, :]
                    out.append(st[n] * c_s[t, rows, :])
                yp_s[t, :, cols] = out[0] + out[1]
        return tuple(st)

    first = tuple(
        state[8 * h : 8 * h + 8, k * LANES : (k + 1) * LANES] for k in range(tiles) for h in range(2)
    )
    st = lax.fori_loop(0, span // UNROLL, positions, first)
    for k in range(tiles):
        for h in range(2):
            state[8 * h : 8 * h + 8, k * LANES : (k + 1) * LANES] = st[2 * k + h]
    final_ref[...] = state[...]
    scanned = fold_all(yp_s) + skip_ref[...] * act
    scanned_ref[...] = scanned
    gate = gate_ref[...].astype(f32)
    gated_ref[...] = (scanned * (gate * sigmoid(gate))).astype(bf16)


def scan_forward(pj, act, gate, step_proj, step_bias, log_decay, skip, modc, modr):
    rows, chans = act.shape
    blocks = rows // LANES
    row = pl.BlockSpec((LANES, chans), lambda i: (i, 0))
    full = lambda shape: pl.BlockSpec(shape, lambda i: (0,) * len(shape))
    wide = pl.BlockSpec((LANES, 16, LANES), lambda i: (i, 0, 0))
    return pl.pallas_call(
        scan_fwd_body,
        grid=(blocks,),
        in_specs=[
            pl.BlockSpec((1,) + pj.shape[1:], lambda i: (i, 0, 0)),
            row, row,
            full(step_proj.shape),
            full((M, chans)),
            full((16, chans)),
            full((1, chans)),
            pl.BlockSpec((LANES, 1), lambda i: (i, 0)),
            pl.BlockSpec((1, 1, LANES), lambda i: (i, 0, 0)),
        ],
        out_specs=[
            row, row, row, row,
            pl.BlockSpec((LANES * 16, chans), lambda i: (i, 0)),
            full((16, chans)),
            wide,
            wide,
        ],
        out_shape=[
            jax.ShapeDtypeStruct((rows, chans), bf16),
            jax.ShapeDtypeStruct((rows, chans), f32),
            jax.ShapeDtypeStruct((rows, chans), bf16),
            jax.ShapeDtypeStruct((rows, chans), f32),
            jax.ShapeDtypeStruct((rows * 16, chans), f32),
            jax.ShapeDtypeStruct((16, chans), f32),
            jax.ShapeDtypeStruct((rows, 16, LANES), f32),
            jax.ShapeDtypeStruct((rows, 16, LANES), f32),
        ],
        scratch_shapes=[pltpu.VMEM((16, chans), f32)] + [pltpu.VMEM((LANES, chans), f32)] * 3
        + [pltpu.VMEM((16, chans), f32)]
        + [pltpu.VMEM((LANES, 8, chans), f32)],
        cost_estimate=cost(40e9, 64 * rows * chans + 20 * rows * chans),
        name="scan_forward",
    )(pj, act, gate, step_proj, step_bias, log_decay, skip, modc, modr)


def scan_bwd_body(pj_ref, act_ref, gate_ref, gg_ref, delta_ref, sig_ref, prev_ref, final_ref, b_s, c_s,
                  sp_ref, ld_ref, skip_ref, modc_ref, modr_ref,
                  gas_ref, gpt_ref, glogd_ref, gskip_ref, gbias_ref, gstep_ref,
                  carry_w, acc, later, d_s, u_s, gs_s, r_s, gp_s, hp_s, p_s, q_s):
    span, chans = act_ref.shape
    rank = pj_ref.shape[1] - 64
    tiles = chans // LANES

    @pl.when(pl.program_id(0) == 0)
    def _():
        carry_w[...] = jnp.zeros_like(carry_w)
        acc[...] = jnp.zeros_like(acc)
        later[...] = final_ref[...]
        gskip_ref[...] = jnp.zeros_like(gskip_ref)
        gbias_ref[...] = jnp.zeros_like(gbias_ref)
        gstep_ref[...] = jnp.zeros_like(gstep_ref)

    rates = -jnp.exp(ld_ref[...])
    r_s[...] = rates * log2e

    act = act_ref[...].astype(f32)
    d = delta_ref[...].astype(f32)
    gate = gate_ref[...].astype(f32)
    gs = gg_ref[...].astype(f32) * (gate * sigmoid(gate))
    d_s[...] = d
    u_s[...] = d * act
    gs_s[...] = gs

    def positions(i, carry):
        w, total = list(carry[0]), list(carry[1])
        for j in range(UNROLL):
            t = span - 1 - (i * UNROLL + j)
            at = pl.multiple_of(t * 16, 16)
            grad = []
            d_row, u_row, gs_row = row_of(d_s, t), row_of(u_s, t), row_of(gs_s, t)
            for k in range(tiles):
                cols = slice(k * LANES, (k + 1) * LANES)
                gl, hl = [], []
                for h in range(2):
                    n = 2 * k + h
                    rows = slice(8 * h, 8 * h + 8)
                    rate = r_s[rows, cols]
                    adj = gs_row[k] * c_s[t, rows, :] + w[n]
                    gl.append(adj * b_s[t, rows, :])
                    w[n] = jnp.exp2(d_row[k] * rate) * adj
                    q = w[n] * prev_ref[pl.ds(at + 8 * h, 8), cols]
                    hl.append(q * rate)
                    total[n] = total[n] + q * d_row[k]
                    grad.append(adj * u_row[k])
                gp_s[t, :, cols] = gl[0] + gl[1]
                hp_s[t, :, cols] = hl[0] + hl[1]
            p_s[t, 0:8, :] = add_all(grad[0::2])
            p_s[t, 8:16, :] = add_all(grad[1::2])
        return tuple(w), tuple(total)

    places = [(slice(8 * h, 8 * h + 8), slice(k * LANES, (k + 1) * LANES)) for k in range(tiles) for h in range(2)]
    def read_grad(t, state):
        gs_row = row_of(gs_s, t)
        for h in range(2):
            rows = slice(8 * h, 8 * h + 8)
            q_s[t, rows, :] = add_all(
                [state(h)[:, k * LANES : (k + 1) * LANES] * gs_row[k] for k in range(tiles)]
            )

    def reads(i, _):
        for j in range(8):
            t = i * 8 + j
            at = pl.multiple_of(jnp.minimum(t + 1, span - 1) * 16, 16)
            read_grad(t, lambda h: prev_ref[pl.ds(at + 8 * h, 8), :])
        return 0

    lax.fori_loop(0, span // 8, reads, 0)
    read_grad(span - 1, lambda h: later[8 * h : 8 * h + 8, :])
    later[...] = prev_ref[0:16, :]

    @pl.when(pl.program_id(0) >= 0)
    def _():
        gpt_ref[0, rank + 16 : rank + 32, :] = fold_columns(q_s).astype(bf16)

    held = (carry_w, acc)
    results = lax.fori_loop(
        0, span // UNROLL, positions, tuple(tuple(ref[at] for at in places) for ref in held)
    )
    for ref, values in zip(held, results):
        for n, at in enumerate(places):
            ref[at] = values[n]
    gb = fold_columns(p_s)
    g = fold_all(gp_s)
    gas_ref[...] = (g * d + skip_ref[...] * gs).astype(bf16)
    gpre = (act * g + fold_all(hp_s) * (1.0 / log2e)).astype(bf16).astype(f32) * sig_ref[...]
    glin = gpre.astype(bf16)
    mc = modc_ref[...]
    gbias_ref[...] += jnp.concatenate(
        [jnp.sum(jnp.where(mc == m, gpre, 0.0), axis=0, keepdims=True) for m in range(M)], axis=0
    )
    gskip_ref[...] += jnp.sum(gs * act, axis=0, keepdims=True)
    mr = modr_ref[0]
    gstep_ref[...] += contract(by_modality(mr, pj_ref[0, :rank, :]), glin, 1, 0)
    lin = contract(sp_ref[...], glin, 1, 1)
    gpt_ref[0, :rank, :] = pick(mr, [lin[m * rank : (m + 1) * rank] for m in range(M)]).astype(bf16)
    gpt_ref[0, rank : rank + 16, :] = gb.astype(bf16)
    glogd_ref[...] = acc[...] * rates


def scan_backward(pj, act, gate, gg, delta, sig, prev, final, b, c, step_proj, log_decay, skip, modc, modr):
    rows, chans = act.shape
    blocks = rows // LANES
    rank = step_proj.shape[0] // M
    last = blocks - 1
    row = pl.BlockSpec((LANES, chans), lambda i: (last - i, 0))
    full = lambda shape: pl.BlockSpec(shape, lambda i: (0,) * len(shape))
    slab = lambda shape: pl.BlockSpec((1,) + shape, lambda i: (last - i, 0, 0))
    wide = pl.BlockSpec((LANES, 16, LANES), lambda i: (last - i, 0, 0))
    return pl.pallas_call(
        scan_bwd_body,
        grid=(blocks,),
        in_specs=[
            slab(pj.shape[1:]),
            row, row, row, row, row,
            pl.BlockSpec((LANES * 16, chans), lambda i: (last - i, 0)),
            full((16, chans)),
            wide,
            wide,
            full(step_proj.shape),
            full((16, chans)),
            full((1, chans)),
            pl.BlockSpec((LANES, 1), lambda i: (last - i, 0)),
            slab((1, LANES)),
        ],
        out_specs=[
            row,
            slab((rank + 32, LANES)),
            full((16, chans)),
            full((1, chans)),
            full((M, chans)),
            full(step_proj.shape),
        ],
        out_shape=[
            jax.ShapeDtypeStruct((rows, chans), bf16),
            jax.ShapeDtypeStruct((blocks, rank + 32, LANES), bf16),
            jax.ShapeDtypeStruct((16, chans), f32),
            jax.ShapeDtypeStruct((1, chans), f32),
            jax.ShapeDtypeStruct((M, chans), f32),
            jax.ShapeDtypeStruct(step_proj.shape, f32),
        ],
        scratch_shapes=[pltpu.VMEM((16, chans), f32)] * 3
        + [pltpu.VMEM((LANES, chans), f32)] * 3
        + [pltpu.VMEM((16, chans), f32)]
        + [pltpu.VMEM((LANES, 8, chans), f32)] * 2
        + [pltpu.VMEM((LANES, 16, LANES), f32)] * 2,
        cost_estimate=cost(60e9, 64 * rows * chans + 20 * rows * chans),
        name="scan_backward",
    )(pj, act, gate, gg, delta, sig, prev, final, b, c, step_proj, log_decay, skip, modc, modr)


def conv_bwd_body(gp_ref, sp_ref, gas_ref, ci_ref, act_ref, cw_ref, cb_ref, modc_ref, modr_ref,
                  gci_ref, gstate_ref, gcw_ref, pad, tail, *, rows):
    cols = pad.shape[1]
    pad[0:8, :] = jnp.zeros((8, cols), f32)
    tail[rows : rows + 8, :] = jnp.zeros((8, cols), f32)
    gstate_ref[...] = jnp.zeros_like(gstate_ref)
    taps = cw_ref[...]
    base = cb_ref[...]

    def first(r, sums):
        at = pl.multiple_of(r * LANES, LANES)
        here = pl.ds(at, LANES)
        pad[pl.ds(at + 8, LANES), :] = ci_ref[here, :].astype(f32)
        v = pad[pl.ds(at, LANES + 8), :]
        shifted = [v[5 + k : 5 + k + LANES, :] for k in range(4)]
        s = base
        for k in range(4):
            s = s + taps[k : k + 1, :] * shifted[k]
        sg = sigmoid(s)
        gp = gp_ref[r]
        ga = pick(modc_ref[here, :], [contract(gp, sp_ref[m], 0, 0) for m in range(M)])
        gcp = (ga + gas_ref[here, :].astype(f32)) * (sg * (1.0 + s * (1.0 - sg)))
        tail[here, :] = gcp
        act = act_ref[here, :]
        mr = modr_ref[r]
        for m in range(M):
            gstate_ref[m] += contract(jnp.where(mr == m, gp, jnp.zeros_like(gp)), act, 1, 0)
        terms = [gcp * part for part in shifted] + [gcp]
        return tuple(
            total + jnp.sum(term.reshape(LANES // 8, 8, cols), axis=0) for total, term in zip(sums, terms)
        )

    sums = lax.fori_loop(0, rows // LANES, first, (jnp.zeros((8, cols), f32),) * 5)
    gcw_ref[...] = jnp.concatenate(
        [jnp.sum(total, axis=0, keepdims=True) for total in sums] + [jnp.zeros((3, cols), f32)], axis=0
    )

    def second(r, _):
        at = pl.multiple_of(r * LANES, LANES)
        v = tail[pl.ds(at, LANES + 8), :]
        s = taps[0:1, :] * v[3 : 3 + LANES, :]
        for k in range(1, 4):
            s = s + taps[k : k + 1, :] * v[3 - k : 3 - k + LANES, :]
        gci_ref[pl.ds(at, LANES), :] = s.astype(bf16)
        return 0

    lax.fori_loop(0, rows // LANES, second, 0)


def conv_backward(gp, sp, gas, ci, act, cw, cb, modc, modr):
    rows, chans = ci.shape
    psize = sp.shape[1]
    tc = min(256, chans)
    col = lambda r: pl.BlockSpec((r, tc), lambda j: (0, j))
    full = lambda shape: pl.BlockSpec(shape, lambda j: (0,) * len(shape))
    wide = pl.BlockSpec((M, psize, tc), lambda j: (0, 0, j))
    return pl.pallas_call(
        functools.partial(conv_bwd_body, rows=rows),
        grid=(chans // tc,),
        in_specs=[full(gp.shape), wide, col(rows), col(rows), col(rows), col(4), col(1), full((rows, 1)), full(modr.shape)],
        out_specs=[col(rows), wide, col(8)],
        out_shape=[
            jax.ShapeDtypeStruct((rows, chans), bf16),
            jax.ShapeDtypeStruct((M, psize, chans), f32),
            jax.ShapeDtypeStruct((8, chans), f32),
        ],
        scratch_shapes=[pltpu.VMEM((rows + 8, tc), f32), pltpu.VMEM((rows + 8, tc), f32)],
        cost_estimate=cost(8 * M * rows * psize * chans, 10 * rows * chans),
        name="conv_backward",
    )(gp, sp, gas, ci, act, cw, cb, modc, modr)


def interleave_body(pos_ref, conv_ref, gate_ref, *rest, group):
    o_ref = rest[-1]
    sub = lax.broadcasted_iota(jnp.int32, (8, LANES), 0)

    def step(r, _):
        at = pl.multiple_of(r * group, group)
        sources = [ref[0, pl.ds(at, group), :].astype(f32) for ref in (conv_ref, gate_ref)]
        for h in range(group // 8):
            vs = [
                source[8 * h : 8 * h + 8, k * LANES : (k + 1) * LANES] for k in range(4) for source in sources
            ]
            for shift in (1, 2, 4):
                mask = (sub & shift) == 0
                swapped = list(vs)
                for j in range(8):
                    if j & shift == 0:
                        a, b = vs[j], vs[j | shift]
                        swapped[j] = jnp.where(mask, a, pltpu.roll(b, shift, 0))
                        swapped[j | shift] = jnp.where(mask, pltpu.roll(a, 8 - shift, 0), b)
                vs = swapped
            for d in range(8):
                o_ref[0, pl.ds((at + 8 * h + d) * 8, 8), :] = vs[d]
        return 0

    lax.fori_loop(0, conv_ref.shape[1] // group, step, 0)


def split_body(pos_ref, conv_ref, gate_ref, *rest):
    o_ref = rest[-1]
    o_ref[0, :, 0, :] = conv_ref[0].astype(f32)
    o_ref[0, :, 1, :] = gate_ref[0].astype(f32)


def place_input_grad(half, conv, gate, target):
    _, height, chans = conv.shape
    td = min(512, height)
    steps = height // td
    packed = chans == 4 * LANES
    if packed:
        shape, block = (M, 2 * height * 8, LANES), (1, td * 8, LANES)
        where = lambda m, i, pos: (m, i + pos[0] * steps, 0)
        body = functools.partial(interleave_body, group=64)
    else:
        shape, block = (M, 2 * height, 2, chans), (1, td, 2, chans)
        where = lambda m, i, pos: (m, i + pos[0] * steps, 0, 0)
        body = split_body
    source = pl.BlockSpec((1, td, chans), lambda m, i, pos: (m, i, 0))
    extra = () if target is None else (target,)
    return pl.pallas_call(
        body,
        grid_spec=pltpu.PrefetchScalarGridSpec(
            num_scalar_prefetch=1,
            grid=(M, steps),
            in_specs=[source, source] + [pl.BlockSpec(memory_space=pl.ANY)] * len(extra),
            out_specs=pl.BlockSpec(block, where),
        ),
        out_shape=jax.ShapeDtypeStruct(shape, f32),
        input_output_aliases={} if target is None else {3: 0},
        cost_estimate=cost(0, 12 * M * height * chans),
        name="place_input_grad",
    )(half, conv, gate, *extra)


def input_grad_layout(value, width, chans):
    if value.ndim == 4:
        return value
    return value.reshape(M, width, chans // LANES, 2, LANES).transpose(0, 1, 3, 2, 4).reshape(M, width, 2, chans)


def join_body(pos_ref, mine_ref, got_ref, o_ref):
    mine = pl.program_id(1) == pos_ref[0]

    @pl.when(mine)
    def _():
        o_ref[0] = mine_ref[0].astype(f32)

    @pl.when(jnp.logical_not(mine))
    def _():
        o_ref[0] = got_ref[0].astype(f32)


def join_halves(core, mine, got):
    _, height, cols = mine.shape
    part = pl.BlockSpec((1, height, cols), lambda m, i, pos: (m, 0, 0))
    return pl.pallas_call(
        join_body,
        grid_spec=pltpu.PrefetchScalarGridSpec(
            num_scalar_prefetch=1,
            grid=(M, 2),
            in_specs=[part, part],
            out_specs=pl.BlockSpec((1, height, cols), lambda m, i, pos: (m, i, 0)),
        ),
        out_shape=jax.ShapeDtypeStruct((M, 2 * height, cols), f32),
        cost_estimate=cost(0, 12 * M * height * cols),
        name="join_halves",
    )(core, mine, got)


def after(value, *others):
    return lax.optimization_barrier((value,) + others)[0]


def swap_core(value):
    count = lax.axis_size("batch")
    return lax.ppermute(value, "batch", [(i, i ^ 1) for i in range(count)])


def y_others(value):
    count = lax.axis_size("batch")
    return [
        lax.ppermute(value, "batch", [(i, (i + shift) % count) for i in range(count)]) for shift in range(2, count, 2)
    ]


def y_sum(value, others):
    if len(others) == 1:
        return value.astype(f32) + others[0].astype(f32)
    chips = len(others) + 1
    mine = lax.axis_index("batch") // 2
    buffer = jnp.zeros((chips,) + value.shape, value.dtype)
    for shift, piece in enumerate([value] + others):
        buffer = lax.dynamic_update_index_in_dim(buffer, piece, (mine + chips - shift) % chips, 0)
    return jnp.sum(buffer.astype(f32), axis=0)


def rounded(value):
    return lax.reduce_precision(value, 8, 7)


def split(value):
    high = rounded(value)
    return jnp.concatenate([high, rounded(value - high)], axis=0).astype(bf16)


def joined(value):
    count = value.shape[0] // 2
    return value[:count].astype(f32) + value[count:].astype(f32)


def small_totals(coarse, fine, first, second):
    rows = coarse.shape[0]
    for step, before in ((lambda value: [swap_core(value)], first), (y_others, second)):
        message = lax.optimization_barrier(jnp.concatenate([rounded(coarse).astype(bf16), split(fine)], axis=0))
        coarse, fine = message[:rows].astype(f32), joined(message[rows:])
        for other in step(message):
            other = after(other, *before)
            coarse, fine = coarse + other[:rows].astype(f32), fine + joined(other[rows:])
    return coarse, fine


def to_owners(pieces):
    return lax.all_to_all(pieces, "own", split_axis=0, concat_axis=0, tiled=False)


def to_all(piece):
    return to_owners(jnp.broadcast_to(piece[None], (lax.axis_size("own"),) + piece.shape))


def gather_small(piece, *before):
    count = lax.axis_size("own")
    mine = lax.axis_index("own")
    held = piece[None]
    bit = 1
    while bit < count:
        got = lax.ppermute(held, "own", [(i, i ^ bit) for i in range(count)])
        got = after(got, before[0])
        before = before[1:] or before
        low = (mine & bit) == 0
        held = jnp.concatenate([jnp.where(low, held, got), jnp.where(low, got, held)], axis=0)
        bit *= 2
    return held


def per_device(
    hidden_in, norm_gain, input_proj, conv_weight, conv_bias, state_proj, step_proj, step_bias,
    log_decay, skip_gain, output_proj, modality, grad_out,
):
    own_count = lax.axis_size("own")
    own_index = lax.axis_index("own")
    core = lax.axis_index("batch") % 2
    width = hidden_in.shape[2]
    rows = modality.shape[1]
    span = rows // own_count
    chans = input_proj.shape[3]
    rank = step_proj.shape[1]
    states = log_decay.shape[0]
    psize = state_proj.shape[2]
    chan_at = own_index * chans

    core_at = core.astype(jnp.int32).reshape(1)
    other_at = (1 - core).astype(jnp.int32).reshape(1)

    modc = modality.reshape(rows, 1)
    modl = modality.reshape(1, rows)
    modr = modality.reshape(rows // LANES, 1, LANES)
    w_in = input_proj.reshape(M, width, 2 * chans)
    sp_t = jnp.swapaxes(state_proj, 1, 2)
    step_rows = step_proj.reshape(M * rank, chans)
    part = lambda table: lax.dynamic_slice_in_dim(table, chan_at, chans, table.ndim - 1)
    cw = part(conv_weight)
    cb = part(conv_bias).reshape(1, chans)
    decay = part(log_decay)
    skip = part(skip_gain).reshape(1, chans)

    resid = hidden_in[0].astype(f32)
    inverse = lax.rsqrt(jnp.mean(resid * resid, axis=-1, keepdims=True) + epsilon)
    normed = (resid * inverse * norm_gain).astype(bf16)
    mod_others, normed_others = y_others(modality), y_others(normed)
    x = lax.all_gather(normed, "own", axis=0, tiled=True)
    cot = lax.all_gather(after(grad_out[0], x, w_in, *mod_others, *normed_others), "own", axis=0, tiled=True)

    conv_in, gate, act, proj_part = input_stage(x, w_in, cw, cb, sp_t, modc, modr)
    modcs = [modc] + [other.reshape(rows, 1) for other in mod_others]
    blocks = rows // LANES
    per_owner = blocks // own_count
    pieces = proj_part.reshape(own_count, per_owner * psize, LANES)
    proj = jnp.sum(to_owners(pieces).astype(f32), axis=0).reshape(per_owner, psize, LANES)
    high = proj.astype(bf16)
    low = (proj[:, rank:] - high[:, rank:].astype(f32)).astype(bf16)
    packed = jnp.concatenate([high, low], axis=1)
    pj = to_all(packed).reshape(blocks, psize + 2 * states, LANES)
    xs = [x] + [lax.all_gather(after(other, pj), "own", axis=0, tiled=True) for other in normed_others]
    delta, sig, gated, scanned, prev, final, b_wide, c_wide = scan_forward(
        pj, act, gate, step_rows, step_bias, decay, skip, modc, modr
    )
    branch_part = select_matmul(gated, output_proj, modc, False, bf16, "output_stage")
    branch = lax.psum_scatter(branch_part, "own", scatter_dimension=0, tiled=True)
    block_out = (resid + branch.astype(f32)).astype(bf16)[None]

    gg, ggate = gated_grads(cot, output_proj, modc, scanned, gate)
    ggates = [ggate] + y_others(ggate)
    gated_t = jnp.swapaxes(gated, 0, 1)
    groups = ((0, 1, 2),)
    out_got = [
        swap_core(value) for value in rows_wgrad(other_at, gated_t, cot, modl, [], groups, "output_wgrad_send")
    ]
    out_half = rows_wgrad(core_at, gated_t, cot, modl, [after(value, branch_part, ggate) for value in out_got], groups, "output_wgrad_keep")
    out_others = y_others(out_half[0])

    gas, gpt, glogd, gskip, gbias, gstep = scan_backward(
        after(pj, branch_part, *out_half), act, gate, gg, delta, sig, prev, final, b_wide, c_wide, step_rows, decay, skip, modc, modr
    )
    gp_own = jnp.sum(to_owners(gpt.reshape(own_count, per_owner * psize, LANES)).astype(f32), axis=0).astype(bf16)
    gp = to_all(gp_own).reshape(blocks, psize, LANES)

    ggates = [ggate] + [after(other, gp_own) for other in ggates[1:]]
    gate_send = half_wgrad(other_at, xs, ggates, modcs, None, "gate_wgrad_send")
    gate_got = swap_core(gate_send)

    gp = after(gp, gate_send, *out_others)
    out_total = y_sum(out_half[0], out_others).astype(bf16)
    gci, gstate, gcw = conv_backward(gp, sp_t, gas, conv_in, act, cw, cb, modc, modr)
    others = y_others(gci)
    gnormed, gain_part = input_dgrad(gci, ggate, w_in, modc, x, norm_gain.reshape(1, width))

    gcis = [gci] + [after(other, gnormed) for other in others]
    gnormed = lax.psum_scatter(gnormed, "own", scatter_dimension=0, tiled=True)
    conv_send = half_wgrad(other_at, xs, gcis, modcs, None, "conv_wgrad_send")
    gate_mine = half_wgrad(core_at, xs, ggates, modcs, after(gate_got, conv_send, branch), "gate_wgrad_keep")
    gate_recv = swap_core(gate_mine)
    conv_got = after(swap_core(conv_send), gate_mine)
    conv_mine = half_wgrad(core_at, xs, gcis, modcs, conv_got, "conv_wgrad_keep")
    conv_recv = swap_core(conv_mine)
    grad_output = join_halves(core_at, out_total, swap_core(out_total))
    half_placed = place_input_grad(core_at, after(conv_mine, grad_output), gate_mine, None)
    grad_input = place_input_grad(other_at, after(conv_recv, gnormed), gate_recv, half_placed)
    gnormed = gnormed.astype(f32)

    weighted = norm_gain * gnormed
    coupled = jnp.mean(resid * weighted, axis=-1, keepdims=True)
    grad_hidden = (
        grad_out[0].astype(f32) + inverse * weighted - resid * (inverse * inverse * inverse) * coupled
    )[None]

    gain_rows = width // chans
    weights, small = small_totals(
        jnp.concatenate([gstep, gstate.reshape(M * psize, chans)], axis=0),
        jnp.concatenate([glogd, gcw[:5], gskip, gain_part.reshape(gain_rows, chans), gbias], axis=0),
        (conv_send,), (half_placed,),
    )
    grad_step = weights[: M * rank].reshape(M, rank, chans)
    grad_state = jnp.swapaxes(weights[M * rank :].reshape(M, psize, chans), 1, 2)
    grad_bias = small[states + 6 + gain_rows :]
    wide = gather_small(small[: states + 6 + gain_rows], half_placed, half_placed, grad_input)
    grad_gain = jnp.sum(wide[:, states + 6 :], axis=0).reshape(width)
    wide = jnp.swapaxes(wide[:, : states + 6], 0, 1).reshape(states + 6, own_count * chans)
    grad_input = input_grad_layout(grad_input, width, chans)
    return (
        block_out,
        grad_hidden,
        grad_gain,
        grad_input,
        wide[states : states + 4],
        wide[states + 4],
        grad_state,
        grad_step,
        grad_bias,
        wide[:states],
        wide[states + 5],
        grad_output,
    )


def solution(mesh):
    placed = (
        P("batch", "own", None),
        P(),
        P(None, None, None, "own"),
        P(),
        P(),
        P(None, "own", None),
        P(None, None, "own"),
        P(None, "own"),
        P(),
        P(),
        P(None, "own", None),
        P("batch", None),
        P("batch", "own", None),
    )
    return jax.shard_map(
        per_device,
        mesh=mesh,
        in_specs=placed,
        out_specs=(
            P("batch", "own", None),
            P("batch", "own", None),
            P(),
            P(None, None, None, "own"),
            P(),
            P(),
            P(None, "own", None),
            P(None, None, "own"),
            P(None, "own"),
            P(),
            P(),
            P(None, "own", None),
        ),
        check_vma=False,
    )
```

```python
import functools

import jax
import jax.numpy as jnp
from jax import lax
from jax.experimental import pallas as pl
from jax.experimental.pallas import tpu as pltpu
from jax.sharding import PartitionSpec as P

M = 3
epsilon = 1e-05
LANES = 128
log2e = 1.4426950408889634
bf16 = jnp.bfloat16
f32 = jnp.float32


def contract(a, b, ca, cb):
    return lax.dot_general(a, b, (((ca,), (cb,)), ((), ())), preferred_element_type=f32)


def pick(mod, parts):
    out = parts[-1]
    for m in reversed(range(len(parts) - 1)):
        out = jnp.where(mod == m, parts[m], out)
    return out


def sigmoid(v):
    return 1.0 / (1.0 + jnp.exp(-v))


def fold_rows(vs):
    sub = lax.broadcasted_iota(jnp.int32, vs[0].shape, 0)
    for shift in (1, 2, 4):
        mask = (sub & shift) == 0
        vs = [
            jnp.where(mask, a, b) + pltpu.roll(jnp.where(mask, b, a), shift, 0)
            for a, b in zip(vs[0::2], vs[1::2])
        ]
    return vs[0]


def fold_lanes(vs, shifts):
    lane = lax.broadcasted_iota(jnp.int32, vs[0].shape, 1)
    for shift in shifts:
        mask = (lane & shift) == 0
        vs = [
            jnp.where(mask, a, b) + pltpu.roll(jnp.where(mask, b, a), shift, 1)
            for a, b in zip(vs[0::2], vs[1::2])
        ]
    return vs[0]


def cost(flops, nbytes):
    return pl.CostEstimate(flops=int(flops), bytes_accessed=int(nbytes), transcendentals=0)


def in_body(x_ref, wc_ref, wg_ref, cw_ref, cb_ref, sp_ref, modc_ref, modr_ref,
            ci_ref, gate_ref, act_ref, proj_ref, pad, sums, *, rows, block):
    tile = pl.program_id(0)
    pad[0:8, :] = jnp.zeros((8, pad.shape[1]), f32)

    def matmul(r, _):
        at = pl.multiple_of(r * block, block)
        x = x_ref[pl.ds(at, block), :]
        mc = modc_ref[pl.ds(at, block), :]
        conv = pick(mc, [contract(x, wc_ref[m], 1, 0) for m in range(M)]).astype(bf16)
        ci_ref[pl.ds(at, block), :] = conv
        pad[pl.ds(at + 8, block), :] = conv.astype(f32)
        gate_ref[pl.ds(at, block), :] = pick(
            mc, [contract(x, wg_ref[m], 1, 0) for m in range(M)]
        ).astype(bf16)
        return 0

    lax.fori_loop(0, rows // block, matmul, 0)
    taps = cw_ref[...]
    base = cb_ref[...]

    def convolve(r, _):
        at = pl.multiple_of(r * LANES, LANES)
        v = pad[pl.ds(at, LANES + 8), :]
        s = base
        for k in range(4):
            s = s + taps[k : k + 1, :] * v[5 + k : 5 + k + LANES, :]
        act = (s * sigmoid(s)).astype(bf16)
        act_ref[pl.ds(at, LANES), :] = act
        part = pick(modr_ref[r], [contract(sp_ref[m], act, 1, 1) for m in range(M)])

        @pl.when(tile == 0)
        def _():
            sums[r] = part

        @pl.when(tile != 0)
        def _():
            sums[r] += part

        proj_ref[r] = sums[r].astype(bf16)
        return 0

    lax.fori_loop(0, rows // LANES, convolve, 0)


def input_stage(x, w, cw, cb, sp, modc, modr):
    rows, width = x.shape
    chans = cw.shape[1]
    psize = sp.shape[1]
    tc = min(256, chans)
    tiles = chans // tc
    full = lambda shape: pl.BlockSpec(shape, lambda j: (0,) * len(shape))
    col = lambda r: pl.BlockSpec((r, tc), lambda j: (0, j))
    return pl.pallas_call(
        functools.partial(in_body, rows=rows, block=min(512, rows)),
        grid=(tiles,),
        in_specs=[
            full((rows, width)),
            pl.BlockSpec((M, width, tc), lambda j: (0, 0, j)),
            pl.BlockSpec((M, width, tc), lambda j: (0, 0, j + tiles)),
            col(4),
            col(1),
            pl.BlockSpec((M, psize, tc), lambda j: (0, 0, j)),
            full((rows, 1)),
            full(modr.shape),
        ],
        out_specs=[col(rows), col(rows), col(rows), full((rows // LANES, psize, LANES))],
        out_shape=[
            jax.ShapeDtypeStruct((rows, chans), bf16),
            jax.ShapeDtypeStruct((rows, chans), bf16),
            jax.ShapeDtypeStruct((rows, chans), bf16),
            jax.ShapeDtypeStruct((rows // LANES, psize, LANES), bf16),
        ],
        scratch_shapes=[pltpu.VMEM((rows + 8, tc), f32), pltpu.VMEM((rows // LANES, psize, LANES), f32)],
        cost_estimate=cost(2 * M * rows * width * 2 * chans, 2 * (rows * width + M * width * 2 * chans)),
        name="input_stage",
    )(x, w, w, cw, cb, sp, modc, modr)


def mm_body(x_ref, w_ref, modc_ref, o_ref, *, rows, block, rhs_dim):
    def step(r, _):
        at = pl.multiple_of(r * block, block)
        x = x_ref[pl.ds(at, block), :]
        mc = modc_ref[pl.ds(at, block), :]
        o_ref[pl.ds(at, block), :] = pick(
            mc, [contract(x, w_ref[m], 1, rhs_dim) for m in range(M)]
        ).astype(o_ref.dtype)
        return 0

    lax.fori_loop(0, rows // block, step, 0)


def select_matmul(x, w, modc, transposed, dtype, name):
    rows, depth = x.shape
    cols = w.shape[1] if transposed else w.shape[2]
    tn = min(256, cols)
    wspec = (
        pl.BlockSpec((M, tn, depth), lambda j: (0, j, 0))
        if transposed
        else pl.BlockSpec((M, depth, tn), lambda j: (0, 0, j))
    )
    return pl.pallas_call(
        functools.partial(mm_body, rows=rows, block=min(1024, rows), rhs_dim=1 if transposed else 0),
        grid=(cols // tn,),
        in_specs=[
            pl.BlockSpec((rows, depth), lambda j: (0, 0)),
            wspec,
            pl.BlockSpec((rows, 1), lambda j: (0, 0)),
        ],
        out_specs=pl.BlockSpec((rows, tn), lambda j: (0, j)),
        out_shape=jax.ShapeDtypeStruct((rows, cols), dtype),
        cost_estimate=cost(2 * M * rows * depth * cols, 2 * (rows * depth + M * depth * cols + rows * cols)),
        name=name,
    )(x, w, modc)


def gated_body(x_ref, w_ref, modc_ref, scanned_ref, gate_ref, gg_ref, ggate_ref):
    block = min(512, x_ref.shape[0])

    def step(r, _):
        here = pl.ds(pl.multiple_of(r * block, block), block)
        x = x_ref[here, :]
        gg = pick(modc_ref[here, :], [contract(x, w_ref[m], 1, 1) for m in range(M)]).astype(bf16)
        gg_ref[here, :] = gg
        gate = gate_ref[here, :].astype(f32)
        s = sigmoid(gate)
        ggate_ref[here, :] = (gg.astype(f32) * scanned_ref[here, :] * (s * (1.0 + gate * (1.0 - s)))).astype(bf16)
        return 0

    lax.fori_loop(0, x_ref.shape[0] // block, step, 0)


def gated_grads(cot, w, modc, scanned, gate):
    rows, depth = cot.shape
    cols = w.shape[1]
    tn = min(256, cols)
    col = pl.BlockSpec((rows, tn), lambda j: (0, j))
    return pl.pallas_call(
        gated_body,
        grid=(cols // tn,),
        in_specs=[
            pl.BlockSpec((rows, depth), lambda j: (0, 0)),
            pl.BlockSpec((M, tn, depth), lambda j: (0, j, 0)),
            pl.BlockSpec((rows, 1), lambda j: (0, 0)),
            col,
            col,
        ],
        out_specs=[col, col],
        out_shape=[jax.ShapeDtypeStruct((rows, cols), bf16)] * 2,
        cost_estimate=cost(2 * M * rows * depth * cols, 2 * (rows * depth + M * depth * cols + 5 * rows * cols)),
        name="gated_grads",
    )(cot, w, modc, scanned, gate)


def dgrad_body(gc_ref, gg_ref, w_ref, modc_ref, x_ref, gain_ref, o_ref, part_ref, *, rows, block, chans):
    sums = jnp.zeros((8, part_ref.shape[1]), f32)
    for r in range(rows // block):
        here = slice(r * block, (r + 1) * block)
        gc = gc_ref[here, :]
        gg = gg_ref[here, :]
        out = pick(
            modc_ref[here, :],
            [contract(gc, w_ref[m, :, :chans], 1, 1) + contract(gg, w_ref[m, :, chans:], 1, 1) for m in range(M)],
        )
        o_ref[here, :] = out.astype(bf16)
        terms = out * x_ref[here, :].astype(f32)
        sums = sums + jnp.sum(terms.reshape(block // 8, 8, terms.shape[1]), axis=0)
    part_ref[...] = jnp.sum(sums, axis=0, keepdims=True) / gain_ref[...]


def input_dgrad(gc, gg, w, modc, x, gain):
    rows, chans = gc.shape
    width = w.shape[1]
    tn = 256
    col = pl.BlockSpec((rows, tn), lambda j: (0, j))
    row = pl.BlockSpec((1, tn), lambda j: (0, j))
    return pl.pallas_call(
        functools.partial(dgrad_body, rows=rows, block=min(1024, rows), chans=chans),
        grid=(width // tn,),
        in_specs=[
            pl.BlockSpec((rows, chans), lambda j: (0, 0)),
            pl.BlockSpec((rows, chans), lambda j: (0, 0)),
            pl.BlockSpec((M, tn, 2 * chans), lambda j: (0, j, 0)),
            pl.BlockSpec((rows, 1), lambda j: (0, 0)),
            col,
            row,
        ],
        out_specs=[col, row],
        out_shape=[jax.ShapeDtypeStruct((rows, width), bf16), jax.ShapeDtypeStruct((1, width), f32)],
        cost_estimate=cost(4 * M * rows * chans * width, 2 * (2 * rows * chans + 2 * M * chans * width + 2 * rows * width)),
        name="input_dgrad",
    )(gc, gg, w, modc, x, gain)


def wgrad_body(*refs, sets, add):
    xs, gs, mods = refs[1 : 1 + sets], refs[1 + sets : 1 + 2 * sets], refs[1 + 2 * sets : 1 + 3 * sets]
    o_ref, masked = refs[-2], refs[-1]

    @pl.when(pl.program_id(0) == 0)
    def _():
        for n in range(sets):
            g = gs[n][...]
            for m in range(M):
                masked[n, m] = jnp.where(mods[n][...] == m, g, jnp.zeros_like(g))

    there = refs[0][0] >= 0

    def each(m, _):
        parts = [jnp.where(there, contract(xs[n][...], masked[n, m], 0, 0), 0.0) for n in range(sets)]
        total = functools.reduce(jnp.add, parts)
        if add:
            total = total + refs[1 + 3 * sets][m].astype(f32)
        o_ref[m] = total.astype(bf16)
        return 0

    lax.fori_loop(0, M, each, 0)


def half_wgrad(half, xs, gs, mods, got, name):
    sets = len(xs)
    rows, width = xs[0].shape
    cols = gs[0].shape[1]
    td = min(512, width // 2)
    steps = width // 2 // td
    full = lambda shape: pl.BlockSpec(shape, lambda i, pos: (0, 0))
    out_spec = pl.BlockSpec((M, td, cols), lambda i, pos: (0, i, 0))
    extra = () if got is None else (got,)
    return pl.pallas_call(
        functools.partial(wgrad_body, sets=sets, add=got is not None),
        grid_spec=pltpu.PrefetchScalarGridSpec(
            num_scalar_prefetch=1,
            grid=(steps,),
            in_specs=[pl.BlockSpec((rows, td), lambda i, pos: (0, i + pos[0] * steps))] * sets
            + [full((rows, cols))] * sets
            + [full((rows, 1))] * sets
            + [out_spec] * len(extra),
            out_specs=out_spec,
            scratch_shapes=[pltpu.VMEM((sets, M, rows, cols), bf16)],
        ),
        out_shape=jax.ShapeDtypeStruct((M, width // 2, cols), bf16),
        cost_estimate=cost(sets * M * rows * width * cols, sets * (rows * width + 2 * rows * cols) + 2 * M * width * cols),
        name=name,
    )(half, *xs, *gs, *mods, *extra)


def rows_wgrad_body(pos_ref, xt_ref, g_ref, modl_ref, *rest, groups):
    outs = rest[len(rest) - len(groups) :]
    xt = xt_ref[...]
    for n, group in enumerate(groups):
        for k, m in enumerate(group):
            total = contract(jnp.where(modl_ref[...] == m, xt, jnp.zeros_like(xt)), g_ref[...], 1, 0)
            if len(rest) > len(groups):
                total = total + rest[n][k].astype(f32)
            outs[n][k] = total.astype(bf16)


def rows_wgrad(half, xt, g, modl, got, groups, name):
    width, rows = xt.shape
    cols = g.shape[1]
    tn = 512
    out_specs = [pl.BlockSpec((len(group), width // 2, tn), lambda i, pos: (0, 0, i)) for group in groups]
    return pl.pallas_call(
        functools.partial(rows_wgrad_body, groups=groups),
        grid_spec=pltpu.PrefetchScalarGridSpec(
            num_scalar_prefetch=1,
            grid=(cols // tn,),
            in_specs=[
                pl.BlockSpec((width // 2, rows), lambda i, pos: (pos[0], 0)),
                pl.BlockSpec((rows, tn), lambda i, pos: (0, i)),
                pl.BlockSpec((1, rows), lambda i, pos: (0, 0)),
            ]
            + (out_specs if got else []),
            out_specs=out_specs,
        ),
        out_shape=[jax.ShapeDtypeStruct((len(group), width // 2, cols), bf16) for group in groups],
        cost_estimate=cost(M * rows * width * cols, rows * width + 2 * rows * cols + 2 * M * width * cols),
        name=name,
    )(half, xt, g, modl, *got)


UNROLL = 4


def spread(value, ref):
    for t in range(LANES):
        ref[t] = jnp.broadcast_to(value[:, t : t + 1], (16, LANES))


def fold_columns(ref):
    halves = []
    for h in range(2):
        groups = [
            fold_lanes([ref[8 * i + j, 8 * h : 8 * h + 8, :] for j in range(8)], (1, 2, 4)) for i in range(16)
        ]
        halves.append(fold_lanes(groups, (8, 16, 32, 64)))
    return jnp.concatenate(halves, axis=0)


def row_of(ref, t):
    wide = jnp.broadcast_to(ref[pl.ds(t, 1), :], (8, ref.shape[1]))
    return [wide[:, k * LANES : (k + 1) * LANES] for k in range(ref.shape[1] // LANES)]


def add_all(parts):
    while len(parts) > 1:
        parts = [functools.reduce(jnp.add, parts[k : k + 2]) for k in range(0, len(parts), 2)]
    return parts[0]


def state_vectors(pj_ref, rank):
    b = pj_ref[0, rank : rank + 16, :].astype(f32) + pj_ref[0, rank + 32 : rank + 48, :].astype(f32)
    c = pj_ref[0, rank + 16 : rank + 32, :].astype(f32) + pj_ref[0, rank + 48 : rank + 64, :].astype(f32)
    return b, c


def by_modality(mod, rows):
    return jnp.concatenate([jnp.where(mod == m, rows, jnp.zeros_like(rows)) for m in range(M)], axis=0)


def fold_all(ref):
    groups = [fold_rows([ref[8 * i + j] for j in range(8)]) for i in range(LANES // 8)]
    return jnp.concatenate(groups, axis=0)


def scan_fwd_body(pj_ref, act_ref, gate_ref, sp_ref, sb_ref, ld_ref, skip_ref, modc_ref, modr_ref,
                  delta_ref, sig_ref, gated_ref, scanned_ref, prev_ref, final_ref, b_s, c_s,
                  state, pre_s, d_s, u_s, r_s, yp_s):
    span, chans = act_ref.shape
    rank = pj_ref.shape[1] - 64
    tiles = chans // LANES

    @pl.when(pl.program_id(0) == 0)
    def _():
        state[...] = jnp.zeros_like(state)

    pre_s[...] = contract(by_modality(modr_ref[0], pj_ref[0, :rank, :]), sp_ref[...], 0, 0)
    r_s[...] = -jnp.exp(ld_ref[...]) * log2e
    b, c = state_vectors(pj_ref, rank)
    spread(b, b_s)
    spread(c, c_s)
    bias = [sb_ref[m : m + 1, :] for m in range(M)]

    pre = pre_s[...] + pick(modc_ref[...], bias)
    z = jnp.exp(-jnp.abs(pre))
    delta = (jnp.maximum(pre, 0.0) + jnp.log1p(z)).astype(bf16)
    delta_ref[...] = delta
    inv = 1.0 / (1.0 + z)
    sig_ref[...] = jnp.where(pre >= 0, inv, z * inv)
    act = act_ref[...].astype(f32)
    d = delta.astype(f32)
    d_s[...] = d
    u_s[...] = d * act

    def positions(i, carry):
        st = list(carry)
        for j in range(8):
            t = i * 8 + j
            at = pl.multiple_of(t * 16, 16)
            d_row, u_row = row_of(d_s, t), row_of(u_s, t)
            for k in range(tiles):
                cols = slice(k * LANES, (k + 1) * LANES)
                out = []
                for h in range(2):
                    n = 2 * k + h
                    rows = slice(8 * h, 8 * h + 8)
                    prev_ref[pl.ds(at + 8 * h, 8), cols] = st[n]
                    st[n] = jnp.exp2(d_row[k] * r_s[rows, cols]) * st[n] + u_row[k] * b_s[t, rows, :]
                    out.append(st[n] * c_s[t, rows, :])
                yp_s[t, :, cols] = out[0] + out[1]
        return tuple(st)

    first = tuple(
        state[8 * h : 8 * h + 8, k * LANES : (k + 1) * LANES] for k in range(tiles) for h in range(2)
    )
    st = lax.fori_loop(0, span // 8, positions, first)
    for k in range(tiles):
        for h in range(2):
            state[8 * h : 8 * h + 8, k * LANES : (k + 1) * LANES] = st[2 * k + h]
    final_ref[...] = state[...]
    scanned = fold_all(yp_s) + skip_ref[...] * act
    scanned_ref[...] = scanned
    gate = gate_ref[...].astype(f32)
    gated_ref[...] = (scanned * (gate * sigmoid(gate))).astype(bf16)


def scan_forward(pj, act, gate, step_proj, step_bias, log_decay, skip, modc, modr):
    rows, chans = act.shape
    blocks = rows // LANES
    row = pl.BlockSpec((LANES, chans), lambda i: (i, 0))
    full = lambda shape: pl.BlockSpec(shape, lambda i: (0,) * len(shape))
    wide = pl.BlockSpec((LANES, 16, LANES), lambda i: (i, 0, 0))
    return pl.pallas_call(
        scan_fwd_body,
        grid=(blocks,),
        in_specs=[
            pl.BlockSpec((1,) + pj.shape[1:], lambda i: (i, 0, 0)),
            row, row,
            full(step_proj.shape),
            full((M, chans)),
            full((16, chans)),
            full((1, chans)),
            pl.BlockSpec((LANES, 1), lambda i: (i, 0)),
            pl.BlockSpec((1, 1, LANES), lambda i: (i, 0, 0)),
        ],
        out_specs=[
            row, row, row, row,
            pl.BlockSpec((LANES * 16, chans), lambda i: (i, 0)),
            full((16, chans)),
            wide,
            wide,
        ],
        out_shape=[
            jax.ShapeDtypeStruct((rows, chans), bf16),
            jax.ShapeDtypeStruct((rows, chans), f32),
            jax.ShapeDtypeStruct((rows, chans), bf16),
            jax.ShapeDtypeStruct((rows, chans), f32),
            jax.ShapeDtypeStruct((rows * 16, chans), f32),
            jax.ShapeDtypeStruct((16, chans), f32),
            jax.ShapeDtypeStruct((rows, 16, LANES), f32),
            jax.ShapeDtypeStruct((rows, 16, LANES), f32),
        ],
        scratch_shapes=[pltpu.VMEM((16, chans), f32)] + [pltpu.VMEM((LANES, chans), f32)] * 3
        + [pltpu.VMEM((16, chans), f32)]
        + [pltpu.VMEM((LANES, 8, chans), f32)],
        cost_estimate=cost(40e9, 64 * rows * chans + 20 * rows * chans),
        name="scan_forward",
    )(pj, act, gate, step_proj, step_bias, log_decay, skip, modc, modr)


def scan_bwd_body(pj_ref, act_ref, gate_ref, gg_ref, delta_ref, sig_ref, prev_ref, final_ref, b_s, c_s,
                  sp_ref, ld_ref, skip_ref, modc_ref, modr_ref,
                  gas_ref, gpt_ref, glogd_ref, gskip_ref, gbias_ref, gstep_ref,
                  carry_w, acc, later, d_s, u_s, gs_s, r_s, gp_s, hp_s, p_s, q_s):
    span, chans = act_ref.shape
    rank = pj_ref.shape[1] - 64
    tiles = chans // LANES

    @pl.when(pl.program_id(0) == 0)
    def _():
        carry_w[...] = jnp.zeros_like(carry_w)
        acc[...] = jnp.zeros_like(acc)
        later[...] = final_ref[...]
        gskip_ref[...] = jnp.zeros_like(gskip_ref)
        gbias_ref[...] = jnp.zeros_like(gbias_ref)
        gstep_ref[...] = jnp.zeros_like(gstep_ref)

    rates = -jnp.exp(ld_ref[...])
    r_s[...] = rates * log2e

    act = act_ref[...].astype(f32)
    d = delta_ref[...].astype(f32)
    gate = gate_ref[...].astype(f32)
    gs = gg_ref[...].astype(f32) * (gate * sigmoid(gate))
    d_s[...] = d
    u_s[...] = d * act
    gs_s[...] = gs

    def positions(i, carry):
        w, total = list(carry[0]), list(carry[1])
        for j in range(UNROLL):
            t = span - 1 - (i * UNROLL + j)
            at = pl.multiple_of(t * 16, 16)
            grad = []
            d_row, u_row, gs_row = row_of(d_s, t), row_of(u_s, t), row_of(gs_s, t)
            for k in range(tiles):
                cols = slice(k * LANES, (k + 1) * LANES)
                gl, hl = [], []
                for h in range(2):
                    n = 2 * k + h
                    rows = slice(8 * h, 8 * h + 8)
                    rate = r_s[rows, cols]
                    adj = gs_row[k] * c_s[t, rows, :] + w[n]
                    gl.append(adj * b_s[t, rows, :])
                    w[n] = jnp.exp2(d_row[k] * rate) * adj
                    q = w[n] * prev_ref[pl.ds(at + 8 * h, 8), cols]
                    hl.append(q * rate)
                    total[n] = total[n] + q * d_row[k]
                    grad.append(adj * u_row[k])
                gp_s[t, :, cols] = gl[0] + gl[1]
                hp_s[t, :, cols] = hl[0] + hl[1]
            p_s[t, 0:8, :] = add_all(grad[0::2])
            p_s[t, 8:16, :] = add_all(grad[1::2])
        return tuple(w), tuple(total)

    places = [(slice(8 * h, 8 * h + 8), slice(k * LANES, (k + 1) * LANES)) for k in range(tiles) for h in range(2)]
    def read_grad(t, state):
        gs_row = row_of(gs_s, t)
        for h in range(2):
            rows = slice(8 * h, 8 * h + 8)
            q_s[t, rows, :] = add_all(
                [state(h)[:, k * LANES : (k + 1) * LANES] * gs_row[k] for k in range(tiles)]
            )

    def reads(i, _):
        for j in range(8):
            t = i * 8 + j
            at = pl.multiple_of(jnp.minimum(t + 1, span - 1) * 16, 16)
            read_grad(t, lambda h: prev_ref[pl.ds(at + 8 * h, 8), :])
        return 0

    lax.fori_loop(0, span // 8, reads, 0)
    read_grad(span - 1, lambda h: later[8 * h : 8 * h + 8, :])
    later[...] = prev_ref[0:16, :]

    @pl.when(pl.program_id(0) >= 0)
    def _():
        gpt_ref[0, rank + 16 : rank + 32, :] = fold_columns(q_s).astype(bf16)

    held = (carry_w, acc)
    results = lax.fori_loop(
        0, span // UNROLL, positions, tuple(tuple(ref[at] for at in places) for ref in held)
    )
    for ref, values in zip(held, results):
        for n, at in enumerate(places):
            ref[at] = values[n]
    gb = fold_columns(p_s)
    g = fold_all(gp_s)
    gas_ref[...] = (g * d + skip_ref[...] * gs).astype(bf16)
    gpre = (act * g + fold_all(hp_s) * (1.0 / log2e)).astype(bf16).astype(f32) * sig_ref[...]
    glin = gpre.astype(bf16)
    mc = modc_ref[...]
    gbias_ref[...] += jnp.concatenate(
        [jnp.sum(jnp.where(mc == m, gpre, 0.0), axis=0, keepdims=True) for m in range(M)], axis=0
    )
    gskip_ref[...] += jnp.sum(gs * act, axis=0, keepdims=True)
    mr = modr_ref[0]
    gstep_ref[...] += contract(by_modality(mr, pj_ref[0, :rank, :]), glin, 1, 0)
    lin = contract(sp_ref[...], glin, 1, 1)
    gpt_ref[0, :rank, :] = pick(mr, [lin[m * rank : (m + 1) * rank] for m in range(M)]).astype(bf16)
    gpt_ref[0, rank : rank + 16, :] = gb.astype(bf16)
    glogd_ref[...] = acc[...] * rates


def scan_backward(pj, act, gate, gg, delta, sig, prev, final, b, c, step_proj, log_decay, skip, modc, modr):
    rows, chans = act.shape
    blocks = rows // LANES
    rank = step_proj.shape[0] // M
    last = blocks - 1
    row = pl.BlockSpec((LANES, chans), lambda i: (last - i, 0))
    full = lambda shape: pl.BlockSpec(shape, lambda i: (0,) * len(shape))
    slab = lambda shape: pl.BlockSpec((1,) + shape, lambda i: (last - i, 0, 0))
    wide = pl.BlockSpec((LANES, 16, LANES), lambda i: (last - i, 0, 0))
    return pl.pallas_call(
        scan_bwd_body,
        grid=(blocks,),
        in_specs=[
            slab(pj.shape[1:]),
            row, row, row, row, row,
            pl.BlockSpec((LANES * 16, chans), lambda i: (last - i, 0)),
            full((16, chans)),
            wide,
            wide,
            full(step_proj.shape),
            full((16, chans)),
            full((1, chans)),
            pl.BlockSpec((LANES, 1), lambda i: (last - i, 0)),
            slab((1, LANES)),
        ],
        out_specs=[
            row,
            slab((rank + 32, LANES)),
            full((16, chans)),
            full((1, chans)),
            full((M, chans)),
            full(step_proj.shape),
        ],
        out_shape=[
            jax.ShapeDtypeStruct((rows, chans), bf16),
            jax.ShapeDtypeStruct((blocks, rank + 32, LANES), bf16),
            jax.ShapeDtypeStruct((16, chans), f32),
            jax.ShapeDtypeStruct((1, chans), f32),
            jax.ShapeDtypeStruct((M, chans), f32),
            jax.ShapeDtypeStruct(step_proj.shape, f32),
        ],
        scratch_shapes=[pltpu.VMEM((16, chans), f32)] * 3
        + [pltpu.VMEM((LANES, chans), f32)] * 3
        + [pltpu.VMEM((16, chans), f32)]
        + [pltpu.VMEM((LANES, 8, chans), f32)] * 2
        + [pltpu.VMEM((LANES, 16, LANES), f32)] * 2,
        cost_estimate=cost(60e9, 64 * rows * chans + 20 * rows * chans),
        name="scan_backward",
    )(pj, act, gate, gg, delta, sig, prev, final, b, c, step_proj, log_decay, skip, modc, modr)


def conv_bwd_body(gp_ref, sp_ref, gas_ref, ci_ref, act_ref, cw_ref, cb_ref, modc_ref, modr_ref,
                  gci_ref, gstate_ref, gcw_ref, pad, tail, *, rows):
    cols = pad.shape[1]
    pad[0:8, :] = jnp.zeros((8, cols), f32)
    tail[rows : rows + 8, :] = jnp.zeros((8, cols), f32)
    gstate_ref[...] = jnp.zeros_like(gstate_ref)
    taps = cw_ref[...]
    base = cb_ref[...]

    def first(r, sums):
        at = pl.multiple_of(r * LANES, LANES)
        here = pl.ds(at, LANES)
        pad[pl.ds(at + 8, LANES), :] = ci_ref[here, :].astype(f32)
        v = pad[pl.ds(at, LANES + 8), :]
        shifted = [v[5 + k : 5 + k + LANES, :] for k in range(4)]
        s = base
        for k in range(4):
            s = s + taps[k : k + 1, :] * shifted[k]
        sg = sigmoid(s)
        gp = gp_ref[r]
        ga = pick(modc_ref[here, :], [contract(gp, sp_ref[m], 0, 0) for m in range(M)])
        gcp = (ga + gas_ref[here, :].astype(f32)) * (sg * (1.0 + s * (1.0 - sg)))
        tail[here, :] = gcp
        act = act_ref[here, :]
        mr = modr_ref[r]
        for m in range(M):
            gstate_ref[m] += contract(jnp.where(mr == m, gp, jnp.zeros_like(gp)), act, 1, 0)
        terms = [gcp * part for part in shifted] + [gcp]
        return tuple(
            total + jnp.sum(term.reshape(LANES // 8, 8, cols), axis=0) for total, term in zip(sums, terms)
        )

    sums = lax.fori_loop(0, rows // LANES, first, (jnp.zeros((8, cols), f32),) * 5)
    gcw_ref[...] = jnp.concatenate(
        [jnp.sum(total, axis=0, keepdims=True) for total in sums] + [jnp.zeros((3, cols), f32)], axis=0
    )

    def second(r, _):
        at = pl.multiple_of(r * LANES, LANES)
        v = tail[pl.ds(at, LANES + 8), :]
        s = taps[0:1, :] * v[3 : 3 + LANES, :]
        for k in range(1, 4):
            s = s + taps[k : k + 1, :] * v[3 - k : 3 - k + LANES, :]
        gci_ref[pl.ds(at, LANES), :] = s.astype(bf16)
        return 0

    lax.fori_loop(0, rows // LANES, second, 0)


def conv_backward(gp, sp, gas, ci, act, cw, cb, modc, modr):
    rows, chans = ci.shape
    psize = sp.shape[1]
    tc = min(256, chans)
    col = lambda r: pl.BlockSpec((r, tc), lambda j: (0, j))
    full = lambda shape: pl.BlockSpec(shape, lambda j: (0,) * len(shape))
    wide = pl.BlockSpec((M, psize, tc), lambda j: (0, 0, j))
    return pl.pallas_call(
        functools.partial(conv_bwd_body, rows=rows),
        grid=(chans // tc,),
        in_specs=[full(gp.shape), wide, col(rows), col(rows), col(rows), col(4), col(1), full((rows, 1)), full(modr.shape)],
        out_specs=[col(rows), wide, col(8)],
        out_shape=[
            jax.ShapeDtypeStruct((rows, chans), bf16),
            jax.ShapeDtypeStruct((M, psize, chans), f32),
            jax.ShapeDtypeStruct((8, chans), f32),
        ],
        scratch_shapes=[pltpu.VMEM((rows + 8, tc), f32), pltpu.VMEM((rows + 8, tc), f32)],
        cost_estimate=cost(8 * M * rows * psize * chans, 10 * rows * chans),
        name="conv_backward",
    )(gp, sp, gas, ci, act, cw, cb, modc, modr)


def interleave_body(pos_ref, conv_ref, gate_ref, *rest, group):
    o_ref = rest[-1]
    sub = lax.broadcasted_iota(jnp.int32, (8, LANES), 0)

    def step(r, _):
        at = pl.multiple_of(r * group, group)
        sources = [ref[0, pl.ds(at, group), :].astype(f32) for ref in (conv_ref, gate_ref)]
        for h in range(group // 8):
            vs = [
                source[8 * h : 8 * h + 8, k * LANES : (k + 1) * LANES] for k in range(4) for source in sources
            ]
            for shift in (1, 2, 4):
                mask = (sub & shift) == 0
                swapped = list(vs)
                for j in range(8):
                    if j & shift == 0:
                        a, b = vs[j], vs[j | shift]
                        swapped[j] = jnp.where(mask, a, pltpu.roll(b, shift, 0))
                        swapped[j | shift] = jnp.where(mask, pltpu.roll(a, 8 - shift, 0), b)
                vs = swapped
            for d in range(8):
                o_ref[0, pl.ds((at + 8 * h + d) * 8, 8), :] = vs[d]
        return 0

    lax.fori_loop(0, conv_ref.shape[1] // group, step, 0)


def split_body(pos_ref, conv_ref, gate_ref, *rest):
    o_ref = rest[-1]
    o_ref[0, :, 0, :] = conv_ref[0].astype(f32)
    o_ref[0, :, 1, :] = gate_ref[0].astype(f32)


def place_input_grad(half, conv, gate, target):
    _, height, chans = conv.shape
    td = min(512, height)
    steps = height // td
    packed = chans == 4 * LANES
    if packed:
        shape, block = (M, 2 * height * 8, LANES), (1, td * 8, LANES)
        where = lambda m, i, pos: (m, i + pos[0] * steps, 0)
        body = functools.partial(interleave_body, group=64)
    else:
        shape, block = (M, 2 * height, 2, chans), (1, td, 2, chans)
        where = lambda m, i, pos: (m, i + pos[0] * steps, 0, 0)
        body = split_body
    source = pl.BlockSpec((1, td, chans), lambda m, i, pos: (m, i, 0))
    extra = () if target is None else (target,)
    return pl.pallas_call(
        body,
        grid_spec=pltpu.PrefetchScalarGridSpec(
            num_scalar_prefetch=1,
            grid=(M, steps),
            in_specs=[source, source] + [pl.BlockSpec(memory_space=pl.ANY)] * len(extra),
            out_specs=pl.BlockSpec(block, where),
        ),
        out_shape=jax.ShapeDtypeStruct(shape, f32),
        input_output_aliases={} if target is None else {3: 0},
        cost_estimate=cost(0, 12 * M * height * chans),
        name="place_input_grad",
    )(half, conv, gate, *extra)


def input_grad_layout(value, width, chans):
    if value.ndim == 4:
        return value
    return value.reshape(M, width, chans // LANES, 2, LANES).transpose(0, 1, 3, 2, 4).reshape(M, width, 2, chans)


def join_body(pos_ref, mine_ref, got_ref, o_ref):
    mine = pl.program_id(1) == pos_ref[0]

    @pl.when(mine)
    def _():
        o_ref[0] = mine_ref[0].astype(f32)

    @pl.when(jnp.logical_not(mine))
    def _():
        o_ref[0] = got_ref[0].astype(f32)


def join_halves(core, mine, got):
    _, height, cols = mine.shape
    part = pl.BlockSpec((1, height, cols), lambda m, i, pos: (m, 0, 0))
    return pl.pallas_call(
        join_body,
        grid_spec=pltpu.PrefetchScalarGridSpec(
            num_scalar_prefetch=1,
            grid=(M, 2),
            in_specs=[part, part],
            out_specs=pl.BlockSpec((1, height, cols), lambda m, i, pos: (m, i, 0)),
        ),
        out_shape=jax.ShapeDtypeStruct((M, 2 * height, cols), f32),
        cost_estimate=cost(0, 12 * M * height * cols),
        name="join_halves",
    )(core, mine, got)


def after(value, *others):
    return lax.optimization_barrier((value,) + others)[0]


def swap_core(value):
    count = lax.axis_size("batch")
    return lax.ppermute(value, "batch", [(i, i ^ 1) for i in range(count)])


def y_others(value):
    count = lax.axis_size("batch")
    return [
        lax.ppermute(value, "batch", [(i, (i + shift) % count) for i in range(count)]) for shift in range(2, count, 2)
    ]


def y_sum(value, others):
    if len(others) == 1:
        return value.astype(f32) + others[0].astype(f32)
    chips = len(others) + 1
    mine = lax.axis_index("batch") // 2
    buffer = jnp.zeros((chips,) + value.shape, value.dtype)
    for shift, piece in enumerate([value] + others):
        buffer = lax.dynamic_update_index_in_dim(buffer, piece, (mine + chips - shift) % chips, 0)
    return jnp.sum(buffer.astype(f32), axis=0)


def rounded(value):
    return lax.reduce_precision(value, 8, 7)


def split(value):
    high = rounded(value)
    return jnp.concatenate([high, rounded(value - high)], axis=0).astype(bf16)


def joined(value):
    count = value.shape[0] // 2
    return value[:count].astype(f32) + value[count:].astype(f32)


def small_totals(coarse, fine, first, second):
    rows = coarse.shape[0]
    for step, before in ((lambda value: [swap_core(value)], first), (y_others, second)):
        message = lax.optimization_barrier(jnp.concatenate([rounded(coarse).astype(bf16), split(fine)], axis=0))
        coarse, fine = message[:rows].astype(f32), joined(message[rows:])
        for other in step(message):
            other = after(other, *before)
            coarse, fine = coarse + other[:rows].astype(f32), fine + joined(other[rows:])
    return coarse, fine


def to_owners(pieces):
    return lax.all_to_all(pieces, "own", split_axis=0, concat_axis=0, tiled=False)


def to_all(piece):
    return to_owners(jnp.broadcast_to(piece[None], (lax.axis_size("own"),) + piece.shape))


def gather_small(piece, *before):
    count = lax.axis_size("own")
    mine = lax.axis_index("own")
    held = piece[None]
    bit = 1
    while bit < count:
        got = lax.ppermute(held, "own", [(i, i ^ bit) for i in range(count)])
        got = after(got, before[0])
        before = before[1:] or before
        low = (mine & bit) == 0
        held = jnp.concatenate([jnp.where(low, held, got), jnp.where(low, got, held)], axis=0)
        bit *= 2
    return held


def per_device(
    hidden_in, norm_gain, input_proj, conv_weight, conv_bias, state_proj, step_proj, step_bias,
    log_decay, skip_gain, output_proj, modality, grad_out,
):
    own_count = lax.axis_size("own")
    own_index = lax.axis_index("own")
    core = lax.axis_index("batch") % 2
    width = hidden_in.shape[2]
    rows = modality.shape[1]
    span = rows // own_count
    chans = input_proj.shape[3]
    rank = step_proj.shape[1]
    states = log_decay.shape[0]
    psize = state_proj.shape[2]
    chan_at = own_index * chans

    core_at = core.astype(jnp.int32).reshape(1)
    other_at = (1 - core).astype(jnp.int32).reshape(1)

    modc = modality.reshape(rows, 1)
    modl = modality.reshape(1, rows)
    modr = modality.reshape(rows // LANES, 1, LANES)
    w_in = input_proj.reshape(M, width, 2 * chans)
    sp_t = jnp.swapaxes(state_proj, 1, 2)
    step_rows = step_proj.reshape(M * rank, chans)
    part = lambda table: lax.dynamic_slice_in_dim(table, chan_at, chans, table.ndim - 1)
    cw = part(conv_weight)
    cb = part(conv_bias).reshape(1, chans)
    decay = part(log_decay)
    skip = part(skip_gain).reshape(1, chans)

    resid = hidden_in[0].astype(f32)
    inverse = lax.rsqrt(jnp.mean(resid * resid, axis=-1, keepdims=True) + epsilon)
    normed = (resid * inverse * norm_gain).astype(bf16)
    mod_others, normed_others = y_others(modality), y_others(normed)
    x = lax.all_gather(normed, "own", axis=0, tiled=True)
    cot = lax.all_gather(after(grad_out[0], x, w_in, *mod_others, *normed_others), "own", axis=0, tiled=True)

    conv_in, gate, act, proj_part = input_stage(x, w_in, cw, cb, sp_t, modc, modr)
    modcs = [modc] + [other.reshape(rows, 1) for other in mod_others]
    blocks = rows // LANES
    per_owner = blocks // own_count
    pieces = proj_part.reshape(own_count, per_owner * psize, LANES)
    proj = jnp.sum(to_owners(pieces).astype(f32), axis=0).reshape(per_owner, psize, LANES)
    high = proj.astype(bf16)
    low = (proj[:, rank:] - high[:, rank:].astype(f32)).astype(bf16)
    packed = jnp.concatenate([high, low], axis=1)
    pj = to_all(packed).reshape(blocks, psize + 2 * states, LANES)
    xs = [x] + [lax.all_gather(after(other, pj), "own", axis=0, tiled=True) for other in normed_others]
    delta, sig, gated, scanned, prev, final, b_wide, c_wide = scan_forward(
        pj, act, gate, step_rows, step_bias, decay, skip, modc, modr
    )
    branch_part = select_matmul(gated, output_proj, modc, False, bf16, "output_stage")
    branch = lax.psum_scatter(branch_part, "own", scatter_dimension=0, tiled=True)
    block_out = (resid + branch.astype(f32)).astype(bf16)[None]

    gg, ggate = gated_grads(cot, output_proj, modc, scanned, gate)
    ggates = [ggate] + y_others(ggate)
    gated_t = jnp.swapaxes(gated, 0, 1)
    groups = ((0, 1, 2),)
    out_got = [
        swap_core(value) for value in rows_wgrad(other_at, gated_t, cot, modl, [], groups, "output_wgrad_send")
    ]
    out_half = rows_wgrad(core_at, gated_t, cot, modl, [after(value, branch_part, ggate) for value in out_got], groups, "output_wgrad_keep")
    out_others = y_others(out_half[0])

    gas, gpt, glogd, gskip, gbias, gstep = scan_backward(
        after(pj, branch_part, *out_half), act, gate, gg, delta, sig, prev, final, b_wide, c_wide, step_rows, decay, skip, modc, modr
    )
    gp_own = jnp.sum(to_owners(gpt.reshape(own_count, per_owner * psize, LANES)).astype(f32), axis=0).astype(bf16)
    gp = to_all(gp_own).reshape(blocks, psize, LANES)

    ggates = [ggate] + [after(other, gp_own) for other in ggates[1:]]
    gate_send = half_wgrad(other_at, xs, ggates, modcs, None, "gate_wgrad_send")
    gate_got = swap_core(gate_send)

    gp = after(gp, gate_send, *out_others)
    out_total = y_sum(out_half[0], out_others).astype(bf16)
    gci, gstate, gcw = conv_backward(gp, sp_t, gas, conv_in, act, cw, cb, modc, modr)
    others = y_others(gci)
    gnormed, gain_part = input_dgrad(gci, ggate, w_in, modc, x, norm_gain.reshape(1, width))

    gcis = [gci] + [after(other, gnormed) for other in others]
    gnormed = lax.psum_scatter(gnormed, "own", scatter_dimension=0, tiled=True)
    conv_send = half_wgrad(other_at, xs, gcis, modcs, None, "conv_wgrad_send")
    gate_mine = half_wgrad(core_at, xs, ggates, modcs, after(gate_got, conv_send, branch), "gate_wgrad_keep")
    gate_recv = swap_core(gate_mine)
    conv_got = after(swap_core(conv_send), gate_mine)
    conv_mine = half_wgrad(core_at, xs, gcis, modcs, conv_got, "conv_wgrad_keep")
    conv_recv = swap_core(conv_mine)
    grad_output = join_halves(core_at, out_total, swap_core(out_total))
    half_placed = place_input_grad(core_at, after(conv_mine, grad_output), gate_mine, None)
    grad_input = place_input_grad(other_at, after(conv_recv, gnormed), gate_recv, half_placed)
    gnormed = gnormed.astype(f32)

    weighted = norm_gain * gnormed
    coupled = jnp.mean(resid * weighted, axis=-1, keepdims=True)
    grad_hidden = (
        grad_out[0].astype(f32) + inverse * weighted - resid * (inverse * inverse * inverse) * coupled
    )[None]

    gain_rows = width // chans
    weights, small = small_totals(
        jnp.concatenate([gstep, gstate.reshape(M * psize, chans)], axis=0),
        jnp.concatenate([glogd, gcw[:5], gskip, gain_part.reshape(gain_rows, chans), gbias], axis=0),
        (conv_send,), (half_placed,),
    )
    grad_step = weights[: M * rank].reshape(M, rank, chans)
    grad_state = jnp.swapaxes(weights[M * rank :].reshape(M, psize, chans), 1, 2)
    grad_bias = small[states + 6 + gain_rows :]
    wide = gather_small(small[: states + 6 + gain_rows], half_placed, half_placed, grad_input)
    grad_gain = jnp.sum(wide[:, states + 6 :], axis=0).reshape(width)
    wide = jnp.swapaxes(wide[:, : states + 6], 0, 1).reshape(states + 6, own_count * chans)
    grad_input = input_grad_layout(grad_input, width, chans)
    return (
        block_out,
        grad_hidden,
        grad_gain,
        grad_input,
        wide[states : states + 4],
        wide[states + 4],
        grad_state,
        grad_step,
        grad_bias,
        wide[:states],
        wide[states + 5],
        grad_output,
    )


def solution(mesh):
    placed = (
        P("batch", "own", None),
        P(),
        P(None, None, None, "own"),
        P(),
        P(),
        P(None, "own", None),
        P(None, None, "own"),
        P(None, "own"),
        P(),
        P(),
        P(None, "own", None),
        P("batch", None),
        P("batch", "own", None),
    )
    return jax.shard_map(
        per_device,
        mesh=mesh,
        in_specs=placed,
        out_specs=(
            P("batch", "own", None),
            P("batch", "own", None),
            P(),
            P(None, None, None, "own"),
            P(),
            P(),
            P(None, "own", None),
            P(None, None, "own"),
            P(None, "own"),
            P(),
            P(),
            P(None, "own", None),
        ),
        check_vma=False,
    )
```
